32 devices in a mesh: groups: 2 (over x), region: 8 (over z, y), head: 2 (over core).
Axes of the slice: x: 2, y: 2, z: 4, core: 2. Of those that a mesh axis runs over, the one named last changes fastest.
Arguments:
- features: bfloat16 [16384, 256], P(('groups', 'region'), 'head'), parts along dimension 0, may hold values from -6 to 6
- element_kinds: int32 [16384], P(('groups', 'region')), parts along dimension 0, may hold values from 0 to 11
- bin_cells: int32 [16384], P(('groups', 'region')), parts along dimension 0, may hold values from 0 to 16383, as said below
- kind_embed: bfloat16 [12, 256], P(None, 'head'), may hold values from -3 to 3
- norm_gain: float32 [256], replicated, may hold values from 0.5 to 1.5
- w_query: bfloat16 [256, 256], P(None, 'head'), may hold values from -10 to 10
- w_key: bfloat16 [256, 256], P(None, 'head'), may hold values from -1 to 1
- w_value: bfloat16 [256, 256], P(None, 'head'), may hold values from -0.375 to 0.375
- w_out: bfloat16 [256, 256], P('head'), may hold values from -0.375 to 0.375
- cotangent: bfloat16 [16384, 256], P(('groups', 'region'), 'head'), parts along dimension 0, may hold values from -6 to 6
Outputs:
- attended: bfloat16 [16384, 256], P(('groups', 'region'), 'head'), parts along dimension 0
- grad_feats: bfloat16 [16384, 256], P(('groups', 'region'), 'head'), parts along dimension 0
- grad_w_query: float32 [512, 256], P('groups', 'head'), parts along dimension 0
- grad_w_key: float32 [512, 256], P('groups', 'head'), parts along dimension 0
- grad_w_value: float32 [512, 256], P('groups', 'head'), parts along dimension 0
- grad_w_out: float32 [512, 256], P(('groups', 'head')), parts along dimension 0
- grad_gain: float32 [512], P('groups'), parts along dimension 0
- grad_embed: float32 [24, 256], P('groups', 'head'), parts along dimension 0
The draws below stay inside these ranges and needn't reach their ends.
There are 2 independent parts, one for each index of `groups`. The reference program is written for one: setup_inputs(seed, part) draws one part's arguments, and reference() takes and returns one part's arrays. A program takes and returns all parts, laid end to end along the dimension named above; an argument that names none is the same for every part. Nothing has to cross between parts.
Inputs may be any that keep to these rules, and one draw needn't show every extreme that they name: No two elements share a cell. The bin block of a cell, bin_cells[e] // 2048, is the index of region that owns that bin. The elements of one index of region put at most 256 cells into one bin block, and in every draw some bin block receives exactly 256 from every index of region.
All inputs are finite; a program needn't handle non-finite values.
Results may differ from the reference program's by a relative error of at most 0.018.
The reference program's roundings to bfloat16 on the way (of `base_rows`, `normed`, `probs_low`, `context`, `d_context`, `d_scores` and `d_slab`) count: a program that leaves them out, or rounds other values in their place, can miss the bound.
Values may be sent and summed in bfloat16 or wider, within the bound.
No kernel may reach another device: no remote copies, remote signals or barrier semaphores. Data moves between devices by JAX's collectives and lax.ppermute only.
A program may use at most 128 MiB of HBM per device.

```python
import jax
import jax.numpy as jnp
from jax import lax

D = 256
HEADS = 8
KINDS = 12
SLOTS = 1024
BINS_DEV = 2
BINS = 16
ELEM_DEV = 1024
ELEMENTS = 8192
N_REGION = 8


def key_matrix(key):
    return jax.random.truncated_normal(jax.random.fold_in(key, 7), -4.0, 4.0, (D, D), jnp.float32) * D ** (-0.5)


def draw_w_key(key, part):
    return key_matrix(key).astype(jnp.bfloat16)


def draw_w_query(key, part):
    jitter = jax.random.truncated_normal(jax.random.fold_in(key, 9), -4.0, 4.0, (D, D), jnp.float32) * (0.5 * D ** (-0.5))
    return jitter.astype(jnp.bfloat16)


def draw_bin_cells(key, part):
    regions = N_REGION
    local_rows = BINS_DEV * SLOTS
    capacity = local_rows // regions
    key_full, key_level, key_perm, key_source = jax.random.split(jax.random.fold_in(key, 3), 4)
    favoured = jax.random.randint(key_full, (), 0, regions)
    levels = jax.random.randint(key_level, (regions,), 0, 4)
    orders = jax.vmap(lambda subkey: jax.random.permutation(subkey, local_rows))(jax.random.split(key_perm, regions))
    owner_ids = jnp.arange(regions, dtype=jnp.int32)

    def one_source(source):
        sub_pick, sub_shuffle = jax.random.split(jax.random.fold_in(key_source, source))
        jitter = jax.random.randint(sub_pick, (regions, capacity), 0, 2 ** 14)
        scores = jitter + levels[:, None] * 2 ** 12 + jnp.where(owner_ids == favoured, 2 ** 16, 0)[:, None]
        ranked_scores = scores.reshape(-1) * local_rows + jnp.arange(local_rows, dtype=jnp.int32)
        top_vals, chosen = jax.lax.top_k(ranked_scores, ELEM_DEV)
        owners = chosen // capacity
        column = chosen % capacity
        slots_hit = orders[owners, source * capacity + column]
        cells_here = owners * local_rows + slots_hit
        return jax.random.permutation(sub_shuffle, cells_here)
    return jax.vmap(one_source)(owner_ids).reshape(-1).astype(jnp.int32)


def set_ends(values, key, low, largest):
    longest = values.shape.index(max(values.shape))
    spots = []
    for shift in (0, 1):
        where = [jax.random.randint(jax.random.fold_in(key, axis), (), 0, length) for axis, length in enumerate(values.shape)]
        where[longest] = (where[longest] + shift) % values.shape[longest]
        spots.append(tuple(where))
    return values.at[spots[0]].set(low).at[spots[1]].set(largest)


def shard_levels(stream_key, shape, pieces, low, largest):
    def one(position, shards_of):
        draws = jax.random.uniform(jax.random.fold_in(jax.random.fold_in(stream_key, 6), position), (shards_of,), jnp.float32, low / len(pieces), largest / len(pieces))
        return jnp.repeat(jnp.exp(draws), shape[position] // shards_of).reshape((-1,) + (1,) * (len(shape) - position - 1))

    factor_of = one(*pieces[0])
    for cut in pieces[1:]:
        factor_of = factor_of * one(*cut)
    return factor_of


def gaussian(rng, extent, spread, most, cuts=(), kind=jnp.bfloat16):
    level = shard_levels(rng, extent, cuts, -0.22, 0.18) if cuts else 1.0
    values = jax.random.normal(rng, extent, jnp.float32) * spread * level
    return jnp.minimum(jnp.maximum(values, -most), most).astype(kind)


def setup_inputs(seed: int = 0, part: int = 0) -> dict:
    seeds = jax.random.split(jax.random.key(seed), 11)
    own_keys = jax.random.split(jax.random.fold_in(seeds[10], part), 11)
    return {
        "features": gaussian(own_keys[0], (ELEMENTS, D), 1.0, 6.0, ((0, 8), (1, 2))),
        "element_kinds": set_ends(jax.random.randint(own_keys[1], (ELEMENTS,), 0, KINDS), jax.random.fold_in(own_keys[1], 1), 0, KINDS - 1).astype(jnp.int32),
        "bin_cells": draw_bin_cells(jax.random.fold_in(jax.random.fold_in(seeds[10], part), 71), part),
        "kind_embed": gaussian(seeds[3], (KINDS, D), 0.5, 3.0, ((1, 2),)),
        "norm_gain": jnp.clip(1.0 + 0.1 * jax.random.normal(seeds[4], (D,), jnp.float32), 0.5, 1.5),
        "w_query": draw_w_query(jax.random.fold_in(seeds[10], 71), part),
        "w_key": draw_w_key(jax.random.fold_in(seeds[10], 71), part),
        "w_value": gaussian(seeds[7], (D, D), D ** -0.5, 0.375, ((1, 2),)),
        "w_out": gaussian(seeds[8], (D, D), D ** -0.5, 0.375, ((0, 2),)),
        "cotangent": gaussian(own_keys[9], (ELEMENTS, D), 1.0, 6.0, ((0, 8), (1, 2))),
    }


MASKED = -1000000000.0
EPSILON = 1e-06

def tile_pass(queries, key_rows, values, keep_mask, d_context):
    factor = queries.shape[1] ** (-0.5)
    scores = jnp.dot(queries, key_rows.T, preferred_element_type=jnp.float32) * factor
    scores = jnp.where(keep_mask[None, :] > 0, scores, MASKED)
    shifted = jnp.exp(scores - lax.optimization_barrier(jnp.max(scores, axis=1, keepdims=True)))
    probs_full = shifted / lax.optimization_barrier(jnp.sum(shifted, axis=1, keepdims=True))
    probs_low = probs_full.astype(jnp.bfloat16)
    context = jnp.dot(probs_low, values, preferred_element_type=jnp.float32).astype(jnp.bfloat16)
    d_probs = jnp.dot(d_context, values.T, preferred_element_type=jnp.float32)
    inner = lax.optimization_barrier(jnp.sum(probs_full * d_probs, axis=1, keepdims=True))
    d_scores = (probs_full * (d_probs - inner) * factor).astype(jnp.bfloat16)
    d_query = jnp.dot(d_scores, key_rows, preferred_element_type=jnp.float32).astype(jnp.bfloat16)
    d_key = jnp.dot(d_scores.T, queries, preferred_element_type=jnp.float32).astype(jnp.bfloat16)
    d_value = jnp.dot(probs_low.T, d_context, preferred_element_type=jnp.float32).astype(jnp.bfloat16)
    return (context, d_query, d_key, d_value)

def split_heads(row_block, bin_count, head_count):
    return row_block.reshape(bin_count, SLOTS, head_count, -1).transpose(0, 2, 1, 3)

def merge_heads(blocks):
    bin_count, head_count, slot_count, head_width = blocks.shape
    return blocks.transpose(0, 2, 1, 3).reshape(bin_count * slot_count, head_count * head_width)

def attend_bins(queries, key_rows, values, keep_mask, d_context, head_count):
    bin_count = queries.shape[0] // SLOTS

    def one_bin(packed):
        bin_query, bin_key, bin_value, bin_keep, bin_grad = packed
        return jax.vmap(tile_pass, in_axes=(0, 0, 0, None, 0))(bin_query, bin_key, bin_value, bin_keep, bin_grad)
    results = lax.map(one_bin, (split_heads(queries, bin_count, head_count), split_heads(key_rows, bin_count, head_count), split_heads(values, bin_count, head_count), keep_mask.reshape(bin_count, SLOTS), split_heads(d_context, bin_count, head_count)))
    return tuple((merge_heads(block_set) for block_set in results))

def reference(features, element_kinds, bin_cells, kind_embed, norm_gain, w_query, w_key, w_value, w_out, cotangent):
    slab_rows = BINS * SLOTS
    kinds_hot = (element_kinds[:, None] == jnp.arange(KINDS, dtype=jnp.int32)[None, :]).astype(jnp.bfloat16)
    base_rows = (features.astype(jnp.float32) + jnp.dot(kinds_hot, kind_embed, preferred_element_type=jnp.float32)).astype(jnp.bfloat16)
    slab = jnp.zeros((slab_rows, D), jnp.bfloat16).at[bin_cells].set(base_rows)
    grad_slab = jnp.zeros((slab_rows, D), jnp.bfloat16).at[bin_cells].set(cotangent)
    keep_mask = jnp.zeros((slab_rows,), jnp.int32).at[bin_cells].set(1)
    widened = slab.astype(jnp.float32)
    inverse = lax.rsqrt(lax.optimization_barrier(jnp.mean(widened * widened, axis=1, keepdims=True)) + EPSILON)
    normed = (widened * inverse * norm_gain).astype(jnp.bfloat16)
    queries = jnp.dot(normed, w_query, preferred_element_type=jnp.float32).astype(jnp.bfloat16)
    key_rows = jnp.dot(normed, w_key, preferred_element_type=jnp.float32).astype(jnp.bfloat16)
    values = jnp.dot(normed, w_value, preferred_element_type=jnp.float32).astype(jnp.bfloat16)
    d_context = jnp.dot(grad_slab, w_out.T, preferred_element_type=jnp.float32).astype(jnp.bfloat16)
    context, d_query, d_key, d_value = attend_bins(queries, key_rows, values, keep_mask, d_context, HEADS)
    attn_rows = jnp.dot(context, w_out, preferred_element_type=jnp.float32)
    d_normed = jnp.dot(d_query, w_query.T, preferred_element_type=jnp.float32) + jnp.dot(d_key, w_key.T, preferred_element_type=jnp.float32) + jnp.dot(d_value, w_value.T, preferred_element_type=jnp.float32)
    scaled = norm_gain * d_normed
    d_slab = inverse * scaled - widened * inverse ** 3 * lax.optimization_barrier(jnp.sum(scaled * widened, axis=1, keepdims=True)) / D
    attended = attn_rows[bin_cells].astype(jnp.bfloat16)
    grad_feats = d_slab.astype(jnp.bfloat16)[bin_cells]
    factor = ELEMENTS ** (-0.5)
    grad_w_query = jnp.dot(normed.T, d_query, preferred_element_type=jnp.float32) * factor
    grad_w_key = jnp.dot(normed.T, d_key, preferred_element_type=jnp.float32) * factor
    grad_w_value = jnp.dot(normed.T, d_value, preferred_element_type=jnp.float32) * factor
    grad_w_out = jnp.dot(context.T, grad_slab, preferred_element_type=jnp.float32) * factor
    grad_gain = lax.optimization_barrier(jnp.sum(d_normed * widened * inverse, axis=0)) * factor
    grad_embed = jnp.dot(kinds_hot.T, grad_feats, preferred_element_type=jnp.float32) * factor
    return (attended, grad_feats, grad_w_query, grad_w_key, grad_w_value, grad_w_out, grad_gain, grad_embed)
```

```python
import functools

import jax
import jax.numpy as jnp
from jax import lax
from jax.experimental import pallas as pl
from jax.experimental.pallas import tpu as pltpu
from jax.sharding import PartitionSpec as P

HEAD_DIM = 32
KINDS = 12
SLOTS = 1024
BINS_DEV = 2
MASKED = -1000000000.0
EPSILON = 1e-06
LOG2E = 1.4426950408889634

F32 = jnp.float32
BF16 = jnp.bfloat16
I32 = jnp.int32
LANES = 128
TAG_ROWS = 16
KIND_ROWS = 16
FAR = 1 << 20
NT = (((1,), (1,)), ((), ()))
TN = (((0,), (0,)), ((), ()))


def iota(shape, axis):
    return lax.broadcasted_iota(I32, shape, axis)


def mm(a, b):
    return jnp.dot(a, b, preferred_element_type=F32)


def mm_nt(a, b):
    return lax.dot_general(a, b, NT, preferred_element_type=F32)


def mm_tn(a, b):
    return lax.dot_general(a, b, TN, preferred_element_type=F32)


def hot(condition):
    return jnp.where(condition, 1.0, 0.0).astype(BF16)


def log2_of(n):
    return n.bit_length() - 1


def pack_kernel(regions, capacity, cells, kinds, feats, embed, cot, w_q, w_k, w_v, w_o, out_base, out_cot, out_target, out_w):
    local_rows = BINS_DEV * SLOTS
    count = feats.shape[0]
    half = feats.shape[1]
    cell = cells[...]
    kind = kinds[...]
    owner = lax.shift_right_logical(cell, log2_of(local_rows))
    local = jnp.bitwise_and(cell, local_rows - 1)
    region_rows = max(regions, 16)
    owner_hot = jnp.where(iota((region_rows, count), 0) == owner, 1.0, 0.0)
    before = hot(iota((count, count), 0) < iota((count, count), 1))
    rank = jnp.sum(mm(owner_hot.astype(BF16), before) * owner_hot, axis=0, keepdims=True)
    target = owner * capacity + rank.astype(I32)
    out_target[...] = target
    kinds_hot = hot(iota((KIND_ROWS, count), 0) == kind)
    base = (feats[...].astype(F32) + mm_tn(kinds_hot, embed[...])).astype(BF16)
    rows = jnp.concatenate([base, cot[...]], axis=1)
    place = iota((TAG_ROWS, count), 0)
    high = lax.shift_right_logical(local, 7) + 1
    low = jnp.bitwise_and(local, 127)
    tags = jnp.where(place == 0, high, jnp.where(place == 1, low, jnp.where(place == 2, kind, 0)))
    tags = tags.astype(F32).astype(BF16)
    for r in range(regions):
        chosen = hot(iota((capacity, count), 0) + r * capacity == target)
        moved = mm(chosen, rows).astype(BF16)
        out_base[r, 0:capacity, :] = moved[:, :half]
        out_cot[r, :, :] = moved[:, half:]
        tag = mm_nt(tags, chosen)
        if capacity >= LANES:
            tag = jnp.concatenate([tag[0:8, 0:LANES], tag[0:8, LANES : 2 * LANES]], axis=0)
        else:
            tag = jnp.concatenate([tag, jnp.zeros((TAG_ROWS, LANES - capacity), F32)], axis=1)
        out_base[r, capacity : capacity + TAG_ROWS, :] = tag.astype(BF16)
    out_w[0] = w_q[...]
    out_w[1] = w_k[...]
    out_w[2] = w_v[...]
    out_w[3, 0:half, :] = w_o[:, 0:half]
    out_w[3, half:, :] = w_o[:, half:]


def group_kernel(regions, capacity, core, got, mine, theirs, out_landing, out_info, flat):
    total = regions * capacity
    tag_rows = jnp.zeros((8, total), F32) if capacity < LANES else None
    pieces = []
    for r in range(regions):
        flat[r * capacity : (r + 1) * capacity, :] = got[r, 0:capacity, :]
        block = got[r, capacity : capacity + TAG_ROWS, :]
        if capacity >= LANES:
            block = block.astype(F32)
            pieces += [block[0:8], block[8:16]]
        else:
            shift = hot(iota((LANES, total), 1) == iota((LANES, total), 0) + r * capacity)
            lanes = jnp.where(iota(block.shape, 1) < capacity, block.astype(F32), 0.0).astype(BF16)
            tag_rows = tag_rows + mm(lanes, shift)[0:8]
    if capacity >= LANES:
        tag_rows = jnp.concatenate(pieces, axis=1)
    tag_rows = tag_rows[0:8]
    high = tag_rows[0:1]
    low = tag_rows[1:2]
    kind = tag_rows[2:3]
    filled = high > 0.5
    local = ((high - 1.0) * 128.0 + low).astype(I32)
    swapped = jnp.bitwise_xor(local, core[0] * SLOTS)
    landing = jnp.where(filled, swapped, FAR)
    out_landing[...] = landing
    place = iota((16, total), 0)
    facts = jnp.where(place == 0, jnp.where(filled, 1.0, 0.0), jnp.where(place == 1, kind, 0.0)).astype(BF16)
    step = 256
    for s in range(0, 2 * SLOTS, step):
        chosen = hot(iota((step, total), 0) + s == landing)
        rows = mm(chosen, flat[...]).astype(BF16)
        if s < SLOTS:
            mine[s : s + step, :] = rows
            out_info[:, s : s + step] = mm_nt(facts, chosen)
        else:
            theirs[s - SLOTS : s - SLOTS + step, :] = rows


def regroup_kernel(regions, capacity, landing_ref, got, mine, theirs):
    total = regions * capacity
    landing = landing_ref[...]
    flat = got[...].reshape(total, got.shape[2])
    step = 256
    for s in range(0, 2 * SLOTS, step):
        chosen = hot(iota((step, total), 0) + s == landing)
        rows = mm(chosen, flat).astype(BF16)
        if s < SLOTS:
            mine[s : s + step, :] = rows
        else:
            theirs[s - SLOTS : s - SLOTS + step, :] = rows


def ungroup_kernel(regions, capacity, landing_ref, mine, other, out):
    total = regions * capacity
    column = jnp.transpose(jnp.broadcast_to(landing_ref[...].astype(F32), (8, total)))[:, 0:1]
    column = column.astype(I32)
    both = jnp.concatenate([mine[...], other[...]], axis=0)
    step = 256
    for s in range(0, total, step):
        chosen = hot(iota((step, 2 * SLOTS), 1) == column[s : s + step])
        rows = mm(chosen, both).astype(BF16)
        if capacity >= step:
            out[s // capacity, s % capacity : s % capacity + step, :] = rows
        else:
            for k in range(step // capacity):
                out[s // capacity + k] = rows[k * capacity : (k + 1) * capacity]


def pick_kernel(target_ref, got, out):
    total = got.shape[0] * got.shape[1]
    count = out.shape[0]
    column = jnp.transpose(jnp.broadcast_to(target_ref[...].astype(F32), (8, count)))[:, 0:1].astype(I32)
    flat = got[...].reshape(total, got.shape[2])
    step = 256
    for s in range(0, count, step):
        chosen = hot(iota((step, total), 1) == column[s : s + step])
        out[s : s + step, :] = mm(chosen, flat).astype(BF16)


def ordered(flag, own, other):
    first = jnp.where(flag, other, own)
    second = jnp.where(flag, own, other)
    return first, second


def full_weights(core, own, other):
    flag = core[0] > 0
    half = own.shape[2]
    columns = []
    for k in range(3):
        columns.append(jnp.concatenate(ordered(flag, own[k], other[k]), axis=1))
    top, bottom = ordered(flag, own[3], other[3])
    rows = [jnp.concatenate([part[0:half], part[half:]], axis=1) for part in (top, bottom)]
    return columns + [jnp.concatenate(rows, axis=0)]


def norm_rows(slab, gain, width):
    wide = slab.astype(F32)
    inverse = lax.rsqrt(jnp.sum(wide * wide, axis=1, keepdims=True) / width + EPSILON)
    return wide, inverse, (wide * inverse * gain).astype(BF16)


def spare_lanes(h, heads):
    last = heads * HEAD_DIM - 1
    is_last = h == heads - 1
    return jnp.where(is_last, 0, last), jnp.where(is_last, 1, last - 1)


def forward_kernel(
    heads, core, mine, other, w_own, w_other, gain, info, queries_out, keys_out, values_out, exps_out, context_out, inv_out,
    keep_out, send_out, queries, keys_t, values, w_out, context
):
    h = pl.program_id(0)
    width = heads * HEAD_DIM
    half = width // 2
    flag = core[0] > 0
    lane = iota((1, width), 1)
    scale = HEAD_DIM**-0.5

    @pl.when(h == 0)
    def _():
        w_q, w_k, w_v, w_o = full_weights(core, w_own, w_other)
        w_out[...] = w_o
        slab = jnp.concatenate(ordered(flag, mine[...], other[...]), axis=1)
        _, _, normed = norm_rows(slab, gain[...], width)
        q = mm(normed, w_q).astype(BF16)
        queries[...] = q
        queries_out[...] = q
        k = mm(normed, w_k)
        k_low = k.astype(BF16)
        keys_out[...] = k_low
        k_t = jnp.transpose(k_low.astype(F32))
        bias = jnp.where(info[0:1, :] > 0.5, 0.0, MASKED / scale)
        row = iota(k_t.shape, 0)
        keys_t[0] = jnp.where(row == width - 1, bias, k_t).astype(BF16)
        keys_t[1] = jnp.where(row == 0, bias, k_t).astype(BF16)
        v = mm(normed, w_v).astype(BF16)
        values_out[...] = v
        v_wide = v.astype(F32)
        values[0] = jnp.where(lane == width - 1, 1.0, v_wide).astype(BF16)
        values[1] = jnp.where(lane == 0, 1.0, v_wide).astype(BF16)
        inv_out[...] = jnp.zeros_like(inv_out)

    spare, _ = spare_lanes(h, heads)
    side = jnp.where(h == heads - 1, 1, 0)
    own_lane = lax.shift_right_logical(lane, log2_of(HEAD_DIM)) == h
    step = 256
    for s in range(0, SLOTS, step):
        rows = slice(s, s + step)
        q = jnp.where(own_lane, queries[rows, :].astype(F32), jnp.where(lane == spare, 1.0, 0.0)).astype(BF16)
        scores = mm(q, keys_t[side])
        top = jnp.max(scores, axis=1, keepdims=True)
        exps = jnp.exp2((scores - top) * (scale * LOG2E)).astype(BF16)
        exps_out[0, rows, :] = exps
        summed = mm(exps, values[side])
        inv = 1.0 / jnp.sum(jnp.where(lane == spare, summed, 0.0), axis=1, keepdims=True)
        context[rows, :] = jnp.where(own_lane, summed * inv, context[rows, :])
        lane_small = iota((1, LANES), 1)
        inv_out[rows, :] = jnp.where(lane_small == h, inv, inv_out[rows, :])

    @pl.when(h == heads - 1)
    def _():
        context_out[...] = context[...]
        rows_out = mm(context[...].astype(BF16), w_out[...]).astype(BF16)
        keep_out[...] = jnp.where(flag, rows_out[:, half:], rows_out[:, :half])
        send_out[...] = jnp.where(flag, rows_out[:, :half], rows_out[:, half:])


def backward_kernel(
    heads, core, mine, other, g_mine, g_other, w_own, w_other, gain, info, queries_in, keys_in, values_in, exps_in, context_in,
    inv_in, keep_out, send_out, grad_keep, grad_send, values_t, queries_t, d_context, d_context_t, inv_t, d_query, d_key_t, d_value_t
):
    h = pl.program_id(0)
    width = heads * HEAD_DIM
    half = width // 2
    flag = core[0] > 0
    lane = iota((1, width), 1)
    lane_small = iota((1, LANES), 1)
    scale = HEAD_DIM**-0.5

    def grad_rows():
        return jnp.concatenate(ordered(flag, g_mine[...], g_other[...]), axis=1)

    @pl.when(h == 0)
    def _():
        w_o = full_weights(core, w_own, w_other)[3]
        dc = mm_nt(grad_rows(), w_o).astype(BF16)
        d_context[...] = dc
        d_context_t[...] = jnp.transpose(dc.astype(F32)).astype(BF16)
        inv_t[...] = jnp.transpose(inv_in[...])
        v_t = jnp.transpose(values_in[...].astype(F32))
        row = iota(v_t.shape, 0)
        values_t[0] = jnp.where(row >= width - 2, 1.0, v_t).astype(BF16)
        values_t[1] = jnp.where(row <= 1, 1.0, v_t).astype(BF16)
        queries_t[...] = jnp.transpose(queries_in[...].astype(F32)).astype(BF16)

    spare, spare_low = spare_lanes(h, heads)
    side = jnp.where(h == heads - 1, 1, 0)
    own_lane = lax.shift_right_logical(lane, log2_of(HEAD_DIM)) == h
    base = pl.multiple_of(h * HEAD_DIM, HEAD_DIM)
    head_rows = pl.ds(base, HEAD_DIM)
    inv_row = inv_t[pl.ds(h, 1), :]
    step = 256
    dk = jnp.zeros((HEAD_DIM, SLOTS), F32)
    dv = jnp.zeros((HEAD_DIM, SLOTS), F32)
    for s in range(0, SLOTS, step):
        rows = slice(s, s + step)
        inv = jnp.sum(jnp.where(lane_small == h, inv_in[rows, :], 0.0), axis=1, keepdims=True)
        scaled = jnp.where(own_lane, d_context[rows, :].astype(F32) * inv, 0.0).astype(BF16)
        wide = scaled.astype(F32)
        dot = -jnp.sum(wide * context_in[rows, :], axis=1, keepdims=True)
        dot_high = dot.astype(BF16).astype(F32)
        dot_low = dot - dot_high
        left = jnp.where(lane == spare, dot_high, jnp.where(lane == spare_low, dot_low, wide)).astype(BF16)
        centred = mm(left, values_t[side])
        exps = exps_in[0, rows, :]
        d_scores = (exps.astype(F32) * centred).astype(BF16)
        dq = mm(d_scores, keys_in[...])
        d_query[rows, :] = jnp.where(own_lane, dq * scale, d_query[rows, :])
        dk = dk + mm(queries_t[head_rows, rows], d_scores)
        scaled_t = (d_context_t[head_rows, rows].astype(F32) * inv_row[:, rows]).astype(BF16)
        dv = dv + mm(scaled_t, exps)
    d_key_t[head_rows, :] = dk * scale
    d_value_t[head_rows, :] = dv

    @pl.when(h == heads - 1)
    def _():
        w_q, w_k, w_v, _ = full_weights(core, w_own, w_other)
        slab = jnp.concatenate(ordered(flag, mine[...], other[...]), axis=1)
        wide, inverse, normed = norm_rows(slab, gain[...], width)
        dq = d_query[...].astype(BF16)
        dk = jnp.transpose(d_key_t[...]).astype(BF16)
        dv = jnp.transpose(d_value_t[...]).astype(BF16)
        d_normed = mm_nt(dq, w_q) + mm_nt(dk, w_k) + mm_nt(dv, w_v)
        scaled = gain[...] * d_normed
        along = jnp.sum(scaled * wide, axis=1, keepdims=True)
        d_slab = (inverse * scaled - wide * (inverse * inverse * inverse) * along / width).astype(BF16)
        keep_out[...] = jnp.where(flag, d_slab[:, half:], d_slab[:, :half])
        send_out[...] = jnp.where(flag, d_slab[:, :half], d_slab[:, half:])
        normed_t = jnp.transpose(normed.astype(F32)).astype(BF16)
        context_t = jnp.transpose(context_in[...]).astype(BF16)
        place = 0
        for d_rows in (dq, dk, dv):
            grad = mm(normed_t, d_rows)
            grad_keep[place : place + width, :] = jnp.where(flag, grad[:, half:], grad[:, :half])
            grad_send[place : place + width, :] = jnp.where(flag, grad[:, :half], grad[:, half:]).astype(BF16)
            place += width
        grad = mm(context_t, grad_rows())
        for part in range(2):
            block = grad[:, part * half : (part + 1) * half]
            grad_keep[place : place + half, :] = jnp.where(flag, block[half:], block[:half])
            grad_send[place : place + half, :] = jnp.where(flag, block[:half], block[half:]).astype(BF16)
            place += half
        kinds_hot = hot(jnp.logical_and(iota((KIND_ROWS, SLOTS), 0) == info[1:2, :].astype(I32), info[0:1, :] > 0.5))
        grad = mm(kinds_hot, d_slab)
        grad_keep[place : place + KIND_ROWS, :] = jnp.where(flag, grad[:, half:], grad[:, :half])
        grad_send[place : place + KIND_ROWS, :] = jnp.where(flag, grad[:, :half], grad[:, half:]).astype(BF16)
        place += KIND_ROWS
        gain_grad = jnp.sum(d_normed * wide * inverse, axis=0, keepdims=True)
        pick = iota((16, half), 0)
        block = jnp.where(pick == 0, gain_grad[:, :half], jnp.where(pick == 1, gain_grad[:, half:], 0.0))
        grad_keep[place : place + 16, :] = block
        grad_send[place : place + 16, :] = block.astype(BF16)
        place += 16
        rest = grad_keep.shape[0] - place
        if rest:
            grad_keep[place:, :] = jnp.zeros((rest, half), F32)
            grad_send[place:, :] = jnp.zeros((rest, half), BF16)


def shape(dims, dtype):
    return jax.ShapeDtypeStruct(tuple(dims), dtype)


SMEM_SPEC = pl.BlockSpec(memory_space=pltpu.SMEM)


def whole(array):
    zeros = (0,) * len(array.shape)
    return pl.BlockSpec(tuple(array.shape), lambda *_: zeros)


def simple_call(kernel, outs, name, inputs, scratch=(), scalars=0):
    specs = [SMEM_SPEC] * scalars + [whole(x) for x in inputs[scalars:]]
    return pl.pallas_call(
        kernel,
        out_shape=outs,
        in_specs=specs,
        out_specs=tuple(whole(x) for x in outs),
        scratch_shapes=scratch,
        name=name,
    )(*inputs)


def on_device(
    features,
    element_kinds,
    bin_cells,
    kind_embed,
    norm_gain,
    w_query,
    w_key,
    w_value,
    w_out,
    cotangent,
):
    regions = lax.axis_size("region")
    cores = lax.axis_size("head")
    local_rows = BINS_DEV * SLOTS
    capacity = local_rows // regions
    count, half = features.shape
    width = w_query.shape[0]
    heads = width // HEAD_DIM
    assert cores == BINS_DEV and half * cores == width and half == LANES
    core = lax.axis_index("head").astype(I32).reshape(1)
    swap = [(i, (i + 1) % cores) for i in range(cores)]

    def other_core(x):
        return lax.ppermute(x, "head", swap)

    def exchange(x):
        return lax.all_to_all(x, "region", split_axis=0, concat_axis=0, tiled=True)

    embed = jnp.concatenate([kind_embed, jnp.zeros((KIND_ROWS - KINDS, half), BF16)], axis=0)
    gain = norm_gain.reshape(1, width)
    packed_base, packed_cot, target, w_own = simple_call(
        functools.partial(pack_kernel, regions, capacity),
        (
            shape((regions, capacity + TAG_ROWS, half), BF16),
            shape((regions, capacity, half), BF16),
            shape((1, count), I32),
            shape((4, width, half), BF16),
        ),
        "pack",
        (bin_cells.reshape(1, count), element_kinds.reshape(1, count), features, embed, cotangent, w_query, w_key, w_value, w_out),
    )
    w_other = other_core(w_own)
    got_base = exchange(packed_base)
    got_cot = exchange(packed_cot)
    rows_shape = shape((SLOTS, half), BF16)
    mine, theirs, landing, info = simple_call(
        functools.partial(group_kernel, regions, capacity),
        (rows_shape, rows_shape, shape((1, local_rows), I32), shape((16, SLOTS), F32)),
        "group",
        (core, got_base),
        scratch=(pltpu.VMEM((local_rows, half), BF16),),
        scalars=1,
    )
    other = other_core(theirs)

    full_shape = shape((SLOTS, width), BF16)
    exps_shape = shape((heads, SLOTS, SLOTS), BF16)
    exps_spec = pl.BlockSpec((1, SLOTS, SLOTS), lambda h: (h, 0, 0))
    inputs = (core, mine, other, w_own, w_other, gain, info)
    outs = (
        full_shape,
        full_shape,
        full_shape,
        exps_shape,
        shape((SLOTS, width), F32),
        shape((SLOTS, LANES), F32),
        rows_shape,
        rows_shape,
    )
    work = heads * SLOTS * SLOTS
    queries, keys, values, exps, context, inv, attn_keep, attn_send = pl.pallas_call(
        functools.partial(forward_kernel, heads),
        grid=(heads,),
        out_shape=outs,
        in_specs=[SMEM_SPEC] + [whole(x) for x in inputs[1:]],
        out_specs=tuple(exps_spec if x is exps_shape else whole(x) for x in outs),
        scratch_shapes=(
            pltpu.VMEM((SLOTS, width), BF16),
            pltpu.VMEM((2, width, SLOTS), BF16),
            pltpu.VMEM((2, SLOTS, width), BF16),
            pltpu.VMEM((width, width), BF16),
            pltpu.VMEM((SLOTS, width), F32),
        ),
        cost_estimate=pl.CostEstimate(flops=4 * work * width, transcendentals=work, bytes_accessed=2 * work),
        name="forward",
    )(*inputs)
    attn_other = other_core(attn_send)

    g_mine, g_theirs = simple_call(
        functools.partial(regroup_kernel, regions, capacity), (rows_shape, rows_shape), "regroup", (landing, got_cot)
    )
    g_other = other_core(g_theirs)

    unit = 16 * regions
    grad_rows = -(-(4 * width + KIND_ROWS + 16) // unit) * unit
    inputs = (core, mine, other, g_mine, g_other, w_own, w_other, gain, info, queries, keys, values, exps, context, inv)
    outs = (rows_shape, rows_shape, shape((grad_rows, half), F32), shape((grad_rows, half), BF16))
    d_keep, d_send, grad_keep, grad_send = pl.pallas_call(
        functools.partial(backward_kernel, heads),
        grid=(heads,),
        out_shape=outs,
        in_specs=[SMEM_SPEC] + [exps_spec if x is exps else whole(x) for x in inputs[1:]],
        out_specs=tuple(whole(x) for x in outs),
        scratch_shapes=(
            pltpu.VMEM((2, width, SLOTS), BF16),
            pltpu.VMEM((width, SLOTS), BF16),
            pltpu.VMEM((SLOTS, width), BF16),
            pltpu.VMEM((width, SLOTS), BF16),
            pltpu.VMEM((LANES, SLOTS), F32),
            pltpu.VMEM((SLOTS, width), F32),
            pltpu.VMEM((width, SLOTS), F32),
            pltpu.VMEM((width, SLOTS), F32),
        ),
        cost_estimate=pl.CostEstimate(flops=8 * work * width, transcendentals=0, bytes_accessed=2 * work),
        name="backward",
    )(*inputs)

    packed_shape = shape((regions, capacity, half), BF16)

    def back(keep, received):
        (packed,) = simple_call(
            functools.partial(ungroup_kernel, regions, capacity), (packed_shape,), "ungroup", (landing, keep, received)
        )
        home = exchange(packed)
        (rows,) = simple_call(pick_kernel, (shape((count, half), BF16),), "pick", (target, home))
        return rows

    attended = back(attn_keep, attn_other)
    grad_feats = back(d_keep, other_core(d_send))

    part = (grad_keep + other_core(grad_send).astype(F32)).astype(BF16)
    shares = exchange(part.reshape(regions, grad_rows // regions, half))
    share = jnp.sum(shares.astype(F32), axis=0).astype(BF16)
    summed = exchange(jnp.broadcast_to(share[None], (regions,) + share.shape)).reshape(grad_rows, half)
    total = summed.astype(F32) * float(count * regions) ** (-0.5)
    place = 3 * width
    grad_out = jnp.concatenate([total[place : place + half], total[place + half : place + width]], axis=1)
    place += width
    grad_embed = total[place : place + KINDS]
    place += KIND_ROWS
    grad_gain = total[place : place + 2].reshape(width)
    return (
        attended,
        grad_feats,
        total[0:width],
        total[width : 2 * width],
        total[2 * width : 3 * width],
        grad_out,
        grad_gain,
        grad_embed,
    )


def solution(mesh):
    placed = (
        P(("groups", "region"), "head"),
        P(("groups", "region")),
        P(("groups", "region")),
        P(None, "head"),
        P(),
        P(None, "head"),
        P(None, "head"),
        P(None, "head"),
        P("head", None),
        P(("groups", "region"), "head"),
    )
    return jax.shard_map(
        on_device,
        mesh=mesh,
        in_specs=placed,
        out_specs=(
            P(("groups", "region"), "head"),
            P(("groups", "region"), "head"),
            P("groups", "head"),
            P("groups", "head"),
            P("groups", "head"),
            P(("groups", "head"), None),
            P("groups"),
            P("groups", "head"),
        ),
        check_vma=False,
    )
```

```python
import functools

import jax
import jax.numpy as jnp
from jax import lax
from jax.experimental import pallas as pl
from jax.experimental.pallas import tpu as pltpu
from jax.sharding import PartitionSpec as P


HEAD_DIM = 32
KINDS = 12
SLOTS = 1024
BINS_DEV = 2
MASKED = -1000000000.0
EPSILON = 1e-06
LOG2E = 1.4426950408889634

F32 = jnp.float32
BF16 = jnp.bfloat16
I32 = jnp.int32
LANES = 128
TAG_ROWS = 16
KIND_ROWS = 16
FAR = 1 << 20
NT = (((1,), (1,)), ((), ()))
TN = (((0,), (0,)), ((), ()))


def iota(shape, axis):
    return lax.broadcasted_iota(I32, shape, axis)


def mm(a, b):
    return jnp.dot(a, b, preferred_element_type=F32)


def mm_nt(a, b):
    return lax.dot_general(a, b, NT, preferred_element_type=F32)


def mm_tn(a, b):
    return lax.dot_general(a, b, TN, preferred_element_type=F32)


def hot(condition):
    return jnp.where(condition, 1.0, 0.0).astype(BF16)


def log2_of(n):
    return n.bit_length() - 1


def pack_kernel(regions, capacity, cells, kinds, feats, embed, cot, w_q, w_k, w_v, w_o, out_base, out_cot, out_target, out_w):
    local_rows = BINS_DEV * SLOTS
    count = feats.shape[0]
    half = feats.shape[1]
    cell = cells[...]
    kind = kinds[...]
    owner = lax.shift_right_logical(cell, log2_of(local_rows))
    local = jnp.bitwise_and(cell, local_rows - 1)
    region_rows = max(regions, 16)
    owner_hot = jnp.where(iota((region_rows, count), 0) == owner, 1.0, 0.0)
    before = hot(iota((count, count), 0) < iota((count, count), 1))
    rank = jnp.sum(mm(owner_hot.astype(BF16), before) * owner_hot, axis=0, keepdims=True)
    target = owner * capacity + rank.astype(I32)
    out_target[...] = target
    kinds_hot = hot(iota((KINDS, count), 0) == kind)
    base = (feats[...].astype(F32) + mm_tn(kinds_hot, embed[...])).astype(BF16)
    rows = jnp.concatenate([base, cot[...]], axis=1)
    place = iota((TAG_ROWS, count), 0)
    high = lax.shift_right_logical(local, 7) + 1
    low = jnp.bitwise_and(local, 127)
    tags = jnp.where(place == 0, high, jnp.where(place == 1, low, jnp.where(place == 2, kind, 0)))
    tags = tags.astype(F32).astype(BF16)
    for r in range(regions):
        chosen = hot(iota((capacity, count), 0) + r * capacity == target)
        moved = mm(chosen, rows).astype(BF16)
        out_base[r, 0:capacity, :] = moved[:, :half]
        out_cot[r, :, :] = moved[:, half:]
        tag = mm_nt(tags, chosen)
        if capacity >= LANES:
            tag = jnp.concatenate([tag[0:8, 0:LANES], tag[0:8, LANES : 2 * LANES]], axis=0)
        else:
            tag = jnp.concatenate([tag, jnp.zeros((TAG_ROWS, LANES - capacity), F32)], axis=1)
        out_base[r, capacity : capacity + TAG_ROWS, :] = tag.astype(BF16)
    out_w[0] = w_q[...]
    out_w[1] = w_k[...]
    out_w[2] = w_v[...]
    out_w[3, 0:half, :] = w_o[:, 0:half]
    out_w[3, half:, :] = w_o[:, half:]


def group_kernel(regions, capacity, core, got, mine, theirs, out_landing, out_info, flat):
    total = regions * capacity
    tag_rows = jnp.zeros((8, total), F32) if capacity < LANES else None
    pieces = []
    for r in range(regions):
        flat[r * capacity : (r + 1) * capacity, :] = got[r, 0:capacity, :]
        block = got[r, capacity : capacity + TAG_ROWS, :]
        if capacity >= LANES:
            block = block.astype(F32)
            pieces += [block[0:8], block[8:16]]
        else:
            shift = hot(iota((LANES, total), 1) == iota((LANES, total), 0) + r * capacity)
            lanes = jnp.where(iota(block.shape, 1) < capacity, block.astype(F32), 0.0).astype(BF16)
            tag_rows = tag_rows + mm(lanes, shift)[0:8]
    if capacity >= LANES:
        tag_rows = jnp.concatenate(pieces, axis=1)
    tag_rows = tag_rows[0:8]
    high = tag_rows[0:1]
    low = tag_rows[1:2]
    kind = tag_rows[2:3]
    filled = high > 0.5
    local = ((high - 1.0) * 128.0 + low).astype(I32)
    swapped = jnp.bitwise_xor(local, core[0] * SLOTS)
    landing = jnp.where(filled, swapped, FAR)
    out_landing[...] = landing
    place = iota((16, total), 0)
    facts = jnp.where(place == 0, jnp.where(filled, 1.0, 0.0), jnp.where(place == 1, kind, 0.0)).astype(BF16)
    step = 256
    for s in range(0, 2 * SLOTS, step):
        chosen = hot(iota((step, total), 0) + s == landing)
        rows = mm(chosen, flat[...]).astype(BF16)
        if s < SLOTS:
            mine[s : s + step, :] = rows
            out_info[:, s : s + step] = mm_nt(facts, chosen)
        else:
            theirs[s - SLOTS : s - SLOTS + step, :] = rows


def regroup_kernel(regions, capacity, landing_ref, got, mine, theirs):
    total = regions * capacity
    landing = landing_ref[...]
    flat = got[...].reshape(total, got.shape[2])
    step = 256
    for s in range(0, 2 * SLOTS, step):
        chosen = hot(iota((step, total), 0) + s == landing)
        rows = mm(chosen, flat).astype(BF16)
        if s < SLOTS:
            mine[s : s + step, :] = rows
        else:
            theirs[s - SLOTS : s - SLOTS + step, :] = rows


def ungroup_kernel(regions, capacity, landing_ref, mine, other, *rest):
    out = rest[-1]
    total = regions * capacity
    column = jnp.transpose(jnp.broadcast_to(landing_ref[...].astype(F32), (8, total)))[:, 0:1]
    column = column.astype(I32)
    both = jnp.concatenate([mine[...], other[...]], axis=0)
    step = 256
    for s in range(0, total, step):
        chosen = hot(iota((step, 2 * SLOTS), 1) == column[s : s + step])
        rows = mm(chosen, both).astype(BF16)
        if capacity >= step:
            out[s // capacity, s % capacity : s % capacity + step, :] = rows
        else:
            for k in range(step // capacity):
                out[s // capacity + k, 0:capacity, :] = rows[k * capacity : (k + 1) * capacity]
    if len(rest) > 1:
        own, received, _ = rest
        share = own.shape[0] // regions
        for r in range(regions):
            rows = slice(r * share, (r + 1) * share)
            out[r, capacity : capacity + share, :] = (own[rows, :] + received[rows, :].astype(F32)).astype(BF16)


def share_kernel(regions, capacity, got, out):
    total = got[0, capacity:, :].astype(F32)
    for r in range(1, regions):
        total = total + got[r, capacity:, :].astype(F32)
    total = total.astype(BF16)
    for r in range(regions):
        out[r] = total


def spread_kernel(factor, got, out_q, out_k, out_v, out_o, out_gain, out_embed):
    total = got[...].reshape(got.shape[0] * got.shape[1], got.shape[2]).astype(F32) * factor
    width, half = out_q.shape
    out_q[...] = total[0:width]
    out_k[...] = total[width : 2 * width]
    out_v[...] = total[2 * width : 3 * width]
    place = 3 * width
    out_o[:, 0:half] = total[place : place + half]
    out_o[:, half:] = total[place + half : place + width]
    place += width
    out_embed[...] = total[place : place + KINDS]
    place += KIND_ROWS
    out_gain[:, 0:half] = total[place : place + 1]
    out_gain[:, half:] = total[place + 1 : place + 2]


def pick_kernel(target_ref, got, out):
    capacity = BINS_DEV * SLOTS // got.shape[0]
    total = got.shape[0] * capacity
    count = out.shape[0]
    column = jnp.transpose(jnp.broadcast_to(target_ref[...].astype(F32), (8, count)))[:, 0:1].astype(I32)
    flat = got[:, 0:capacity, :].reshape(total, got.shape[2])
    step = 256
    for s in range(0, count, step):
        chosen = hot(iota((step, total), 1) == column[s : s + step])
        out[s : s + step, :] = mm(chosen, flat).astype(BF16)


def ordered(flag, own, other):
    first = jnp.where(flag, other, own)
    second = jnp.where(flag, own, other)
    return first, second


def full_weights(core, own, other):
    flag = core[0] > 0
    half = own.shape[2]
    columns = []
    for k in range(3):
        columns.append(jnp.concatenate(ordered(flag, own[k], other[k]), axis=1))
    top, bottom = ordered(flag, own[3], other[3])
    rows = [jnp.concatenate([part[0:half], part[half:]], axis=1) for part in (top, bottom)]
    return columns + [jnp.concatenate(rows, axis=0)]


def norm_rows(slab, gain, width):
    wide = slab.astype(F32)
    inverse = lax.rsqrt(jnp.sum(wide * wide, axis=1, keepdims=True) / width + EPSILON)
    return wide, inverse, (wide * inverse * gain).astype(BF16)


def spare_lanes(h, heads):
    last = heads * HEAD_DIM - 1
    is_last = h == heads - 1
    return jnp.where(is_last, 0, last), jnp.where(is_last, 1, last - 1)


def forward_kernel(
    heads, core, mine, other, w_own, w_other, gain, info, queries_out, keys_out, values_out, exps_out, context_out, inv_out,
    keep_out, send_out, queries, keys_t, values, w_out, context
):
    h = pl.program_id(0)
    width = heads * HEAD_DIM
    half = width // 2
    flag = core[0] > 0
    lane = iota((1, width), 1)
    scale = HEAD_DIM**-0.5

    @pl.when(h == 0)
    def _():
        w_q, w_k, w_v, w_o = full_weights(core, w_own, w_other)
        w_out[...] = w_o
        slab = jnp.concatenate(ordered(flag, mine[...], other[...]), axis=1)
        _, _, normed = norm_rows(slab, gain[...], width)
        q = mm(normed, w_q).astype(BF16)
        queries[...] = q
        queries_out[...] = q
        k = mm(normed, w_k)
        k_low = k.astype(BF16)
        keys_out[...] = k_low
        k_t = jnp.transpose(k_low.astype(F32))
        bias = jnp.where(info[0:1, :] > 0.5, 0.0, MASKED / scale)
        row = iota(k_t.shape, 0)
        keys_t[0] = jnp.where(row == width - 1, bias, k_t).astype(BF16)
        keys_t[1] = jnp.where(row == 0, bias, k_t).astype(BF16)
        v = mm(normed, w_v).astype(BF16)
        values_out[...] = v
        v_wide = v.astype(F32)
        values[0] = jnp.where(lane == width - 1, 1.0, v_wide).astype(BF16)
        values[1] = jnp.where(lane == 0, 1.0, v_wide).astype(BF16)
        inv_out[...] = jnp.zeros_like(inv_out)

    spare, _ = spare_lanes(h, heads)
    side = jnp.where(h == heads - 1, 1, 0)
    own_lane = lax.shift_right_logical(lane, log2_of(HEAD_DIM)) == h
    step = 256
    for s in range(0, SLOTS, step):
        rows = slice(s, s + step)
        q = jnp.where(own_lane, queries[rows, :].astype(F32), jnp.where(lane == spare, 1.0, 0.0)).astype(BF16)
        scores = mm(q, keys_t[side])
        top = jnp.max(scores, axis=1, keepdims=True)
        exps = jnp.exp2((scores - top) * (scale * LOG2E)).astype(BF16)
        exps_out[0, rows, :] = exps
        summed = mm(exps, values[side])
        inv = 1.0 / jnp.sum(jnp.where(lane == spare, summed, 0.0), axis=1, keepdims=True)
        context[rows, :] = jnp.where(own_lane, summed * inv, context[rows, :])
        lane_small = iota((1, LANES), 1)
        inv_out[rows, :] = jnp.where(lane_small == h, inv, inv_out[rows, :])

    @pl.when(h == heads - 1)
    def _():
        context_out[...] = context[...]
        rows_out = mm(context[...].astype(BF16), w_out[...]).astype(BF16)
        keep_out[...] = jnp.where(flag, rows_out[:, half:], rows_out[:, :half])
        send_out[...] = jnp.where(flag, rows_out[:, :half], rows_out[:, half:])


def backward_kernel(
    heads, core, mine, other, g_mine, g_other, w_own, w_other, gain, info, queries_in, keys_in, values_in, exps_in, context_in,
    inv_in, keep_out, send_out, grad_keep, grad_send, values_t, queries_t, d_context, d_context_t, inv_t, d_query, d_key_t, d_value_t
):
    h = pl.program_id(0)
    width = heads * HEAD_DIM
    half = width // 2
    flag = core[0] > 0
    lane = iota((1, width), 1)
    lane_small = iota((1, LANES), 1)
    scale = HEAD_DIM**-0.5

    def grad_rows():
        return jnp.concatenate(ordered(flag, g_mine[...], g_other[...]), axis=1)

    @pl.when(h == 0)
    def _():
        w_o = full_weights(core, w_own, w_other)[3]
        dc = mm_nt(grad_rows(), w_o).astype(BF16)
        d_context[...] = dc
        d_context_t[...] = jnp.transpose(dc.astype(F32)).astype(BF16)
        inv_t[...] = jnp.transpose(inv_in[...])
        v_t = jnp.transpose(values_in[...].astype(F32))
        row = iota(v_t.shape, 0)
        values_t[0] = jnp.where(row >= width - 2, 1.0, v_t).astype(BF16)
        values_t[1] = jnp.where(row <= 1, 1.0, v_t).astype(BF16)
        queries_t[...] = jnp.transpose(queries_in[...].astype(F32)).astype(BF16)

    spare, spare_low = spare_lanes(h, heads)
    side = jnp.where(h == heads - 1, 1, 0)
    own_lane = lax.shift_right_logical(lane, log2_of(HEAD_DIM)) == h
    base = pl.multiple_of(h * HEAD_DIM, HEAD_DIM)
    head_rows = pl.ds(base, HEAD_DIM)
    inv_row = inv_t[pl.ds(h, 1), :]
    step = 256
    dk = jnp.zeros((HEAD_DIM, SLOTS), F32)
    dv = jnp.zeros((HEAD_DIM, SLOTS), F32)
    for s in range(0, SLOTS, step):
        rows = slice(s, s + step)
        inv = jnp.sum(jnp.where(lane_small == h, inv_in[rows, :], 0.0), axis=1, keepdims=True)
        scaled = jnp.where(own_lane, d_context[rows, :].astype(F32) * inv, 0.0).astype(BF16)
        wide = scaled.astype(F32)
        dot = -jnp.sum(wide * context_in[rows, :], axis=1, keepdims=True)
        dot_high = dot.astype(BF16).astype(F32)
        dot_low = dot - dot_high
        left = jnp.where(lane == spare, dot_high, jnp.where(lane == spare_low, dot_low, wide)).astype(BF16)
        centred = mm(left, values_t[side])
        exps = exps_in[0, rows, :]
        d_scores = (exps.astype(F32) * centred).astype(BF16)
        dq = mm(d_scores, keys_in[...])
        d_query[rows, :] = jnp.where(own_lane, dq * scale, d_query[rows, :])
        dk = dk + mm(queries_t[head_rows, rows], d_scores)
        scaled_t = (d_context_t[head_rows, rows].astype(F32) * inv_row[:, rows]).astype(BF16)
        dv = dv + mm(scaled_t, exps)
    d_key_t[head_rows, :] = dk * scale
    d_value_t[head_rows, :] = dv

    @pl.when(h == heads - 1)
    def _():
        w_q, w_k, w_v, _ = full_weights(core, w_own, w_other)
        slab = jnp.concatenate(ordered(flag, mine[...], other[...]), axis=1)
        wide, inverse, normed = norm_rows(slab, gain[...], width)
        dq = d_query[...].astype(BF16)
        dk = jnp.transpose(d_key_t[...]).astype(BF16)
        dv = jnp.transpose(d_value_t[...]).astype(BF16)
        d_normed = mm_nt(dq, w_q) + mm_nt(dk, w_k) + mm_nt(dv, w_v)
        scaled = gain[...] * d_normed
        along = jnp.sum(scaled * wide, axis=1, keepdims=True)
        d_slab = (inverse * scaled - wide * (inverse * inverse * inverse) * along / width).astype(BF16)
        keep_out[...] = jnp.where(flag, d_slab[:, half:], d_slab[:, :half])
        send_out[...] = jnp.where(flag, d_slab[:, :half], d_slab[:, half:])
        normed_t = jnp.transpose(normed.astype(F32)).astype(BF16)
        context_t = jnp.transpose(context_in[...]).astype(BF16)
        place = 0
        for d_rows in (dq, dk, dv):
            grad = mm(normed_t, d_rows)
            grad_keep[place : place + width, :] = jnp.where(flag, grad[:, half:], grad[:, :half])
            grad_send[place : place + width, :] = jnp.where(flag, grad[:, :half], grad[:, half:]).astype(BF16)
            place += width
        grad = mm(context_t, grad_rows())
        for part in range(2):
            block = grad[:, part * half : (part + 1) * half]
            grad_keep[place : place + half, :] = jnp.where(flag, block[half:], block[:half])
            grad_send[place : place + half, :] = jnp.where(flag, block[:half], block[half:]).astype(BF16)
            place += half
        kinds_hot = hot(jnp.logical_and(iota((KIND_ROWS, SLOTS), 0) == info[1:2, :].astype(I32), info[0:1, :] > 0.5))
        grad = mm(kinds_hot, d_slab)
        grad_keep[place : place + KIND_ROWS, :] = jnp.where(flag, grad[:, half:], grad[:, :half])
        grad_send[place : place + KIND_ROWS, :] = jnp.where(flag, grad[:, :half], grad[:, half:]).astype(BF16)
        place += KIND_ROWS
        gain_grad = jnp.sum(d_normed * wide * inverse, axis=0, keepdims=True)
        pick = iota((16, half), 0)
        block = jnp.where(pick == 0, gain_grad[:, :half], jnp.where(pick == 1, gain_grad[:, half:], 0.0))
        grad_keep[place : place + 16, :] = block
        grad_send[place : place + 16, :] = block.astype(BF16)
        place += 16
        rest = grad_keep.shape[0] - place
        if rest:
            grad_keep[place:, :] = jnp.zeros((rest, half), F32)
            grad_send[place:, :] = jnp.zeros((rest, half), BF16)


def shape(dims, dtype):
    return jax.ShapeDtypeStruct(tuple(dims), dtype)


SMEM_SPEC = pl.BlockSpec(memory_space=pltpu.SMEM)


def whole(array):
    zeros = (0,) * len(array.shape)
    return pl.BlockSpec(tuple(array.shape), lambda *_: zeros)


def simple_call(kernel, outs, inputs, scratch=(), scalars=0):
    specs = [SMEM_SPEC] * scalars + [whole(x) for x in inputs[scalars:]]
    return pl.pallas_call(
        kernel, out_shape=outs, in_specs=specs, out_specs=tuple(whole(x) for x in outs), scratch_shapes=scratch
    )(*inputs)


def on_device(
    features,
    element_kinds,
    bin_cells,
    kind_embed,
    norm_gain,
    w_query,
    w_key,
    w_value,
    w_out,
    cotangent,
):
    regions = lax.axis_size("region")
    cores = lax.axis_size("head")
    local_rows = BINS_DEV * SLOTS
    capacity = local_rows // regions
    count, half = features.shape
    width = w_query.shape[0]
    heads = width // HEAD_DIM
    assert cores == BINS_DEV and half * cores == width and half == LANES
    core = lax.axis_index("head").astype(I32).reshape(1)
    swap = [(i, (i + 1) % cores) for i in range(cores)]

    def other_core(x):
        return lax.ppermute(x, "head", swap)

    def exchange(x):
        return lax.all_to_all(x, "region", split_axis=0, concat_axis=0, tiled=True)

    gain = norm_gain.reshape(1, width)
    packed_base, packed_cot, target, w_own = simple_call(
        functools.partial(pack_kernel, regions, capacity),
        (
            shape((regions, capacity + TAG_ROWS, half), BF16),
            shape((regions, capacity, half), BF16),
            shape((1, count), I32),
            shape((4, width, half), BF16),
        ),
        (bin_cells.reshape(1, count), element_kinds.reshape(1, count), features, kind_embed, cotangent, w_query, w_key, w_value, w_out),
    )
    w_other = other_core(w_own)
    got_base = exchange(packed_base)
    got_base, packed_cot = lax.optimization_barrier((got_base, packed_cot))
    got_cot = exchange(packed_cot)
    rows_shape = shape((SLOTS, half), BF16)
    mine, theirs, landing, info = simple_call(
        functools.partial(group_kernel, regions, capacity),
        (rows_shape, rows_shape, shape((1, local_rows), I32), shape((16, SLOTS), F32)),
        (core, got_base),
        scratch=(pltpu.VMEM((local_rows, half), BF16),),
        scalars=1,
    )
    other = other_core(theirs)

    full_shape = shape((SLOTS, width), BF16)
    exps_shape = shape((heads, SLOTS, SLOTS), BF16)
    exps_spec = pl.BlockSpec((1, SLOTS, SLOTS), lambda h: (h, 0, 0))
    inputs = (core, mine, other, w_own, w_other, gain, info)
    outs = (
        full_shape,
        full_shape,
        full_shape,
        exps_shape,
        shape((SLOTS, width), F32),
        shape((SLOTS, LANES), F32),
        rows_shape,
        rows_shape,
    )
    work = heads * SLOTS * SLOTS
    queries, keys, values, exps, context, inv, attn_keep, attn_send = pl.pallas_call(
        functools.partial(forward_kernel, heads),
        grid=(heads,),
        out_shape=outs,
        in_specs=[SMEM_SPEC] + [whole(x) for x in inputs[1:]],
        out_specs=tuple(exps_spec if x is exps_shape else whole(x) for x in outs),
        scratch_shapes=(
            pltpu.VMEM((SLOTS, width), BF16),
            pltpu.VMEM((2, width, SLOTS), BF16),
            pltpu.VMEM((2, SLOTS, width), BF16),
            pltpu.VMEM((width, width), BF16),
            pltpu.VMEM((SLOTS, width), F32),
        ),
        cost_estimate=pl.CostEstimate(flops=4 * work * width, transcendentals=work, bytes_accessed=2 * work),
        name="forward",
    )(*inputs)
    attn_other = other_core(attn_send)
    (packed_attn,) = simple_call(
        functools.partial(ungroup_kernel, regions, capacity),
        (shape((regions, capacity, half), BF16),),
        (landing, attn_keep, attn_other),
    )

    g_mine, g_theirs = simple_call(
        functools.partial(regroup_kernel, regions, capacity), (rows_shape, rows_shape), (landing, got_cot)
    )
    g_other = other_core(g_theirs)

    unit = 16 * regions
    grad_rows = -(-(4 * width + KIND_ROWS + 16) // unit) * unit
    inputs = (core, mine, other, g_mine, g_other, w_own, w_other, gain, info, queries, keys, values, exps, context, inv)
    outs = (rows_shape, rows_shape, shape((grad_rows, half), F32), shape((grad_rows, half), BF16))
    d_keep, d_send, grad_keep, grad_send = pl.pallas_call(
        functools.partial(backward_kernel, heads),
        grid=(heads,),
        out_shape=outs,
        in_specs=[SMEM_SPEC] + [exps_spec if x is exps else whole(x) for x in inputs[1:]],
        out_specs=tuple(whole(x) for x in outs),
        scratch_shapes=(
            pltpu.VMEM((2, width, SLOTS), BF16),
            pltpu.VMEM((width, SLOTS), BF16),
            pltpu.VMEM((SLOTS, width), BF16),
            pltpu.VMEM((width, SLOTS), BF16),
            pltpu.VMEM((LANES, SLOTS), F32),
            pltpu.VMEM((SLOTS, width), F32),
            pltpu.VMEM((width, SLOTS), F32),
            pltpu.VMEM((width, SLOTS), F32),
        ),
        cost_estimate=pl.CostEstimate(flops=8 * work * width, transcendentals=0, bytes_accessed=2 * work),
        name="backward",
    )(*inputs)

    def pick(home):
        (rows,) = simple_call(pick_kernel, (shape((count, half), BF16),), (target, home))
        return rows

    share = grad_rows // regions
    (packed_grad,) = simple_call(
        functools.partial(ungroup_kernel, regions, capacity),
        (shape((regions, capacity + share, half), BF16),),
        (landing, d_keep, other_core(d_send), grad_keep, other_core(grad_send)),
    )
    got_cot, packed_attn = lax.optimization_barrier((got_cot, packed_attn))
    home_attn = exchange(packed_attn)
    home_attn, packed_grad = lax.optimization_barrier((home_attn, packed_grad))
    home_grad = exchange(packed_grad)
    (shares,) = simple_call(
        functools.partial(share_kernel, regions, capacity), (shape((regions, share, half), BF16),), (home_grad,)
    )
    summed = exchange(shares)
    attended = pick(home_attn)
    grad_feats = pick(home_grad)
    column_shape = shape((width, half), F32)
    grad_q, grad_k, grad_v, grad_o, grad_gain, grad_embed = simple_call(
        functools.partial(spread_kernel, float(count * regions) ** (-0.5)),
        (column_shape, column_shape, column_shape, shape((half, width), F32), shape((1, width), F32), shape((KINDS, half), F32)),
        (summed,),
    )
    return (attended, grad_feats, grad_q, grad_k, grad_v, grad_o, grad_gain.reshape(width), grad_embed)


def solution(mesh):
    placed = (
        P(("groups", "region"), "head"),
        P(("groups", "region")),
        P(("groups", "region")),
        P(None, "head"),
        P(),
        P(None, "head"),
        P(None, "head"),
        P(None, "head"),
        P("head", None),
        P(("groups", "region"), "head"),
    )

    return jax.shard_map(
        on_device,
        mesh=mesh,
        in_specs=placed,
        out_specs=(
            P(("groups", "region"), "head"),
            P(("groups", "region"), "head"),
            P("groups", "head"),
            P("groups", "head"),
            P("groups", "head"),
            P(("groups", "head"), None),
            P("groups"),
            P("groups", "head"),
        ),
        check_vma=False,
    )
```

```python
import functools

import jax
import jax.numpy as jnp
from jax import lax
from jax.experimental import pallas as pl
from jax.experimental.pallas import tpu as pltpu
from jax.sharding import PartitionSpec as P


HEAD_DIM = 32
KINDS = 12
SLOTS = 1024
BINS_DEV = 2
MASKED = -1000000000.0
EPSILON = 1e-06
LOG2E = 1.4426950408889634

F32 = jnp.float32
BF16 = jnp.bfloat16
I32 = jnp.int32
LANES = 128
TAG_ROWS = 16
KIND_ROWS = 16
NT = (((1,), (1,)), ((), ()))
TN = (((0,), (0,)), ((), ()))


def iota(shape, axis):
    return lax.broadcasted_iota(I32, shape, axis)


def mm(a, b):
    return jnp.dot(a, b, preferred_element_type=F32)


def mm_nt(a, b):
    return lax.dot_general(a, b, NT, preferred_element_type=F32)


def mm_tn(a, b):
    return lax.dot_general(a, b, TN, preferred_element_type=F32)


def hot(condition):
    return jnp.where(condition, 1.0, 0.0).astype(BF16)


def log2_of(n):
    return n.bit_length() - 1


def positions(regions, capacity, cell):
    count = cell.shape[1]
    local_rows = BINS_DEV * SLOTS
    owner = lax.shift_right_logical(cell, log2_of(local_rows))
    group = lax.shift_right_logical(cell, log2_of(SLOTS))
    classes = max(BINS_DEV * regions, 16)
    group_hot = jnp.where(iota((classes, count), 0) == group, 1.0, 0.0)
    before = hot(iota((count, count), 0) < iota((count, count), 1))
    rank = jnp.sum(mm(group_hot.astype(BF16), before) * group_hot, axis=0, keepdims=True).astype(I32)
    second = jnp.bitwise_and(group, 1) > 0
    target = owner * capacity + jnp.where(second, capacity - 1 - rank, rank)
    return target, jnp.sum(group_hot, axis=1, keepdims=True)


def pack_kernel(regions, capacity, cells, kinds, feats, embed, w_q, w_k, w_v, w_o, out_base, out_target, out_w):
    count, half = feats.shape
    target, counts = positions(regions, capacity, cells[...])
    out_target[...] = target
    kinds_hot = hot(iota((KINDS, count), 0) == kinds[...])
    base = (feats[...].astype(F32) + mm_tn(kinds_hot, embed[...])).astype(BF16)
    place = iota((TAG_ROWS, half), 0)
    for r in range(regions):
        chosen = hot(iota((capacity, count), 0) + r * capacity == target)
        out_base[r, 0:capacity, :] = mm(chosen, base).astype(BF16)
        first = counts[2 * r : 2 * r + 1]
        second = counts[2 * r + 1 : 2 * r + 2]
        tags = jnp.where(place == 0, first, jnp.where(place == 1, second, 0.0))
        out_base[r, capacity : capacity + TAG_ROWS, :] = tags.astype(BF16)
    out_w[0] = w_q[...]
    out_w[1] = w_k[...]
    out_w[2] = w_v[...]
    out_w[3, 0:half, :] = w_o[:, 0:half]
    out_w[3, half:, :] = w_o[:, half:]


def pack_cot_kernel(regions, capacity, target_ref, kinds, cot, out_cot):
    count = cot.shape[0]
    target = target_ref[...]
    rows = cot[...]
    tags = jnp.where(iota((TAG_ROWS, count), 0) == 0, kinds[...] + 1, 0).astype(F32).astype(BF16)
    for r in range(regions):
        chosen = hot(iota((capacity, count), 0) + r * capacity == target)
        out_cot[r, 0:capacity, :] = mm(chosen, rows).astype(BF16)
        tag = mm_nt(tags, chosen)
        if capacity >= LANES:
            tag = jnp.concatenate([tag[0:8, 0:LANES], tag[0:8, LANES : 2 * LANES]], axis=0)
        else:
            tag = jnp.concatenate([tag, jnp.zeros((TAG_ROWS, LANES - capacity), F32)], axis=1)
        out_cot[r, capacity : capacity + TAG_ROWS, :] = tag.astype(BF16)


def place_rows(regions, capacity, got, marks, front, back):
    for r in range(regions):
        rows = got[r, 0:capacity, :].astype(F32)
        front[pl.ds(marks[0, r], capacity), :] = rows
        back[pl.ds(marks[1, r], capacity), :] = rows


def bins_of(regions, capacity, core, marks, front, back):
    row = iota((SLOTS, 1), 0)
    first = jnp.where(row < marks[0, regions], front[0:SLOTS, :], 0.0)
    second = jnp.where(row >= marks[1, regions], back[capacity : capacity + SLOTS, :], 0.0)
    flag = core[0] > 0
    return jnp.where(flag, second, first).astype(BF16), jnp.where(flag, first, second).astype(BF16)


def group_kernel(regions, capacity, core, got, mine, theirs, keep, marks, front, back):
    start = jnp.int32(0)
    end = jnp.int32(SLOTS)
    for r in range(regions):
        block = got[r, capacity : capacity + TAG_ROWS, :].astype(F32)
        marks[0, r] = start
        marks[1, r] = end
        start = start + jnp.max(block[0:1, :]).astype(I32)
        end = end - jnp.max(block[1:2, :]).astype(I32)
    marks[0, regions] = start
    marks[1, regions] = end
    place_rows(regions, capacity, got, marks, front, back)
    mine[...], theirs[...] = bins_of(regions, capacity, core, marks, front, back)
    lane = iota((8, SLOTS), 1)
    filled = jnp.where(core[0] > 0, jnp.where(lane >= end, 1.0, 0.0), jnp.where(lane < start, 1.0, 0.0))
    keep[...] = filled


def regroup_kernel(regions, capacity, core, marks, got, mine, theirs, front, back):
    place_rows(regions, capacity, got, marks, front, back)
    mine[...], theirs[...] = bins_of(regions, capacity, core, marks, front, back)


def arrival_rows(regions, capacity, core, marks, own, other, out, front, back):
    flag = core[0] > 0
    x = own[...].astype(F32)
    y = other[...].astype(F32)
    front[0:SLOTS, :] = jnp.where(flag, y, x)
    front[SLOTS:, :] = jnp.zeros((capacity, x.shape[1]), F32)
    back[0:capacity, :] = jnp.zeros((capacity, x.shape[1]), F32)
    back[capacity:, :] = jnp.where(flag, x, y)
    row = iota((capacity, 1), 0)
    for r in range(regions):
        held = marks[0, r + 1] - marks[0, r]
        rows = jnp.where(row < held, front[pl.ds(marks[0, r], capacity), :], back[pl.ds(marks[1, r], capacity), :])
        out[r, 0:capacity, :] = rows.astype(BF16)


def ungroup_kernel(regions, capacity, core, marks, own, other, out, front, back):
    arrival_rows(regions, capacity, core, marks, own, other, out, front, back)


def ungroup_grad_kernel(regions, capacity, core, marks, own, other, tagged, out, embed, front, back):
    arrival_rows(regions, capacity, core, marks, own, other, out, front, back)
    total = jnp.zeros((KIND_ROWS, own.shape[1]), F32)
    for r in range(regions):
        block = tagged[r, capacity : capacity + TAG_ROWS, :].astype(F32)
        if capacity >= LANES:
            kind = jnp.concatenate([block[0:1], block[8:9]], axis=1)
        else:
            kind = block[0:1, 0:capacity]
        kinds_hot = hot(iota((KIND_ROWS, capacity), 0) == kind.astype(I32) - 1)
        total = total + mm(kinds_hot, out[r, 0:capacity, :])
    embed[...] = total


def pair_kernel(regions, region, own, received, out_wide, out_low):
    share = out_wide.shape[1]
    for j in range(regions):
        first = pl.multiple_of(jnp.bitwise_xor(region[0], j) * share, share)
        total = own[pl.ds(first, share), :] + received[pl.ds(first, share), :].astype(F32)
        out_wide[j] = total
        out_low[j] = total.astype(BF16)


def spread_kernel(regions, factor, region, got, out_q, out_k, out_v, out_o, out_gain, out_embed, flat):
    width, half = out_q.shape
    share = 4 * width // regions
    extra = jnp.zeros((KIND_ROWS + 16, half), F32)
    for r in range(regions):
        chunk = got[jnp.bitwise_xor(region[0], r)].astype(F32) * factor
        flat[r * share : (r + 1) * share, :] = chunk[0:share]
        extra = extra + chunk[share : share + KIND_ROWS + 16]
    out_q[...] = flat[0:width]
    out_k[...] = flat[width : 2 * width]
    out_v[...] = flat[2 * width : 3 * width]
    out_o[:, 0:half] = flat[3 * width : 3 * width + half]
    out_o[:, half:] = flat[3 * width + half : 4 * width]
    out_embed[...] = extra[0:KINDS]
    out_gain[:, 0:half] = extra[KIND_ROWS : KIND_ROWS + 1]
    out_gain[:, half:] = extra[KIND_ROWS + 1 : KIND_ROWS + 2]


def pick_kernel(target_ref, got, out):
    capacity = BINS_DEV * SLOTS // got.shape[0]
    total = got.shape[0] * capacity
    count = out.shape[0]
    column = jnp.transpose(jnp.broadcast_to(target_ref[...].astype(F32), (8, count)))[:, 0:1].astype(I32)
    flat = got[:, 0:capacity, :].reshape(total, got.shape[2])
    step = 256
    for s in range(0, count, step):
        chosen = hot(iota((step, total), 1) == column[s : s + step])
        out[s : s + step, :] = mm(chosen, flat).astype(BF16)


def ordered(flag, own, other):
    first = jnp.where(flag, other, own)
    second = jnp.where(flag, own, other)
    return first, second


def full_weights(core, own, other):
    flag = core[0] > 0
    half = own.shape[2]
    columns = []
    for k in range(3):
        columns.append(jnp.concatenate(ordered(flag, own[k], other[k]), axis=1))
    top, bottom = ordered(flag, own[3], other[3])
    rows = [jnp.concatenate([part[0:half], part[half:]], axis=1) for part in (top, bottom)]
    return columns + [jnp.concatenate(rows, axis=0)]


def norm_rows(slab, gain, width):
    wide = slab.astype(F32)
    inverse = lax.rsqrt(jnp.sum(wide * wide, axis=1, keepdims=True) / width + EPSILON)
    return wide, inverse, (wide * inverse * gain).astype(BF16)


def spare_lanes(h, heads):
    last = heads * HEAD_DIM - 1
    is_last = h == heads - 1
    return jnp.where(is_last, 0, last), jnp.where(is_last, 1, last - 1)


def forward_kernel(
    heads, core, mine, other, w_own, w_other, gain, info, queries_out, keys_out, values_out, exps_out, context_out, inv_out,
    keep_out, send_out, queries, keys_t, values, w_out, context
):
    h = pl.program_id(0)
    width = heads * HEAD_DIM
    half = width // 2
    flag = core[0] > 0
    lane = iota((1, width), 1)
    scale = HEAD_DIM**-0.5

    @pl.when(h == 0)
    def _():
        w_q, w_k, w_v, w_o = full_weights(core, w_own, w_other)
        w_out[...] = w_o
        slab = jnp.concatenate(ordered(flag, mine[...], other[...]), axis=1)
        _, _, normed = norm_rows(slab, gain[...], width)
        q = mm(normed, w_q).astype(BF16)
        queries[...] = q
        queries_out[...] = q
        k = mm(normed, w_k)
        k_low = k.astype(BF16)
        keys_out[...] = k_low
        k_t = jnp.transpose(k_low.astype(F32))
        bias = jnp.where(info[0:1, :] > 0.5, 0.0, MASKED / scale)
        row = iota(k_t.shape, 0)
        keys_t[0] = jnp.where(row == width - 1, bias, k_t).astype(BF16)
        keys_t[1] = jnp.where(row == 0, bias, k_t).astype(BF16)
        v = mm(normed, w_v).astype(BF16)
        values_out[...] = v
        v_wide = v.astype(F32)
        values[0] = jnp.where(lane == width - 1, 1.0, v_wide).astype(BF16)
        values[1] = jnp.where(lane == 0, 1.0, v_wide).astype(BF16)
        inv_out[...] = jnp.zeros_like(inv_out)

    spare, _ = spare_lanes(h, heads)
    side = jnp.where(h == heads - 1, 1, 0)
    own_lane = lax.shift_right_logical(lane, log2_of(HEAD_DIM)) == h
    step = 256
    for s in range(0, SLOTS, step):
        rows = slice(s, s + step)
        q = jnp.where(own_lane, queries[rows, :].astype(F32), jnp.where(lane == spare, 1.0, 0.0)).astype(BF16)
        scores = mm(q, keys_t[side])
        top = jnp.max(scores, axis=1, keepdims=True)
        exps = jnp.exp2((scores - top) * (scale * LOG2E)).astype(BF16)
        exps_out[0, rows, :] = exps
        summed = mm(exps, values[side])
        inv = 1.0 / jnp.sum(jnp.where(lane == spare, summed, 0.0), axis=1, keepdims=True)
        context[rows, :] = jnp.where(own_lane, summed * inv, context[rows, :])
        lane_small = iota((1, LANES), 1)
        inv_out[rows, :] = jnp.where(lane_small == h, inv, inv_out[rows, :])

    @pl.when(h == heads - 1)
    def _():
        context_out[...] = context[...]
        rows_out = mm(context[...].astype(BF16), w_out[...]).astype(BF16)
        keep_out[...] = jnp.where(flag, rows_out[:, half:], rows_out[:, :half])
        send_out[...] = jnp.where(flag, rows_out[:, :half], rows_out[:, half:])


def backward_kernel(
    heads, core, mine, other, g_mine, g_other, w_own, w_other, gain, info, queries_in, keys_in, values_in, exps_in, context_in,
    inv_in, keep_out, send_out, grad_keep, grad_send, values_t, queries_t, d_context, d_context_t, inv_t, d_query, d_key_t, d_value_t
):
    h = pl.program_id(0)
    width = heads * HEAD_DIM
    half = width // 2
    flag = core[0] > 0
    lane = iota((1, width), 1)
    lane_small = iota((1, LANES), 1)
    scale = HEAD_DIM**-0.5

    def grad_rows():
        return jnp.concatenate(ordered(flag, g_mine[...], g_other[...]), axis=1)

    @pl.when(h == 0)
    def _():
        w_o = full_weights(core, w_own, w_other)[3]
        dc = mm_nt(grad_rows(), w_o).astype(BF16)
        d_context[...] = dc
        d_context_t[...] = jnp.transpose(dc.astype(F32)).astype(BF16)
        inv_t[...] = jnp.transpose(inv_in[...])
        v_t = jnp.transpose(values_in[...].astype(F32))
        row = iota(v_t.shape, 0)
        values_t[0] = jnp.where(row >= width - 2, 1.0, v_t).astype(BF16)
        values_t[1] = jnp.where(row <= 1, 1.0, v_t).astype(BF16)
        queries_t[...] = jnp.transpose(queries_in[...].astype(F32)).astype(BF16)

    spare, spare_low = spare_lanes(h, heads)
    side = jnp.where(h == heads - 1, 1, 0)
    own_lane = lax.shift_right_logical(lane, log2_of(HEAD_DIM)) == h
    base = pl.multiple_of(h * HEAD_DIM, HEAD_DIM)
    head_rows = pl.ds(base, HEAD_DIM)
    inv_row = inv_t[pl.ds(h, 1), :]
    step = 256
    dk = jnp.zeros((HEAD_DIM, SLOTS), F32)
    dv = jnp.zeros((HEAD_DIM, SLOTS), F32)
    for s in range(0, SLOTS, step):
        rows = slice(s, s + step)
        inv = jnp.sum(jnp.where(lane_small == h, inv_in[rows, :], 0.0), axis=1, keepdims=True)
        scaled = jnp.where(own_lane, d_context[rows, :].astype(F32) * inv, 0.0).astype(BF16)
        wide = scaled.astype(F32)
        dot = -jnp.sum(wide * context_in[rows, :], axis=1, keepdims=True)
        dot_high = dot.astype(BF16).astype(F32)
        dot_low = dot - dot_high
        left = jnp.where(lane == spare, dot_high, jnp.where(lane == spare_low, dot_low, wide)).astype(BF16)
        centred = mm(left, values_t[side])
        exps = exps_in[0, rows, :]
        d_scores = (exps.astype(F32) * centred).astype(BF16)
        dq = mm(d_scores, keys_in[...])
        d_query[rows, :] = jnp.where(own_lane, dq * scale, d_query[rows, :])
        dk = dk + mm(queries_t[head_rows, rows], d_scores)
        scaled_t = (d_context_t[head_rows, rows].astype(F32) * inv_row[:, rows]).astype(BF16)
        dv = dv + mm(scaled_t, exps)
    d_key_t[head_rows, :] = dk * scale
    d_value_t[head_rows, :] = dv

    @pl.when(h == heads - 1)
    def _():
        w_q, w_k, w_v, _ = full_weights(core, w_own, w_other)
        slab = jnp.concatenate(ordered(flag, mine[...], other[...]), axis=1)
        wide, inverse, normed = norm_rows(slab, gain[...], width)
        dq = d_query[...].astype(BF16)
        dk = jnp.transpose(d_key_t[...]).astype(BF16)
        dv = jnp.transpose(d_value_t[...]).astype(BF16)
        d_normed = mm_nt(dq, w_q) + mm_nt(dk, w_k) + mm_nt(dv, w_v)
        scaled = gain[...] * d_normed
        along = jnp.sum(scaled * wide, axis=1, keepdims=True)
        d_slab = (inverse * scaled - wide * (inverse * inverse * inverse) * along / width).astype(BF16)
        keep_out[...] = jnp.where(flag, d_slab[:, half:], d_slab[:, :half])
        send_out[...] = jnp.where(flag, d_slab[:, :half], d_slab[:, half:])
        normed_t = jnp.transpose(normed.astype(F32)).astype(BF16)
        context_t = jnp.transpose(context_in[...]).astype(BF16)
        place = 0
        for d_rows in (dq, dk, dv):
            grad = mm(normed_t, d_rows)
            grad_keep[place : place + width, :] = jnp.where(flag, grad[:, half:], grad[:, :half])
            grad_send[place : place + width, :] = jnp.where(flag, grad[:, :half], grad[:, half:]).astype(BF16)
            place += width
        grad = mm(context_t, grad_rows())
        for part in range(2):
            block = grad[:, part * half : (part + 1) * half]
            grad_keep[place : place + half, :] = jnp.where(flag, block[half:], block[:half])
            grad_send[place : place + half, :] = jnp.where(flag, block[:half], block[half:]).astype(BF16)
            place += half
        gain_grad = jnp.sum(d_normed * wide * inverse, axis=0, keepdims=True)
        pick = iota((16, half), 0)
        block = jnp.where(pick == 0, gain_grad[:, :half], jnp.where(pick == 1, gain_grad[:, half:], 0.0))
        grad_keep[place : place + 16, :] = block
        grad_send[place : place + 16, :] = block.astype(BF16)


def shape(dims, dtype):
    return jax.ShapeDtypeStruct(tuple(dims), dtype)


SMEM_SPEC = pl.BlockSpec(memory_space=pltpu.SMEM)


def whole(array):
    zeros = (0,) * len(array.shape)
    return pl.BlockSpec(tuple(array.shape), lambda *_: zeros)


def simple_call(kernel, outs, inputs, scratch=(), scalars=0, scalar_outs=0):
    specs = [SMEM_SPEC] * scalars + [whole(x) for x in inputs[scalars:]]
    return pl.pallas_call(
        kernel,
        out_shape=outs,
        in_specs=specs,
        out_specs=tuple(whole(x) for x in outs[: len(outs) - scalar_outs]) + (SMEM_SPEC,) * scalar_outs,
        scratch_shapes=scratch,
    )(*inputs)


def on_device(
    features,
    element_kinds,
    bin_cells,
    kind_embed,
    norm_gain,
    w_query,
    w_key,
    w_value,
    w_out,
    cotangent,
):
    regions = lax.axis_size("region")
    cores = lax.axis_size("head")
    local_rows = BINS_DEV * SLOTS
    capacity = local_rows // regions
    count, half = features.shape
    width = w_query.shape[0]
    heads = width // HEAD_DIM
    assert cores == BINS_DEV and half * cores == width and half == LANES
    core = lax.axis_index("head").astype(I32).reshape(1)
    swap = [(i, (i + 1) % cores) for i in range(cores)]

    def other_core(x):
        return lax.ppermute(x, "head", swap)

    def exchange(x):
        return lax.all_to_all(x, "region", split_axis=0, concat_axis=0, tiled=True)

    gain = norm_gain.reshape(1, width)
    kinds_row = element_kinds.reshape(1, count)
    packed_shape = shape((regions, capacity, half), BF16)
    tagged_shape = shape((regions, capacity + TAG_ROWS, half), BF16)
    packed_base, target, w_own = simple_call(
        functools.partial(pack_kernel, regions, capacity),
        (tagged_shape, shape((1, count), I32), shape((4, width, half), BF16)),
        (bin_cells.reshape(1, count), kinds_row, features, kind_embed, w_query, w_key, w_value, w_out),
    )
    w_other = other_core(w_own)
    got_base = exchange(packed_base)
    (packed_cot,) = simple_call(
        functools.partial(pack_cot_kernel, regions, capacity), (tagged_shape,), (target, kinds_row, cotangent)
    )
    got_base, packed_cot = lax.optimization_barrier((got_base, packed_cot))
    got_cot = exchange(packed_cot)
    rows_shape = shape((SLOTS, half), BF16)
    lift = pltpu.VMEM((SLOTS + capacity, half), F32)
    mine, theirs, info, marks = simple_call(
        functools.partial(group_kernel, regions, capacity),
        (rows_shape, rows_shape, shape((8, SLOTS), F32), shape((2, regions + 1), I32)),
        (core, got_base),
        scratch=(lift, lift),
        scalars=1,
        scalar_outs=1,
    )
    other = other_core(theirs)

    full_shape = shape((SLOTS, width), BF16)
    exps_shape = shape((heads, SLOTS, SLOTS), BF16)
    exps_spec = pl.BlockSpec((1, SLOTS, SLOTS), lambda h: (h, 0, 0))
    inputs = (core, mine, other, w_own, w_other, gain, info)
    outs = (
        full_shape,
        full_shape,
        full_shape,
        exps_shape,
        shape((SLOTS, width), F32),
        shape((SLOTS, LANES), F32),
        rows_shape,
        rows_shape,
    )
    work = heads * SLOTS * SLOTS
    queries, keys, values, exps, context, inv, attn_keep, attn_send = pl.pallas_call(
        functools.partial(forward_kernel, heads),
        grid=(heads,),
        out_shape=outs,
        in_specs=[SMEM_SPEC] + [whole(x) for x in inputs[1:]],
        out_specs=tuple(exps_spec if x is exps_shape else whole(x) for x in outs),
        scratch_shapes=(
            pltpu.VMEM((SLOTS, width), BF16),
            pltpu.VMEM((2, width, SLOTS), BF16),
            pltpu.VMEM((2, SLOTS, width), BF16),
            pltpu.VMEM((width, width), BF16),
            pltpu.VMEM((SLOTS, width), F32),
        ),
        cost_estimate=pl.CostEstimate(flops=4 * work * width, transcendentals=work, bytes_accessed=2 * work),
        name="forward",
    )(*inputs)
    attn_other = other_core(attn_send)
    (packed_attn,) = simple_call(
        functools.partial(ungroup_kernel, regions, capacity),
        (packed_shape,),
        (core, marks, attn_keep, attn_other),
        scratch=(lift, lift),
        scalars=2,
    )

    g_mine, g_theirs = simple_call(
        functools.partial(regroup_kernel, regions, capacity),
        (rows_shape, rows_shape),
        (core, marks, got_cot),
        scratch=(lift, lift),
        scalars=2,
    )
    g_other = other_core(g_theirs)

    grad_rows = 4 * width + 16
    inputs = (core, mine, other, g_mine, g_other, w_own, w_other, gain, info, queries, keys, values, exps, context, inv)
    outs = (rows_shape, rows_shape, shape((grad_rows, half), F32), shape((grad_rows, half), BF16))
    d_keep, d_send, grad_keep, grad_send = pl.pallas_call(
        functools.partial(backward_kernel, heads),
        grid=(heads,),
        out_shape=outs,
        in_specs=[SMEM_SPEC] + [exps_spec if x is exps else whole(x) for x in inputs[1:]],
        out_specs=tuple(whole(x) for x in outs),
        scratch_shapes=(
            pltpu.VMEM((2, width, SLOTS), BF16),
            pltpu.VMEM((width, SLOTS), BF16),
            pltpu.VMEM((SLOTS, width), BF16),
            pltpu.VMEM((width, SLOTS), BF16),
            pltpu.VMEM((LANES, SLOTS), F32),
            pltpu.VMEM((SLOTS, width), F32),
            pltpu.VMEM((width, SLOTS), F32),
            pltpu.VMEM((width, SLOTS), F32),
        ),
        cost_estimate=pl.CostEstimate(flops=8 * work * width, transcendentals=0, bytes_accessed=2 * work),
        name="backward",
    )(*inputs)

    def pick(home):
        (rows,) = simple_call(pick_kernel, (shape((count, half), BF16),), (target, home))
        return rows

    packed_grad, embed_part = simple_call(
        functools.partial(ungroup_grad_kernel, regions, capacity),
        (packed_shape, shape((KIND_ROWS, half), F32)),
        (core, marks, d_keep, other_core(d_send), got_cot),
        scratch=(lift, lift),
        scalars=2,
    )
    got_cot, packed_attn = lax.optimization_barrier((got_cot, packed_attn))
    home_attn = exchange(packed_attn)
    home_attn, packed_grad = lax.optimization_barrier((home_attn, packed_grad))
    home_grad = exchange(packed_grad)

    region = lax.axis_index("region").astype(I32).reshape(1)
    share = 4 * width // regions
    grad_other = other_core(grad_send)
    wide, low = simple_call(
        functools.partial(pair_kernel, regions),
        (shape((regions, share, half), F32), shape((regions, share, half), BF16)),
        (region, grad_keep, grad_other),
        scalars=1,
    )
    gain_part = grad_keep[4 * width :] + grad_other[4 * width :].astype(F32)

    def partner(x, bit):
        return lax.ppermute(x, "region", [(i, i ^ bit) for i in range(regions)])

    bit = regions // 2
    while bit:
        got = partner(low[bit : 2 * bit], bit)
        wide = wide[:bit] + got.astype(F32)
        low = wide.astype(BF16)
        bit //= 2
    gathered = jnp.concatenate([low[0], embed_part.astype(BF16), gain_part.astype(BF16)], axis=0)[None]
    bit = 1
    while bit < regions:
        gathered = jnp.concatenate([gathered, partner(gathered, bit)], axis=0)
        bit *= 2
    column_shape = shape((width, half), F32)
    grad_q, grad_k, grad_v, grad_o, grad_gain, grad_embed = simple_call(
        functools.partial(spread_kernel, regions, float(count * regions) ** (-0.5)),
        (column_shape, column_shape, column_shape, shape((half, width), F32), shape((1, width), F32), shape((KINDS, half), F32)),
        (region, gathered),
        scratch=(pltpu.VMEM((4 * width, half), F32),),
        scalars=1,
    )
    attended = pick(home_attn)
    grad_feats = pick(home_grad)
    return (attended, grad_feats, grad_q, grad_k, grad_v, grad_o, grad_gain.reshape(width), grad_embed)


def solution(mesh):
    placed = (
        P(("groups", "region"), "head"),
        P(("groups", "region")),
        P(("groups", "region")),
        P(None, "head"),
        P(),
        P(None, "head"),
        P(None, "head"),
        P(None, "head"),
        P("head", None),
        P(("groups", "region"), "head"),
    )

    return jax.shard_map(
        on_device,
        mesh=mesh,
        in_specs=placed,
        out_specs=(
            P(("groups", "region"), "head"),
            P(("groups", "region"), "head"),
            P("groups", "head"),
            P("groups", "head"),
            P("groups", "head"),
            P(("groups", "head"), None),
            P("groups"),
            P("groups", "head"),
        ),
        check_vma=False,
    )
```

```python
import functools

import jax
import jax.numpy as jnp
from jax import lax
from jax.experimental import pallas as pl
from jax.experimental.pallas import tpu as pltpu
from jax.sharding import PartitionSpec as P


HEAD_DIM = 32
KINDS = 12
SLOTS = 1024
BINS_DEV = 2
MASKED = -1000000000.0
EPSILON = 1e-06
LOG2E = 1.4426950408889634

F32 = jnp.float32
BF16 = jnp.bfloat16
I32 = jnp.int32
LANES = 128
TAG_ROWS = 16
KIND_ROWS = 16
NT = (((1,), (1,)), ((), ()))
TN = (((0,), (0,)), ((), ()))


def iota(shape, axis):
    return lax.broadcasted_iota(I32, shape, axis)


def mm(a, b):
    return jnp.dot(a, b, preferred_element_type=F32)


def mm_nt(a, b):
    return lax.dot_general(a, b, NT, preferred_element_type=F32)


def mm_tn(a, b):
    return lax.dot_general(a, b, TN, preferred_element_type=F32)


def hot(condition):
    return jnp.where(condition, 1.0, 0.0).astype(BF16)


def log2_of(n):
    return n.bit_length() - 1


def positions(regions, capacity, cell):
    count = cell.shape[1]
    local_rows = BINS_DEV * SLOTS
    owner = lax.shift_right_logical(cell, log2_of(local_rows))
    group = lax.shift_right_logical(cell, log2_of(SLOTS))
    classes = max(BINS_DEV * regions, 16)
    group_hot = jnp.where(iota((classes, count), 0) == group, 1.0, 0.0)
    before = hot(iota((count, count), 0) < iota((count, count), 1))
    rank = jnp.sum(mm(group_hot.astype(BF16), before) * group_hot, axis=0, keepdims=True).astype(I32)
    second = jnp.bitwise_and(group, 1) > 0
    target = owner * capacity + jnp.where(second, capacity - 1 - rank, rank)
    return target, jnp.sum(group_hot, axis=1, keepdims=True)


def pack_kernel(regions, capacity, cells, kinds, feats, embed, w_q, w_k, w_v, w_o, out_base, out_target, out_w):
    count, half = feats.shape
    target, counts = positions(regions, capacity, cells[...])
    out_target[...] = target
    kinds_hot = hot(iota((KINDS, count), 0) == kinds[...])
    base = (feats[...].astype(F32) + mm_tn(kinds_hot, embed[...])).astype(BF16)
    place = iota((TAG_ROWS, half), 0)
    for r in range(regions):
        chosen = hot(iota((capacity, count), 0) + r * capacity == target)
        out_base[r, 0:capacity, :] = mm(chosen, base).astype(BF16)
        first = counts[2 * r : 2 * r + 1]
        second = counts[2 * r + 1 : 2 * r + 2]
        tags = jnp.where(place == 0, first, jnp.where(place == 1, second, 0.0))
        out_base[r, capacity : capacity + TAG_ROWS, :] = tags.astype(BF16)
    out_w[0] = w_q[...]
    out_w[1] = w_k[...]
    out_w[2] = w_v[...]
    out_w[3, 0:half, :] = w_o[:, 0:half]
    out_w[3, half:, :] = w_o[:, half:]


def pack_cot_kernel(regions, capacity, target_ref, kinds, cot, out_cot):
    count = cot.shape[0]
    target = target_ref[...]
    rows = cot[...]
    tags = jnp.where(iota((TAG_ROWS, count), 0) == 0, kinds[...] + 1, 0).astype(F32).astype(BF16)
    for r in range(regions):
        chosen = hot(iota((capacity, count), 0) + r * capacity == target)
        out_cot[r, 0:capacity, :] = mm(chosen, rows).astype(BF16)
        tag = mm_nt(tags, chosen)
        if capacity >= LANES:
            tag = jnp.concatenate([tag[0:8, 0:LANES], tag[0:8, LANES : 2 * LANES]], axis=0)
        else:
            tag = jnp.concatenate([tag, jnp.zeros((TAG_ROWS, LANES - capacity), F32)], axis=1)
        out_cot[r, capacity : capacity + TAG_ROWS, :] = tag.astype(BF16)


def place_rows(regions, capacity, got, marks, front, back):
    for r in range(regions):
        rows = got[r, 0:capacity, :].astype(F32)
        front[pl.ds(marks[0, r], capacity), :] = rows
        back[pl.ds(marks[1, r], capacity), :] = rows


def bins_of(regions, capacity, core, marks, front, back):
    row = iota((SLOTS, 1), 0)
    first = jnp.where(row < marks[0, regions], front[0:SLOTS, :], 0.0)
    second = jnp.where(row >= marks[1, regions], back[capacity : capacity + SLOTS, :], 0.0)
    flag = core[0] > 0
    return jnp.where(flag, second, first).astype(BF16), jnp.where(flag, first, second).astype(BF16)


def group_kernel(regions, capacity, core, got, mine, theirs, keep, marks, front, back):
    start = jnp.int32(0)
    end = jnp.int32(SLOTS)
    for r in range(regions):
        block = got[r, capacity : capacity + TAG_ROWS, :].astype(F32)
        marks[0, r] = start
        marks[1, r] = end
        start = start + jnp.max(block[0:1, :]).astype(I32)
        end = end - jnp.max(block[1:2, :]).astype(I32)
    marks[0, regions] = start
    marks[1, regions] = end
    place_rows(regions, capacity, got, marks, front, back)
    mine[...], theirs[...] = bins_of(regions, capacity, core, marks, front, back)
    lane = iota((8, SLOTS), 1)
    filled = jnp.where(core[0] > 0, jnp.where(lane >= end, 1.0, 0.0), jnp.where(lane < start, 1.0, 0.0))
    keep[...] = filled


def regroup_kernel(regions, capacity, core, marks, got, mine, theirs, front, back):
    place_rows(regions, capacity, got, marks, front, back)
    mine[...], theirs[...] = bins_of(regions, capacity, core, marks, front, back)


def arrival_rows(regions, capacity, core, marks, own, other, out, front, back):
    flag = core[0] > 0
    x = own[...].astype(F32)
    y = other[...].astype(F32)
    front[0:SLOTS, :] = jnp.where(flag, y, x)
    front[SLOTS:, :] = jnp.zeros((capacity, x.shape[1]), F32)
    back[0:capacity, :] = jnp.zeros((capacity, x.shape[1]), F32)
    back[capacity:, :] = jnp.where(flag, x, y)
    row = iota((capacity, 1), 0)
    for r in range(regions):
        held = marks[0, r + 1] - marks[0, r]
        rows = jnp.where(row < held, front[pl.ds(marks[0, r], capacity), :], back[pl.ds(marks[1, r], capacity), :])
        out[r, 0:capacity, :] = rows.astype(BF16)


def ungroup_kernel(regions, capacity, core, marks, own, other, out, front, back):
    arrival_rows(regions, capacity, core, marks, own, other, out, front, back)


def ungroup_grad_kernel(regions, capacity, core, marks, own, other, tagged, grad_own, grad_other, out, extra, front, back):
    arrival_rows(regions, capacity, core, marks, own, other, out, front, back)
    total = jnp.zeros((KIND_ROWS, own.shape[1]), F32)
    share = out.shape[1] - capacity
    for r in range(regions):
        block = tagged[r, capacity : capacity + TAG_ROWS, :].astype(F32)
        if capacity >= LANES:
            kind = jnp.concatenate([block[0:1], block[8:9]], axis=1)
        else:
            kind = block[0:1, 0:capacity]
        kinds_hot = hot(iota((KIND_ROWS, capacity), 0) == kind.astype(I32) - 1)
        total = total + mm(kinds_hot, out[r, 0:capacity, :])
        rows = slice(r * share, (r + 1) * share)
        out[r, capacity:, :] = (grad_own[rows, :] + grad_other[rows, :].astype(F32)).astype(BF16)
    extra[0:KIND_ROWS, :] = total.astype(BF16)
    rows = slice(regions * share, regions * share + 16)
    extra[KIND_ROWS:, :] = (grad_own[rows, :] + grad_other[rows, :].astype(F32)).astype(BF16)


def share_kernel(regions, capacity, got, extra, out):
    total = got[0, capacity:, :].astype(F32)
    for r in range(1, regions):
        total = total + got[r, capacity:, :].astype(F32)
    share = total.shape[0]
    total = total.astype(BF16)
    for r in range(regions):
        out[r, 0:share, :] = total
        out[r, share:, :] = extra[...]


def spread_kernel(regions, factor, got, out_q, out_k, out_v, out_o, out_gain, out_embed, flat):
    width, half = out_q.shape
    share = 4 * width // regions
    extra = jnp.zeros((KIND_ROWS + 16, half), F32)
    for r in range(regions):
        chunk = got[r].astype(F32) * factor
        flat[r * share : (r + 1) * share, :] = chunk[0:share]
        extra = extra + chunk[share : share + KIND_ROWS + 16]
    out_q[...] = flat[0:width]
    out_k[...] = flat[width : 2 * width]
    out_v[...] = flat[2 * width : 3 * width]
    out_o[:, 0:half] = flat[3 * width : 3 * width + half]
    out_o[:, half:] = flat[3 * width + half : 4 * width]
    out_embed[...] = extra[0:KINDS]
    out_gain[:, 0:half] = extra[KIND_ROWS : KIND_ROWS + 1]
    out_gain[:, half:] = extra[KIND_ROWS + 1 : KIND_ROWS + 2]


def pick_kernel(target_ref, got, out):
    capacity = BINS_DEV * SLOTS // got.shape[0]
    total = got.shape[0] * capacity
    count = out.shape[0]
    column = jnp.transpose(jnp.broadcast_to(target_ref[...].astype(F32), (8, count)))[:, 0:1].astype(I32)
    flat = got[:, 0:capacity, :].reshape(total, got.shape[2])
    step = 256
    for s in range(0, count, step):
        chosen = hot(iota((step, total), 1) == column[s : s + step])
        out[s : s + step, :] = mm(chosen, flat).astype(BF16)


def ordered(flag, own, other):
    first = jnp.where(flag, other, own)
    second = jnp.where(flag, own, other)
    return first, second


def full_weights(core, own, other):
    flag = core[0] > 0
    half = own.shape[2]
    columns = []
    for k in range(3):
        columns.append(jnp.concatenate(ordered(flag, own[k], other[k]), axis=1))
    top, bottom = ordered(flag, own[3], other[3])
    rows = [jnp.concatenate([part[0:half], part[half:]], axis=1) for part in (top, bottom)]
    return columns + [jnp.concatenate(rows, axis=0)]


def norm_rows(slab, gain, width):
    wide = slab.astype(F32)
    inverse = lax.rsqrt(jnp.sum(wide * wide, axis=1, keepdims=True) / width + EPSILON)
    return wide, inverse, (wide * inverse * gain).astype(BF16)


def spare_lanes(h, heads):
    last = heads * HEAD_DIM - 1
    is_last = h == heads - 1
    return jnp.where(is_last, 0, last), jnp.where(is_last, 1, last - 1)


def forward_kernel(
    heads, core, mine, other, w_own, w_other, gain, info, queries_out, keys_out, values_out, exps_out, context_out, inv_out,
    keep_out, send_out, queries, keys_t, values, w_out, context
):
    h = pl.program_id(0)
    width = heads * HEAD_DIM
    half = width // 2
    flag = core[0] > 0
    lane = iota((1, width), 1)
    scale = HEAD_DIM**-0.5

    @pl.when(h == 0)
    def _():
        w_q, w_k, w_v, w_o = full_weights(core, w_own, w_other)
        w_out[...] = w_o
        slab = jnp.concatenate(ordered(flag, mine[...], other[...]), axis=1)
        _, _, normed = norm_rows(slab, gain[...], width)
        q = mm(normed, w_q).astype(BF16)
        queries[...] = q
        queries_out[...] = q
        k = mm(normed, w_k)
        k_low = k.astype(BF16)
        keys_out[...] = k_low
        k_t = jnp.transpose(k_low.astype(F32))
        bias = jnp.where(info[0:1, :] > 0.5, 0.0, MASKED / scale)
        row = iota(k_t.shape, 0)
        keys_t[0] = jnp.where(row == width - 1, bias, k_t).astype(BF16)
        keys_t[1] = jnp.where(row == 0, bias, k_t).astype(BF16)
        v = mm(normed, w_v).astype(BF16)
        values_out[...] = v
        v_wide = v.astype(F32)
        values[0] = jnp.where(lane == width - 1, 1.0, v_wide).astype(BF16)
        values[1] = jnp.where(lane == 0, 1.0, v_wide).astype(BF16)
        inv_out[...] = jnp.zeros_like(inv_out)

    spare, _ = spare_lanes(h, heads)
    side = jnp.where(h == heads - 1, 1, 0)
    own_lane = lax.shift_right_logical(lane, log2_of(HEAD_DIM)) == h
    step = 256
    for s in range(0, SLOTS, step):
        rows = slice(s, s + step)
        q = jnp.where(own_lane, queries[rows, :].astype(F32), jnp.where(lane == spare, 1.0, 0.0)).astype(BF16)
        scores = mm(q, keys_t[side])
        top = jnp.max(scores, axis=1, keepdims=True)
        exps = jnp.exp2((scores - top) * (scale * LOG2E)).astype(BF16)
        exps_out[0, rows, :] = exps
        summed = mm(exps, values[side])
        inv = 1.0 / jnp.sum(jnp.where(lane == spare, summed, 0.0), axis=1, keepdims=True)
        context[rows, :] = jnp.where(own_lane, summed * inv, context[rows, :])
        lane_small = iota((1, LANES), 1)
        inv_out[rows, :] = jnp.where(lane_small == h, inv, inv_out[rows, :])

    @pl.when(h == heads - 1)
    def _():
        context_out[...] = context[...]
        rows_out = mm(context[...].astype(BF16), w_out[...]).astype(BF16)
        keep_out[...] = jnp.where(flag, rows_out[:, half:], rows_out[:, :half])
        send_out[...] = jnp.where(flag, rows_out[:, :half], rows_out[:, half:])


def backward_kernel(
    heads, core, mine, other, g_mine, g_other, w_own, w_other, gain, info, queries_in, keys_in, values_in, exps_in, context_in,
    inv_in, keep_out, send_out, grad_keep, grad_send, values_t, queries_t, d_context, d_context_t, inv_t, d_query, d_key_t, d_value_t
):
    h = pl.program_id(0)
    width = heads * HEAD_DIM
    half = width // 2
    flag = core[0] > 0
    lane = iota((1, width), 1)
    lane_small = iota((1, LANES), 1)
    scale = HEAD_DIM**-0.5

    def grad_rows():
        return jnp.concatenate(ordered(flag, g_mine[...], g_other[...]), axis=1)

    @pl.when(h == 0)
    def _():
        w_o = full_weights(core, w_own, w_other)[3]
        dc = mm_nt(grad_rows(), w_o).astype(BF16)
        d_context[...] = dc
        d_context_t[...] = jnp.transpose(dc.astype(F32)).astype(BF16)
        inv_t[...] = jnp.transpose(inv_in[...])
        v_t = jnp.transpose(values_in[...].astype(F32))
        row = iota(v_t.shape, 0)
        values_t[0] = jnp.where(row >= width - 2, 1.0, v_t).astype(BF16)
        values_t[1] = jnp.where(row <= 1, 1.0, v_t).astype(BF16)
        queries_t[...] = jnp.transpose(queries_in[...].astype(F32)).astype(BF16)

    spare, spare_low = spare_lanes(h, heads)
    side = jnp.where(h == heads - 1, 1, 0)
    own_lane = lax.shift_right_logical(lane, log2_of(HEAD_DIM)) == h
    base = pl.multiple_of(h * HEAD_DIM, HEAD_DIM)
    head_rows = pl.ds(base, HEAD_DIM)
    inv_row = inv_t[pl.ds(h, 1), :]
    step = 256
    dk = jnp.zeros((HEAD_DIM, SLOTS), F32)
    dv = jnp.zeros((HEAD_DIM, SLOTS), F32)
    for s in range(0, SLOTS, step):
        rows = slice(s, s + step)
        inv = jnp.sum(jnp.where(lane_small == h, inv_in[rows, :], 0.0), axis=1, keepdims=True)
        scaled = jnp.where(own_lane, d_context[rows, :].astype(F32) * inv, 0.0).astype(BF16)
        wide = scaled.astype(F32)
        dot = -jnp.sum(wide * context_in[rows, :], axis=1, keepdims=True)
        dot_high = dot.astype(BF16).astype(F32)
        dot_low = dot - dot_high
        left = jnp.where(lane == spare, dot_high, jnp.where(lane == spare_low, dot_low, wide)).astype(BF16)
        centred = mm(left, values_t[side])
        exps = exps_in[0, rows, :]
        d_scores = (exps.astype(F32) * centred).astype(BF16)
        dq = mm(d_scores, keys_in[...])
        d_query[rows, :] = jnp.where(own_lane, dq * scale, d_query[rows, :])
        dk = dk + mm(queries_t[head_rows, rows], d_scores)
        scaled_t = (d_context_t[head_rows, rows].astype(F32) * inv_row[:, rows]).astype(BF16)
        dv = dv + mm(scaled_t, exps)
    d_key_t[head_rows, :] = dk * scale
    d_value_t[head_rows, :] = dv

    @pl.when(h == heads - 1)
    def _():
        w_q, w_k, w_v, _ = full_weights(core, w_own, w_other)
        slab = jnp.concatenate(ordered(flag, mine[...], other[...]), axis=1)
        wide, inverse, normed = norm_rows(slab, gain[...], width)
        dq = d_query[...].astype(BF16)
        dk = jnp.transpose(d_key_t[...]).astype(BF16)
        dv = jnp.transpose(d_value_t[...]).astype(BF16)
        d_normed = mm_nt(dq, w_q) + mm_nt(dk, w_k) + mm_nt(dv, w_v)
        scaled = gain[...] * d_normed
        along = jnp.sum(scaled * wide, axis=1, keepdims=True)
        d_slab = (inverse * scaled - wide * (inverse * inverse * inverse) * along / width).astype(BF16)
        keep_out[...] = jnp.where(flag, d_slab[:, half:], d_slab[:, :half])
        send_out[...] = jnp.where(flag, d_slab[:, :half], d_slab[:, half:])
        normed_t = jnp.transpose(normed.astype(F32)).astype(BF16)
        context_t = jnp.transpose(context_in[...]).astype(BF16)
        place = 0
        for d_rows in (dq, dk, dv):
            grad = mm(normed_t, d_rows)
            grad_keep[place : place + width, :] = jnp.where(flag, grad[:, half:], grad[:, :half])
            grad_send[place : place + width, :] = jnp.where(flag, grad[:, :half], grad[:, half:]).astype(BF16)
            place += width
        grad = mm(context_t, grad_rows())
        for part in range(2):
            block = grad[:, part * half : (part + 1) * half]
            grad_keep[place : place + half, :] = jnp.where(flag, block[half:], block[:half])
            grad_send[place : place + half, :] = jnp.where(flag, block[:half], block[half:]).astype(BF16)
            place += half
        gain_grad = jnp.sum(d_normed * wide * inverse, axis=0, keepdims=True)
        pick = iota((16, half), 0)
        block = jnp.where(pick == 0, gain_grad[:, :half], jnp.where(pick == 1, gain_grad[:, half:], 0.0))
        grad_keep[place : place + 16, :] = block
        grad_send[place : place + 16, :] = block.astype(BF16)


def shape(dims, dtype):
    return jax.ShapeDtypeStruct(tuple(dims), dtype)


SMEM_SPEC = pl.BlockSpec(memory_space=pltpu.SMEM)


def whole(array):
    zeros = (0,) * len(array.shape)
    return pl.BlockSpec(tuple(array.shape), lambda *_: zeros)


def simple_call(kernel, outs, inputs, scratch=(), scalars=0, scalar_outs=0):
    specs = [SMEM_SPEC] * scalars + [whole(x) for x in inputs[scalars:]]
    return pl.pallas_call(
        kernel,
        out_shape=outs,
        in_specs=specs,
        out_specs=tuple(whole(x) for x in outs[: len(outs) - scalar_outs]) + (SMEM_SPEC,) * scalar_outs,
        scratch_shapes=scratch,
    )(*inputs)


def on_device(
    features,
    element_kinds,
    bin_cells,
    kind_embed,
    norm_gain,
    w_query,
    w_key,
    w_value,
    w_out,
    cotangent,
):
    regions = lax.axis_size("region")
    cores = lax.axis_size("head")
    local_rows = BINS_DEV * SLOTS
    capacity = local_rows // regions
    count, half = features.shape
    width = w_query.shape[0]
    heads = width // HEAD_DIM
    assert cores == BINS_DEV and half * cores == width and half == LANES
    core = lax.axis_index("head").astype(I32).reshape(1)
    swap = [(i, (i + 1) % cores) for i in range(cores)]

    def other_core(x):
        return lax.ppermute(x, "head", swap)

    def exchange(x):
        return lax.all_to_all(x, "region", split_axis=0, concat_axis=0, tiled=True)

    gain = norm_gain.reshape(1, width)
    kinds_row = element_kinds.reshape(1, count)
    packed_shape = shape((regions, capacity, half), BF16)
    tagged_shape = shape((regions, capacity + TAG_ROWS, half), BF16)
    packed_base, target, w_own = simple_call(
        functools.partial(pack_kernel, regions, capacity),
        (tagged_shape, shape((1, count), I32), shape((4, width, half), BF16)),
        (bin_cells.reshape(1, count), kinds_row, features, kind_embed, w_query, w_key, w_value, w_out),
    )
    w_other = other_core(w_own)
    got_base = exchange(packed_base)
    (packed_cot,) = simple_call(
        functools.partial(pack_cot_kernel, regions, capacity), (tagged_shape,), (target, kinds_row, cotangent)
    )
    got_base, packed_cot = lax.optimization_barrier((got_base, packed_cot))
    got_cot = exchange(packed_cot)
    rows_shape = shape((SLOTS, half), BF16)
    lift = pltpu.VMEM((SLOTS + capacity, half), F32)
    mine, theirs, info, marks = simple_call(
        functools.partial(group_kernel, regions, capacity),
        (rows_shape, rows_shape, shape((8, SLOTS), F32), shape((2, regions + 1), I32)),
        (core, got_base),
        scratch=(lift, lift),
        scalars=1,
        scalar_outs=1,
    )
    other = other_core(theirs)

    full_shape = shape((SLOTS, width), BF16)
    exps_shape = shape((heads, SLOTS, SLOTS), BF16)
    exps_spec = pl.BlockSpec((1, SLOTS, SLOTS), lambda h: (h, 0, 0))
    inputs = (core, mine, other, w_own, w_other, gain, info)
    outs = (
        full_shape,
        full_shape,
        full_shape,
        exps_shape,
        shape((SLOTS, width), F32),
        shape((SLOTS, LANES), F32),
        rows_shape,
        rows_shape,
    )
    work = heads * SLOTS * SLOTS
    queries, keys, values, exps, context, inv, attn_keep, attn_send = pl.pallas_call(
        functools.partial(forward_kernel, heads),
        grid=(heads,),
        out_shape=outs,
        in_specs=[SMEM_SPEC] + [whole(x) for x in inputs[1:]],
        out_specs=tuple(exps_spec if x is exps_shape else whole(x) for x in outs),
        scratch_shapes=(
            pltpu.VMEM((SLOTS, width), BF16),
            pltpu.VMEM((2, width, SLOTS), BF16),
            pltpu.VMEM((2, SLOTS, width), BF16),
            pltpu.VMEM((width, width), BF16),
            pltpu.VMEM((SLOTS, width), F32),
        ),
        cost_estimate=pl.CostEstimate(flops=4 * work * width, transcendentals=work, bytes_accessed=2 * work),
        name="forward",
    )(*inputs)
    attn_other = other_core(attn_send)
    (packed_attn,) = simple_call(
        functools.partial(ungroup_kernel, regions, capacity),
        (packed_shape,),
        (core, marks, attn_keep, attn_other),
        scratch=(lift, lift),
        scalars=2,
    )

    g_mine, g_theirs = simple_call(
        functools.partial(regroup_kernel, regions, capacity),
        (rows_shape, rows_shape),
        (core, marks, got_cot),
        scratch=(lift, lift),
        scalars=2,
    )
    g_other = other_core(g_theirs)

    grad_rows = 4 * width + 16
    inputs = (core, mine, other, g_mine, g_other, w_own, w_other, gain, info, queries, keys, values, exps, context, inv)
    outs = (rows_shape, rows_shape, shape((grad_rows, half), F32), shape((grad_rows, half), BF16))
    d_keep, d_send, grad_keep, grad_send = pl.pallas_call(
        functools.partial(backward_kernel, heads),
        grid=(heads,),
        out_shape=outs,
        in_specs=[SMEM_SPEC] + [exps_spec if x is exps else whole(x) for x in inputs[1:]],
        out_specs=tuple(whole(x) for x in outs),
        scratch_shapes=(
            pltpu.VMEM((2, width, SLOTS), BF16),
            pltpu.VMEM((width, SLOTS), BF16),
            pltpu.VMEM((SLOTS, width), BF16),
            pltpu.VMEM((width, SLOTS), BF16),
            pltpu.VMEM((LANES, SLOTS), F32),
            pltpu.VMEM((SLOTS, width), F32),
            pltpu.VMEM((width, SLOTS), F32),
            pltpu.VMEM((width, SLOTS), F32),
        ),
        cost_estimate=pl.CostEstimate(flops=8 * work * width, transcendentals=0, bytes_accessed=2 * work),
        name="backward",
    )(*inputs)

    def pick(home):
        (rows,) = simple_call(pick_kernel, (shape((count, half), BF16),), (target, home))
        return rows

    share = 4 * width // regions
    packed_grad, extra = simple_call(
        functools.partial(ungroup_grad_kernel, regions, capacity),
        (shape((regions, capacity + share, half), BF16), shape((KIND_ROWS + 16, half), BF16)),
        (core, marks, d_keep, other_core(d_send), got_cot, grad_keep, other_core(grad_send)),
        scratch=(lift, lift),
        scalars=2,
    )
    got_cot, packed_attn = lax.optimization_barrier((got_cot, packed_attn))
    home_attn = exchange(packed_attn)
    home_attn, packed_grad = lax.optimization_barrier((home_attn, packed_grad))
    home_grad = exchange(packed_grad)
    (shares,) = simple_call(
        functools.partial(share_kernel, regions, capacity),
        (shape((regions, share + KIND_ROWS + 16, half), BF16),),
        (home_grad, extra),
    )
    summed = exchange(shares)
    column_shape = shape((width, half), F32)
    grad_q, grad_k, grad_v, grad_o, grad_gain, grad_embed = simple_call(
        functools.partial(spread_kernel, regions, float(count * regions) ** (-0.5)),
        (column_shape, column_shape, column_shape, shape((half, width), F32), shape((1, width), F32), shape((KINDS, half), F32)),
        (summed,),
        scratch=(pltpu.VMEM((4 * width, half), F32),),
    )
    attended = pick(home_attn)
    grad_feats = pick(home_grad)
    return (attended, grad_feats, grad_q, grad_k, grad_v, grad_o, grad_gain.reshape(width), grad_embed)


def solution(mesh):
    placed = (
        P(("groups", "region"), "head"),
        P(("groups", "region")),
        P(("groups", "region")),
        P(None, "head"),
        P(),
        P(None, "head"),
        P(None, "head"),
        P(None, "head"),
        P("head", None),
        P(("groups", "region"), "head"),
    )

    return jax.shard_map(
        on_device,
        mesh=mesh,
        in_specs=placed,
        out_specs=(
            P(("groups", "region"), "head"),
            P(("groups", "region"), "head"),
            P("groups", "head"),
            P("groups", "head"),
            P("groups", "head"),
            P(("groups", "head"), None),
            P("groups"),
            P("groups", "head"),
        ),
        check_vma=False,
    )
```

```python
import functools

import jax
import jax.numpy as jnp
from jax import lax
from jax.experimental import pallas as pl
from jax.experimental.pallas import tpu as pltpu
from jax.sharding import PartitionSpec as P


HEAD_DIM = 32
KINDS = 12
SLOTS = 1024
BINS_DEV = 2
MASKED = -1000000000.0
EPSILON = 1e-06
LOG2E = 1.4426950408889634

F32 = jnp.float32
BF16 = jnp.bfloat16
I32 = jnp.int32
LANES = 128
TAG_ROWS = 16
KIND_ROWS = 16
HEAD_PAD = 48
PER_STEP = 2
NT = (((1,), (1,)), ((), ()))
TN = (((0,), (0,)), ((), ()))


def iota(shape, axis):
    return lax.broadcasted_iota(I32, shape, axis)


def mm(a, b):
    return jnp.dot(a, b, preferred_element_type=F32)


def mm_nt(a, b):
    return lax.dot_general(a, b, NT, preferred_element_type=F32)


def mm_tn(a, b):
    return lax.dot_general(a, b, TN, preferred_element_type=F32)


def hot(condition):
    return jnp.where(condition, 1.0, 0.0).astype(BF16)


def log2_of(n):
    return n.bit_length() - 1


def positions(regions, capacity, cell):
    count = cell.shape[1]
    local_rows = BINS_DEV * SLOTS
    owner = lax.shift_right_logical(cell, log2_of(local_rows))
    group = lax.shift_right_logical(cell, log2_of(SLOTS))
    classes = max(BINS_DEV * regions, 16)
    group_hot = jnp.where(iota((classes, count), 0) == group, 1.0, 0.0)
    before = hot(iota((count, count), 0) < iota((count, count), 1))
    rank = jnp.sum(mm(group_hot.astype(BF16), before) * group_hot, axis=0, keepdims=True).astype(I32)
    second = jnp.bitwise_and(group, 1) > 0
    target = owner * capacity + jnp.where(second, capacity - 1 - rank, rank)
    return target, jnp.sum(group_hot, axis=1, keepdims=True)


def pack_kernel(regions, capacity, cells, kinds, feats, embed, w_q, w_k, w_v, w_o, out_base, out_target, out_w):
    count, half = feats.shape
    target, counts = positions(regions, capacity, cells[...])
    out_target[...] = target
    kinds_hot = hot(iota((KINDS, count), 0) == kinds[...])
    base = (feats[...].astype(F32) + mm_tn(kinds_hot, embed[...])).astype(BF16)
    place = iota((TAG_ROWS, half), 0)
    for r in range(regions):
        chosen = hot(iota((capacity, count), 0) + r * capacity == target)
        out_base[r, 0:capacity, :] = mm(chosen, base).astype(BF16)
        first = counts[2 * r : 2 * r + 1]
        second = counts[2 * r + 1 : 2 * r + 2]
        tags = jnp.where(place == 0, first, jnp.where(place == 1, second, 0.0))
        out_base[r, capacity : capacity + TAG_ROWS, :] = tags.astype(BF16)
    out_w[0] = w_q[...]
    out_w[1] = w_k[...]
    out_w[2] = w_v[...]
    out_w[3, 0:half, :] = w_o[:, 0:half]
    out_w[3, half:, :] = w_o[:, half:]


def pack_cot_kernel(regions, capacity, target_ref, kinds, cot, out_cot):
    count = cot.shape[0]
    target = target_ref[...]
    rows = cot[...]
    tags = jnp.where(iota((TAG_ROWS, count), 0) == 0, kinds[...] + 1, 0).astype(F32).astype(BF16)
    for r in range(regions):
        chosen = hot(iota((capacity, count), 0) + r * capacity == target)
        out_cot[r, 0:capacity, :] = mm(chosen, rows).astype(BF16)
        tag = mm_nt(tags, chosen)
        if capacity >= LANES:
            tag = jnp.concatenate([tag[0:8, 0:LANES], tag[0:8, LANES : 2 * LANES]], axis=0)
        else:
            tag = jnp.concatenate([tag, jnp.zeros((TAG_ROWS, LANES - capacity), F32)], axis=1)
        out_cot[r, capacity : capacity + TAG_ROWS, :] = tag.astype(BF16)


def place_rows(regions, capacity, got, marks, front, back):
    for r in range(regions):
        rows = got[r, 0:capacity, :].astype(F32)
        front[pl.ds(marks[0, r], capacity), :] = rows
        back[pl.ds(marks[1, r], capacity), :] = rows


def bins_of(regions, capacity, core, marks, front, back):
    row = iota((SLOTS, 1), 0)
    first = jnp.where(row < marks[0, regions], front[0:SLOTS, :], 0.0)
    second = jnp.where(row >= marks[1, regions], back[capacity : capacity + SLOTS, :], 0.0)
    flag = core[0] > 0
    return jnp.where(flag, second, first).astype(BF16), jnp.where(flag, first, second).astype(BF16)


def group_kernel(regions, capacity, core, got, mine, theirs, keep, marks, front, back):
    start = jnp.int32(0)
    end = jnp.int32(SLOTS)
    for r in range(regions):
        block = got[r, capacity : capacity + TAG_ROWS, :].astype(F32)
        marks[0, r] = start
        marks[1, r] = end
        start = start + jnp.max(block[0:1, :]).astype(I32)
        end = end - jnp.max(block[1:2, :]).astype(I32)
    marks[0, regions] = start
    marks[1, regions] = end
    place_rows(regions, capacity, got, marks, front, back)
    mine[...], theirs[...] = bins_of(regions, capacity, core, marks, front, back)
    lane = iota((8, SLOTS), 1)
    filled = jnp.where(core[0] > 0, jnp.where(lane >= end, 1.0, 0.0), jnp.where(lane < start, 1.0, 0.0))
    keep[...] = filled


def regroup_kernel(regions, capacity, core, marks, got, mine, theirs, front, back):
    place_rows(regions, capacity, got, marks, front, back)
    mine[...], theirs[...] = bins_of(regions, capacity, core, marks, front, back)


def arrival_rows(regions, capacity, core, marks, own, other, out, front, back):
    flag = core[0] > 0
    x = own[...].astype(F32)
    y = other[...].astype(F32)
    front[0:SLOTS, :] = jnp.where(flag, y, x)
    front[SLOTS:, :] = jnp.zeros((capacity, x.shape[1]), F32)
    back[0:capacity, :] = jnp.zeros((capacity, x.shape[1]), F32)
    back[capacity:, :] = jnp.where(flag, x, y)
    row = iota((capacity, 1), 0)
    for r in range(regions):
        held = marks[0, r + 1] - marks[0, r]
        rows = jnp.where(row < held, front[pl.ds(marks[0, r], capacity), :], back[pl.ds(marks[1, r], capacity), :])
        out[r, 0:capacity, :] = rows.astype(BF16)


def ungroup_kernel(regions, capacity, core, marks, own, other, out, front, back):
    arrival_rows(regions, capacity, core, marks, own, other, out, front, back)


def ungroup_grad_kernel(regions, capacity, core, marks, own, other, tagged, grad_own, grad_other, out, extra, front, back):
    arrival_rows(regions, capacity, core, marks, own, other, out, front, back)
    total = jnp.zeros((KIND_ROWS, own.shape[1]), F32)
    share = out.shape[1] - capacity
    for r in range(regions):
        block = tagged[r, capacity : capacity + TAG_ROWS, :].astype(F32)
        if capacity >= LANES:
            kind = jnp.concatenate([block[0:1], block[8:9]], axis=1)
        else:
            kind = block[0:1, 0:capacity]
        kinds_hot = hot(iota((KIND_ROWS, capacity), 0) == kind.astype(I32) - 1)
        total = total + mm(kinds_hot, out[r, 0:capacity, :])
        rows = slice(r * share, (r + 1) * share)
        out[r, capacity:, :] = (grad_own[rows, :] + grad_other[rows, :].astype(F32)).astype(BF16)
    extra[0:KIND_ROWS, :] = total.astype(BF16)
    rows = slice(regions * share, regions * share + 16)
    extra[KIND_ROWS:, :] = (grad_own[rows, :] + grad_other[rows, :].astype(F32)).astype(BF16)


def share_kernel(regions, capacity, got, extra, out):
    total = got[0, capacity:, :].astype(F32)
    for r in range(1, regions):
        total = total + got[r, capacity:, :].astype(F32)
    share = total.shape[0]
    total = total.astype(BF16)
    for r in range(regions):
        out[r, 0:share, :] = total
        out[r, share:, :] = extra[...]


def spread_kernel(regions, factor, got, out_q, out_k, out_v, out_o, out_gain, out_embed, flat):
    width, half = out_q.shape
    share = 4 * width // regions
    extra = jnp.zeros((KIND_ROWS + 16, half), F32)
    for r in range(regions):
        chunk = got[r].astype(F32) * factor
        flat[r * share : (r + 1) * share, :] = chunk[0:share]
        extra = extra + chunk[share : share + KIND_ROWS + 16]
    out_q[...] = flat[0:width]
    out_k[...] = flat[width : 2 * width]
    out_v[...] = flat[2 * width : 3 * width]
    out_o[:, 0:half] = flat[3 * width : 3 * width + half]
    out_o[:, half:] = flat[3 * width + half : 4 * width]
    out_embed[...] = extra[0:KINDS]
    out_gain[:, 0:half] = extra[KIND_ROWS : KIND_ROWS + 1]
    out_gain[:, half:] = extra[KIND_ROWS + 1 : KIND_ROWS + 2]


def pick_kernel(target_ref, got, out):
    capacity = BINS_DEV * SLOTS // got.shape[0]
    total = got.shape[0] * capacity
    count = out.shape[0]
    column = jnp.transpose(jnp.broadcast_to(target_ref[...].astype(F32), (8, count)))[:, 0:1].astype(I32)
    flat = got[:, 0:capacity, :].reshape(total, got.shape[2])
    step = 256
    for s in range(0, count, step):
        chosen = hot(iota((step, total), 1) == column[s : s + step])
        out[s : s + step, :] = mm(chosen, flat).astype(BF16)


def ordered(flag, own, other):
    first = jnp.where(flag, other, own)
    second = jnp.where(flag, own, other)
    return first, second


def full_weights(core, own, other):
    flag = core[0] > 0
    half = own.shape[2]
    columns = []
    for k in range(3):
        columns.append(jnp.concatenate(ordered(flag, own[k], other[k]), axis=1))
    top, bottom = ordered(flag, own[3], other[3])
    rows = [jnp.concatenate([part[0:half], part[half:]], axis=1) for part in (top, bottom)]
    return columns + [jnp.concatenate(rows, axis=0)]


def norm_rows(slab, gain, width):
    wide = slab.astype(F32)
    inverse = lax.rsqrt(jnp.sum(wide * wide, axis=1, keepdims=True) / width + EPSILON)
    return wide, inverse, (wide * inverse * gain).astype(BF16)


def stack_rows(rows, extra):
    place = iota((HEAD_PAD - HEAD_DIM, rows.shape[1]), 0)
    tail = jnp.zeros(place.shape, F32)
    for k, value in enumerate(extra):
        tail = jnp.where(place == k, value, tail)
    return jnp.concatenate([rows.astype(F32), tail], axis=0)


def forward_kernel(
    heads, core, mine, other, w_own, w_other, gain, keep, queries_t, keys_out, values_t, exps_out, context_t, inv_t,
    keep_out, send_out, keys_t, w_out
):
    step = pl.program_id(0)
    width = heads * HEAD_DIM
    half = width // 2
    flag = core[0] > 0
    scale = HEAD_DIM**-0.5

    @pl.when(step == 0)
    def _():
        w_q, w_k, w_v, w_o = full_weights(core, w_own, w_other)
        w_out[...] = w_o
        slab = jnp.concatenate(ordered(flag, mine[...], other[...]), axis=1)
        _, _, normed = norm_rows(slab, gain[...], width)
        queries_t[...] = jnp.transpose(mm(normed, w_q)).astype(BF16)
        k = mm(normed, w_k)
        keys_out[...] = k.astype(BF16)
        keys_t[...] = jnp.transpose(k).astype(BF16)
        values_t[...] = jnp.transpose(mm(normed, w_v)).astype(BF16)

    bias = jnp.where(keep[0:1, :] > 0.5, 0.0, MASKED / scale)
    for k in range(PER_STEP):
        h = step * PER_STEP + k
        head_rows = pl.ds(pl.multiple_of(h * HEAD_DIM, HEAD_DIM), HEAD_DIM)
        left = jnp.transpose(stack_rows(queries_t[head_rows, :], (1.0,))).astype(BF16)
        scores = mm(left, stack_rows(keys_t[head_rows, :], (bias,)).astype(BF16))
        top = jnp.max(scores, axis=1, keepdims=True)
        exps = jnp.exp2((scores - top) * (scale * LOG2E)).astype(BF16)
        exps_out[k] = exps
        summed = mm_nt(stack_rows(values_t[head_rows, :], (1.0,)).astype(BF16), exps)
        inv = 1.0 / summed[HEAD_DIM : HEAD_DIM + 1]
        context_t[head_rows, :] = summed[0:HEAD_DIM] * inv
        inv_t[pl.ds(h, 1), :] = inv

    @pl.when(step == heads // PER_STEP - 1)
    def _():
        rows_out = mm(jnp.transpose(context_t[...]).astype(BF16), w_out[...]).astype(BF16)
        keep_out[...] = jnp.where(flag, rows_out[:, half:], rows_out[:, :half])
        send_out[...] = jnp.where(flag, rows_out[:, :half], rows_out[:, half:])


def backward_kernel(
    heads, core, mine, other, g_mine, g_other, w_own, w_other, gain, queries_t, keys_in, values_t, exps_in, context_t,
    inv_t, keep_out, send_out, grad_keep, grad_send, d_context_t, d_query, d_key_t, d_value_t
):
    step = pl.program_id(0)
    width = heads * HEAD_DIM
    half = width // 2
    flag = core[0] > 0
    lane = iota((1, width), 1)
    scale = HEAD_DIM**-0.5

    def grad_rows():
        return jnp.concatenate(ordered(flag, g_mine[...], g_other[...]), axis=1)

    @pl.when(step == 0)
    def _():
        w_o = full_weights(core, w_own, w_other)[3]
        d_context_t[...] = mm_nt(w_o, grad_rows()).astype(BF16)

    for k in range(PER_STEP):
        h = step * PER_STEP + k
        head_rows = pl.ds(pl.multiple_of(h * HEAD_DIM, HEAD_DIM), HEAD_DIM)
        own_lane = lax.shift_right_logical(lane, log2_of(HEAD_DIM)) == h
        scaled = (d_context_t[head_rows, :].astype(F32) * inv_t[pl.ds(h, 1), :]).astype(BF16)
        dot = -jnp.sum(scaled.astype(F32) * context_t[head_rows, :], axis=0, keepdims=True)
        dot_high = dot.astype(BF16).astype(F32)
        left = jnp.transpose(stack_rows(scaled, (dot_high, dot - dot_high))).astype(BF16)
        centred = mm(left, stack_rows(values_t[head_rows, :], (1.0, 1.0)).astype(BF16))
        exps = exps_in[k]
        d_scores = (exps.astype(F32) * centred).astype(BF16)
        dq = mm(d_scores, keys_in[...])
        d_query[...] = jnp.where(own_lane, dq * scale, d_query[...])
        d_key_t[head_rows, :] = mm(queries_t[head_rows, :], d_scores) * scale
        d_value_t[head_rows, :] = mm(scaled, exps)

    @pl.when(step == heads // PER_STEP - 1)
    def _():
        w_q, w_k, w_v, _ = full_weights(core, w_own, w_other)
        slab = jnp.concatenate(ordered(flag, mine[...], other[...]), axis=1)
        wide, inverse, normed = norm_rows(slab, gain[...], width)
        dq = d_query[...].astype(BF16)
        dk = jnp.transpose(d_key_t[...]).astype(BF16)
        dv = jnp.transpose(d_value_t[...]).astype(BF16)
        d_normed = mm_nt(dq, w_q) + mm_nt(dk, w_k) + mm_nt(dv, w_v)
        scaled = gain[...] * d_normed
        along = jnp.sum(scaled * wide, axis=1, keepdims=True)
        d_slab = (inverse * scaled - wide * (inverse * inverse * inverse) * along / width).astype(BF16)
        keep_out[...] = jnp.where(flag, d_slab[:, half:], d_slab[:, :half])
        send_out[...] = jnp.where(flag, d_slab[:, :half], d_slab[:, half:])
        normed_t = jnp.transpose(normed.astype(F32)).astype(BF16)
        place = 0
        for d_rows in (dq, dk, dv):
            grad = mm(normed_t, d_rows)
            grad_keep[place : place + width, :] = jnp.where(flag, grad[:, half:], grad[:, :half])
            grad_send[place : place + width, :] = jnp.where(flag, grad[:, :half], grad[:, half:]).astype(BF16)
            place += width
        grad = mm(context_t[...].astype(BF16), grad_rows())
        for part in range(2):
            block = grad[:, part * half : (part + 1) * half]
            grad_keep[place : place + half, :] = jnp.where(flag, block[half:], block[:half])
            grad_send[place : place + half, :] = jnp.where(flag, block[:half], block[half:]).astype(BF16)
            place += half
        gain_grad = jnp.sum(d_normed * wide * inverse, axis=0, keepdims=True)
        pick = iota((16, half), 0)
        block = jnp.where(pick == 0, gain_grad[:, :half], jnp.where(pick == 1, gain_grad[:, half:], 0.0))
        grad_keep[place : place + 16, :] = block
        grad_send[place : place + 16, :] = block.astype(BF16)


def shape(dims, dtype):
    return jax.ShapeDtypeStruct(tuple(dims), dtype)


SMEM_SPEC = pl.BlockSpec(memory_space=pltpu.SMEM)


def whole(array):
    zeros = (0,) * len(array.shape)
    return pl.BlockSpec(tuple(array.shape), lambda *_: zeros)


def simple_call(kernel, outs, inputs, scratch=(), scalars=0, scalar_outs=0):
    specs = [SMEM_SPEC] * scalars + [whole(x) for x in inputs[scalars:]]
    return pl.pallas_call(
        kernel,
        out_shape=outs,
        in_specs=specs,
        out_specs=tuple(whole(x) for x in outs[: len(outs) - scalar_outs]) + (SMEM_SPEC,) * scalar_outs,
        scratch_shapes=scratch,
    )(*inputs)


def on_device(
    features,
    element_kinds,
    bin_cells,
    kind_embed,
    norm_gain,
    w_query,
    w_key,
    w_value,
    w_out,
    cotangent,
):
    regions = lax.axis_size("region")
    cores = lax.axis_size("head")
    local_rows = BINS_DEV * SLOTS
    capacity = local_rows // regions
    count, half = features.shape
    width = w_query.shape[0]
    heads = width // HEAD_DIM
    assert cores == BINS_DEV and half * cores == width and half == LANES
    core = lax.axis_index("head").astype(I32).reshape(1)
    swap = [(i, (i + 1) % cores) for i in range(cores)]

    def other_core(x):
        return lax.ppermute(x, "head", swap)

    def exchange(x):
        return lax.all_to_all(x, "region", split_axis=0, concat_axis=0, tiled=True)

    gain = norm_gain.reshape(1, width)
    kinds_row = element_kinds.reshape(1, count)
    packed_shape = shape((regions, capacity, half), BF16)
    tagged_shape = shape((regions, capacity + TAG_ROWS, half), BF16)
    packed_base, target, w_own = simple_call(
        functools.partial(pack_kernel, regions, capacity),
        (tagged_shape, shape((1, count), I32), shape((4, width, half), BF16)),
        (bin_cells.reshape(1, count), kinds_row, features, kind_embed, w_query, w_key, w_value, w_out),
    )
    w_other = other_core(w_own)
    got_base = exchange(packed_base)
    (packed_cot,) = simple_call(
        functools.partial(pack_cot_kernel, regions, capacity), (tagged_shape,), (target, kinds_row, cotangent)
    )
    got_base, packed_cot = lax.optimization_barrier((got_base, packed_cot))
    got_cot = exchange(packed_cot)
    rows_shape = shape((SLOTS, half), BF16)
    lift = pltpu.VMEM((SLOTS + capacity, half), F32)
    mine, theirs, info, marks = simple_call(
        functools.partial(group_kernel, regions, capacity),
        (rows_shape, rows_shape, shape((8, SLOTS), F32), shape((2, regions + 1), I32)),
        (core, got_base),
        scratch=(lift, lift),
        scalars=1,
        scalar_outs=1,
    )
    other = other_core(theirs)

    turned_shape = shape((width, SLOTS), BF16)
    exps_shape = shape((heads, SLOTS, SLOTS), BF16)
    exps_spec = pl.BlockSpec((PER_STEP, SLOTS, SLOTS), lambda h: (h, 0, 0))
    inputs = (core, mine, other, w_own, w_other, gain, info)
    outs = (
        turned_shape,
        shape((SLOTS, width), BF16),
        turned_shape,
        exps_shape,
        shape((width, SLOTS), F32),
        shape((heads, SLOTS), F32),
        rows_shape,
        rows_shape,
    )
    work = heads * SLOTS * SLOTS
    queries_t, keys, values_t, exps, context_t, inv_t, attn_keep, attn_send = pl.pallas_call(
        functools.partial(forward_kernel, heads),
        grid=(heads // PER_STEP,),
        out_shape=outs,
        in_specs=[SMEM_SPEC] + [whole(x) for x in inputs[1:]],
        out_specs=tuple(exps_spec if x is exps_shape else whole(x) for x in outs),
        scratch_shapes=(pltpu.VMEM((width, SLOTS), BF16), pltpu.VMEM((width, width), BF16)),
        cost_estimate=pl.CostEstimate(flops=4 * work * width, transcendentals=work, bytes_accessed=2 * work),
        name="forward",
    )(*inputs)
    attn_other = other_core(attn_send)
    (packed_attn,) = simple_call(
        functools.partial(ungroup_kernel, regions, capacity),
        (packed_shape,),
        (core, marks, attn_keep, attn_other),
        scratch=(lift, lift),
        scalars=2,
    )

    g_mine, g_theirs = simple_call(
        functools.partial(regroup_kernel, regions, capacity),
        (rows_shape, rows_shape),
        (core, marks, got_cot),
        scratch=(lift, lift),
        scalars=2,
    )
    g_other = other_core(g_theirs)

    grad_rows = 4 * width + 16
    inputs = (core, mine, other, g_mine, g_other, w_own, w_other, gain, queries_t, keys, values_t, exps, context_t, inv_t)
    outs = (rows_shape, rows_shape, shape((grad_rows, half), F32), shape((grad_rows, half), BF16))
    d_keep, d_send, grad_keep, grad_send = pl.pallas_call(
        functools.partial(backward_kernel, heads),
        grid=(heads // PER_STEP,),
        out_shape=outs,
        in_specs=[SMEM_SPEC] + [exps_spec if x is exps else whole(x) for x in inputs[1:]],
        out_specs=tuple(whole(x) for x in outs),
        scratch_shapes=(
            pltpu.VMEM((width, SLOTS), BF16),
            pltpu.VMEM((SLOTS, width), F32),
            pltpu.VMEM((width, SLOTS), F32),
            pltpu.VMEM((width, SLOTS), F32),
        ),
        cost_estimate=pl.CostEstimate(flops=8 * work * width, transcendentals=0, bytes_accessed=2 * work),
        name="backward",
    )(*inputs)

    def pick(home):
        (rows,) = simple_call(pick_kernel, (shape((count, half), BF16),), (target, home))
        return rows

    share = 4 * width // regions
    packed_grad, extra = simple_call(
        functools.partial(ungroup_grad_kernel, regions, capacity),
        (shape((regions, capacity + share, half), BF16), shape((KIND_ROWS + 16, half), BF16)),
        (core, marks, d_keep, other_core(d_send), got_cot, grad_keep, other_core(grad_send)),
        scratch=(lift, lift),
        scalars=2,
    )
    got_cot, packed_attn = lax.optimization_barrier((got_cot, packed_attn))
    home_attn = exchange(packed_attn)
    home_attn, packed_grad = lax.optimization_barrier((home_attn, packed_grad))
    home_grad = exchange(packed_grad)
    (shares,) = simple_call(
        functools.partial(share_kernel, regions, capacity),
        (shape((regions, share + KIND_ROWS + 16, half), BF16),),
        (home_grad, extra),
    )
    summed = exchange(shares)
    column_shape = shape((width, half), F32)
    grad_q, grad_k, grad_v, grad_o, grad_gain, grad_embed = simple_call(
        functools.partial(spread_kernel, regions, float(count * regions) ** (-0.5)),
        (column_shape, column_shape, column_shape, shape((half, width), F32), shape((1, width), F32), shape((KINDS, half), F32)),
        (summed,),
        scratch=(pltpu.VMEM((4 * width, half), F32),),
    )
    attended = pick(home_attn)
    grad_feats = pick(home_grad)
    return (attended, grad_feats, grad_q, grad_k, grad_v, grad_o, grad_gain.reshape(width), grad_embed)


def solution(mesh):
    placed = (
        P(("groups", "region"), "head"),
        P(("groups", "region")),
        P(("groups", "region")),
        P(None, "head"),
        P(),
        P(None, "head"),
        P(None, "head"),
        P(None, "head"),
        P("head", None),
        P(("groups", "region"), "head"),
    )

    return jax.shard_map(
        on_device,
        mesh=mesh,
        in_specs=placed,
        out_specs=(
            P(("groups", "region"), "head"),
            P(("groups", "region"), "head"),
            P("groups", "head"),
            P("groups", "head"),
            P("groups", "head"),
            P(("groups", "head"), None),
            P("groups"),
            P("groups", "head"),
        ),
        check_vma=False,
    )
```

```python
import functools

import jax
import jax.numpy as jnp
from jax import lax
from jax.experimental import pallas as pl
from jax.experimental.pallas import tpu as pltpu
from jax.sharding import PartitionSpec as P


HEAD_DIM = 32
KINDS = 12
SLOTS = 1024
BINS_DEV = 2
MASKED = -1000000000.0
EPSILON = 1e-06
LOG2E = 1.4426950408889634

F32 = jnp.float32
BF16 = jnp.bfloat16
I32 = jnp.int32
LANES = 128
TAG_ROWS = 16
KIND_ROWS = 16
HEAD_PAD = 48
PER_STEP = 2
NT = (((1,), (1,)), ((), ()))
TN = (((0,), (0,)), ((), ()))


def iota(shape, axis):
    return lax.broadcasted_iota(I32, shape, axis)


def mm(a, b):
    return jnp.dot(a, b, preferred_element_type=F32)


def mm_nt(a, b):
    return lax.dot_general(a, b, NT, preferred_element_type=F32)


def mm_tn(a, b):
    return lax.dot_general(a, b, TN, preferred_element_type=F32)


def hot(condition):
    return jnp.where(condition, 1.0, 0.0).astype(BF16)


def log2_of(n):
    return n.bit_length() - 1


def positions(regions, capacity, cell):
    count = cell.shape[1]
    local_rows = BINS_DEV * SLOTS
    owner = lax.shift_right_logical(cell, log2_of(local_rows))
    group = lax.shift_right_logical(cell, log2_of(SLOTS))
    classes = max(BINS_DEV * regions, 16)
    group_hot = jnp.where(iota((classes, count), 0) == group, 1.0, 0.0)
    before = hot(iota((count, count), 0) < iota((count, count), 1))
    rank = jnp.sum(mm(group_hot.astype(BF16), before) * group_hot, axis=0, keepdims=True).astype(I32)
    second = jnp.bitwise_and(group, 1) > 0
    target = owner * capacity + jnp.where(second, capacity - 1 - rank, rank)
    return target, jnp.sum(group_hot, axis=1, keepdims=True)


def pack_kernel(regions, capacity, cells, kinds, feats, embed, w_q, w_k, w_v, w_o, out_base, out_target, out_w):
    count, half = feats.shape
    target, counts = positions(regions, capacity, cells[...])
    out_target[...] = target
    kinds_hot = hot(iota((KINDS, count), 0) == kinds[...])
    base = (feats[...].astype(F32) + mm_tn(kinds_hot, embed[...])).astype(BF16)
    place = iota((TAG_ROWS, half), 0)
    for r in range(regions):
        chosen = hot(iota((capacity, count), 0) + r * capacity == target)
        out_base[r, 0:capacity, :] = mm(chosen, base).astype(BF16)
        first = counts[2 * r : 2 * r + 1]
        second = counts[2 * r + 1 : 2 * r + 2]
        tags = jnp.where(place == 0, first, jnp.where(place == 1, second, 0.0))
        out_base[r, capacity : capacity + TAG_ROWS, :] = tags.astype(BF16)
    out_w[0] = w_q[...]
    out_w[1] = w_k[...]
    out_w[2] = w_v[...]
    out_w[3, 0:half, :] = w_o[:, 0:half]
    out_w[3, half:, :] = w_o[:, half:]


def pack_cot_kernel(regions, capacity, target_ref, kinds, cot, out_cot):
    count = cot.shape[0]
    target = target_ref[...]
    rows = cot[...]
    tags = jnp.where(iota((TAG_ROWS, count), 0) == 0, kinds[...] + 1, 0).astype(F32).astype(BF16)
    for r in range(regions):
        chosen = hot(iota((capacity, count), 0) + r * capacity == target)
        out_cot[r, 0:capacity, :] = mm(chosen, rows).astype(BF16)
        tag = mm_nt(tags, chosen)
        if capacity >= LANES:
            tag = jnp.concatenate([tag[0:8, 0:LANES], tag[0:8, LANES : 2 * LANES]], axis=0)
        else:
            tag = jnp.concatenate([tag, jnp.zeros((TAG_ROWS, LANES - capacity), F32)], axis=1)
        out_cot[r, capacity : capacity + TAG_ROWS, :] = tag.astype(BF16)


def count_rows(regions, capacity, got, marks):
    start = jnp.int32(0)
    end = jnp.int32(SLOTS)
    for r in range(regions):
        block = got[r, capacity : capacity + TAG_ROWS, :].astype(F32)
        marks[0, r] = start
        marks[1, r] = end
        start = start + jnp.max(block[0:1, :]).astype(I32)
        end = end - jnp.max(block[1:2, :]).astype(I32)
    marks[0, regions] = start
    marks[1, regions] = end


def is_filled(regions, core, marks, place):
    first = jnp.where(place < marks[0, regions], 1.0, 0.0)
    second = jnp.where(place >= marks[1, regions], 1.0, 0.0)
    return jnp.where(core[0] > 0, second, first)


def bin_rows(regions, capacity, core, marks, own, other, lift, lift_other):
    flag = core[0] > 0
    for r in range(regions):
        place = pl.ds(marks[core[0], r], capacity)
        lift[place, :] = own[r, 0:capacity, :].astype(F32)
        lift_other[place, :] = other[r, 0:capacity, :].astype(F32)
    place = pl.ds(pl.multiple_of(core[0] * capacity, capacity), SLOTS)
    rows = jnp.concatenate(ordered(flag, lift[place, :], lift_other[place, :]), axis=1)
    filled = is_filled(regions, core, marks, iota((SLOTS, 1), 0))
    return jnp.where(filled > 0.5, rows, 0.0).astype(BF16)


def arrival_rows(regions, capacity, core, marks, own, other, out, front, back):
    flag = core[0] > 0
    x = own[...].astype(F32)
    y = other[...].astype(F32)
    front[0:SLOTS, :] = jnp.where(flag, y, x)
    front[SLOTS:, :] = jnp.zeros((capacity, x.shape[1]), F32)
    back[0:capacity, :] = jnp.zeros((capacity, x.shape[1]), F32)
    back[capacity:, :] = jnp.where(flag, x, y)
    row = iota((capacity, 1), 0)
    for r in range(regions):
        held = marks[0, r + 1] - marks[0, r]
        rows = jnp.where(row < held, front[pl.ds(marks[0, r], capacity), :], back[pl.ds(marks[1, r], capacity), :])
        out[r, 0:capacity, :] = rows.astype(BF16)


def ungroup_kernel(regions, capacity, core, marks, own, other, out, front, back):
    arrival_rows(regions, capacity, core, marks, own, other, out, front, back)


def ungroup_grad_kernel(regions, capacity, core, marks, own, other, tagged, gain_part, out, extra, front, back):
    arrival_rows(regions, capacity, core, marks, own, other, out, front, back)
    total = jnp.zeros((KIND_ROWS, own.shape[1]), F32)
    for r in range(regions):
        block = tagged[r, capacity : capacity + TAG_ROWS, :].astype(F32)
        if capacity >= LANES:
            kind = jnp.concatenate([block[0:1], block[8:9]], axis=1)
        else:
            kind = block[0:1, 0:capacity]
        kinds_hot = hot(iota((KIND_ROWS, capacity), 0) == kind.astype(I32) - 1)
        total = total + mm(kinds_hot, out[r, 0:capacity, :])
    place = iota((KIND_ROWS, 1), 0)
    first = gain_part[0:1, :].astype(F32)
    second = gain_part[1:2, :].astype(F32)
    extra[...] = jnp.where(place == KINDS, first, jnp.where(place == KINDS + 1, second, total)).astype(BF16)


def pair_kernel(regions, own, received, out, gain_part):
    share = out.shape[1]
    for r in range(regions):
        rows = slice(r * share, (r + 1) * share)
        out[r] = (own[rows, :] + received[rows, :].astype(F32)).astype(BF16)
    gain_part[...] = (own[regions * share :, :] + received[regions * share :, :].astype(F32)).astype(BF16)


def share_kernel(regions, capacity, got, extra, packed, out, tail, sems):
    total = got[0].astype(F32)
    for r in range(1, regions):
        total = total + got[r].astype(F32)
    share = total.shape[0]
    tail[0:share, :] = total.astype(BF16)
    tail[share:, :] = extra[...]
    copies = [
        pltpu.make_async_copy(tail, out.at[r, pl.ds(capacity, share + KIND_ROWS), :], sems.at[r]) for r in range(regions)
    ]
    for copy in copies:
        copy.start()
    for copy in copies:
        copy.wait()


def last_kernel(regions, capacity, factor, target_ref, got, out, out_q, out_k, out_v, out_o, out_gain, out_embed, flat):
    pick_kernel(target_ref, got, out)
    width, half = out_q.shape
    share = 4 * width // regions
    extra = jnp.zeros((KIND_ROWS, half), F32)
    for r in range(regions):
        flat[r * share : (r + 1) * share, :] = got[r, capacity : capacity + share, :].astype(F32) * factor
        extra = extra + got[r, capacity + share : capacity + share + KIND_ROWS, :].astype(F32)
    extra = extra * factor
    out_q[...] = flat[0:width]
    out_k[...] = flat[width : 2 * width]
    out_v[...] = flat[2 * width : 3 * width]
    out_o[:, 0:half] = flat[3 * width : 3 * width + half]
    out_o[:, half:] = flat[3 * width + half : 4 * width]
    out_embed[...] = extra[0:KINDS]
    out_gain[:, 0:half] = extra[KINDS : KINDS + 1]
    out_gain[:, half:] = extra[KINDS + 1 : KINDS + 2]


def pick_kernel(target_ref, got, out):
    capacity = BINS_DEV * SLOTS // got.shape[0]
    total = got.shape[0] * capacity
    count = out.shape[0]
    column = jnp.transpose(jnp.broadcast_to(target_ref[...].astype(F32), (8, count)))[:, 0:1].astype(I32)
    flat = got[:, 0:capacity, :].reshape(total, got.shape[2])
    step = 256
    for s in range(0, count, step):
        chosen = hot(iota((step, total), 1) == column[s : s + step])
        out[s : s + step, :] = mm(chosen, flat).astype(BF16)


def ordered(flag, own, other):
    first = jnp.where(flag, other, own)
    second = jnp.where(flag, own, other)
    return first, second


def full_weights(core, own, other):
    flag = core[0] > 0
    half = own.shape[2]
    columns = []
    for k in range(3):
        columns.append(jnp.concatenate(ordered(flag, own[k], other[k]), axis=1))
    top, bottom = ordered(flag, own[3], other[3])
    rows = [jnp.concatenate([part[0:half], part[half:]], axis=1) for part in (top, bottom)]
    return columns + [jnp.concatenate(rows, axis=0)]


def norm_rows(slab, gain, width):
    wide = slab.astype(F32)
    inverse = lax.rsqrt(jnp.sum(wide * wide, axis=1, keepdims=True) / width + EPSILON)
    return wide, inverse, (wide * inverse * gain).astype(BF16)


def stack_rows(rows, extra):
    place = iota((HEAD_PAD - HEAD_DIM, rows.shape[1]), 0)
    tail = jnp.zeros(place.shape, F32)
    for k, value in enumerate(extra):
        tail = jnp.where(place == k, value, tail)
    return jnp.concatenate([rows.astype(F32), tail], axis=0)


def forward_kernel(
    heads, regions, capacity, core, got, got_other, w_own, w_other, gain, slab_out, queries_t, keys_out, values_t, exps_out,
    context_t, inv_t, keep_out, send_out, marks, keys_t, w_out, lift, lift_other
):
    step = pl.program_id(0)
    width = heads * HEAD_DIM
    half = width // 2
    flag = core[0] > 0
    scale = HEAD_DIM**-0.5

    @pl.when(step == 0)
    def _():
        w_q, w_k, w_v, w_o = full_weights(core, w_own, w_other)
        w_out[...] = w_o
        count_rows(regions, capacity, got, marks)
        slab = bin_rows(regions, capacity, core, marks, got, got_other, lift, lift_other)
        slab_out[...] = slab
        _, _, normed = norm_rows(slab, gain[...], width)
        queries_t[...] = jnp.transpose(mm(normed, w_q)).astype(BF16)
        k = mm(normed, w_k)
        keys_out[...] = k.astype(BF16)
        keys_t[...] = jnp.transpose(k).astype(BF16)
        values_t[...] = jnp.transpose(mm(normed, w_v)).astype(BF16)

    bias = jnp.where(is_filled(regions, core, marks, iota((1, SLOTS), 1)) > 0.5, 0.0, MASKED / scale)
    for k in range(PER_STEP):
        h = step * PER_STEP + k
        head_rows = pl.ds(pl.multiple_of(h * HEAD_DIM, HEAD_DIM), HEAD_DIM)
        scaled = queries_t[head_rows, :].astype(F32) * (scale * LOG2E)
        high = scaled.astype(BF16).astype(F32)
        left = jnp.transpose(jnp.concatenate([high, stack_rows(scaled - high, (1.0,))], axis=0)).astype(BF16)
        k_rows = keys_t[head_rows, :].astype(F32)
        scores = mm(left, jnp.concatenate([k_rows, stack_rows(k_rows, (bias,))], axis=0).astype(BF16))
        top = jnp.max(scores, axis=1, keepdims=True)
        exps = jnp.exp2(scores - top).astype(BF16)
        exps_out[k] = exps
        summed = mm_nt(stack_rows(values_t[head_rows, :], (1.0,)).astype(BF16), exps)
        inv = 1.0 / summed[HEAD_DIM : HEAD_DIM + 1]
        context_t[head_rows, :] = summed[0:HEAD_DIM] * inv
        inv_t[pl.ds(h, 1), :] = inv

    @pl.when(step == heads // PER_STEP - 1)
    def _():
        rows_out = mm(jnp.transpose(context_t[...]).astype(BF16), w_out[...]).astype(BF16)
        keep_out[...] = jnp.where(flag, rows_out[:, half:], rows_out[:, :half])
        send_out[...] = jnp.where(flag, rows_out[:, :half], rows_out[:, half:])


def backward_kernel(
    heads, regions, capacity, core, marks, slab_in, got, got_other, w_own, w_other, gain, queries_t, keys_in, values_t, exps_in,
    context_t, inv_t, keep_out, send_out, grad_keep, grad_send, d_context_t, d_query, d_key_t, d_value_t, grad_slab, lift, lift_other
):
    step = pl.program_id(0)
    width = heads * HEAD_DIM
    half = width // 2
    flag = core[0] > 0
    lane = iota((1, width), 1)
    scale = HEAD_DIM**-0.5

    @pl.when(step == 0)
    def _():
        w_o = full_weights(core, w_own, w_other)[3]
        grad_slab[...] = bin_rows(regions, capacity, core, marks, got, got_other, lift, lift_other)
        d_context_t[...] = mm_nt(w_o, grad_slab[...]).astype(BF16)

    for k in range(PER_STEP):
        h = step * PER_STEP + k
        head_rows = pl.ds(pl.multiple_of(h * HEAD_DIM, HEAD_DIM), HEAD_DIM)
        own_lane = lax.shift_right_logical(lane, log2_of(HEAD_DIM)) == h
        scaled = (d_context_t[head_rows, :].astype(F32) * inv_t[pl.ds(h, 1), :]).astype(BF16)
        dot = -jnp.sum(scaled.astype(F32) * context_t[head_rows, :], axis=0, keepdims=True)
        dot_high = dot.astype(BF16).astype(F32)
        left = jnp.transpose(stack_rows(scaled, (dot_high, dot - dot_high))).astype(BF16)
        centred = mm(left, stack_rows(values_t[head_rows, :], (1.0, 1.0)).astype(BF16))
        exps = exps_in[k]
        d_scores = (exps.astype(F32) * centred).astype(BF16)
        dq = mm(d_scores, keys_in[...])
        d_query[...] = jnp.where(own_lane, dq * scale, d_query[...])
        d_key_t[head_rows, :] = mm(queries_t[head_rows, :], d_scores) * scale
        d_value_t[head_rows, :] = mm(scaled, exps)

    @pl.when(step == heads // PER_STEP - 1)
    def _():
        w_q, w_k, w_v, _ = full_weights(core, w_own, w_other)
        slab = slab_in[...]
        wide, inverse, normed = norm_rows(slab, gain[...], width)
        dq = d_query[...].astype(BF16)
        dk = jnp.transpose(d_key_t[...]).astype(BF16)
        dv = jnp.transpose(d_value_t[...]).astype(BF16)
        d_normed = mm_nt(dq, w_q) + mm_nt(dk, w_k) + mm_nt(dv, w_v)
        scaled = gain[...] * d_normed
        along = jnp.sum(scaled * wide, axis=1, keepdims=True)
        d_slab = (inverse * scaled - wide * (inverse * inverse * inverse) * along / width).astype(BF16)
        keep_out[...] = jnp.where(flag, d_slab[:, half:], d_slab[:, :half])
        send_out[...] = jnp.where(flag, d_slab[:, :half], d_slab[:, half:])
        normed_t = jnp.transpose(normed.astype(F32)).astype(BF16)
        place = 0
        for d_rows in (dq, dk, dv):
            grad = mm(normed_t, d_rows)
            grad_keep[place : place + width, :] = jnp.where(flag, grad[:, half:], grad[:, :half])
            grad_send[place : place + width, :] = jnp.where(flag, grad[:, :half], grad[:, half:]).astype(BF16)
            place += width
        grad = mm(context_t[...].astype(BF16), grad_slab[...])
        for part in range(2):
            block = grad[:, part * half : (part + 1) * half]
            grad_keep[place : place + half, :] = jnp.where(flag, block[half:], block[:half])
            grad_send[place : place + half, :] = jnp.where(flag, block[:half], block[half:]).astype(BF16)
            place += half
        gain_grad = jnp.sum(d_normed * wide * inverse, axis=0, keepdims=True)
        pick = iota((16, half), 0)
        block = jnp.where(pick == 0, gain_grad[:, :half], jnp.where(pick == 1, gain_grad[:, half:], 0.0))
        grad_keep[place : place + 16, :] = block
        grad_send[place : place + 16, :] = block.astype(BF16)


def shape(dims, dtype):
    return jax.ShapeDtypeStruct(tuple(dims), dtype)


SMEM_SPEC = pl.BlockSpec(memory_space=pltpu.SMEM)


def whole(array):
    zeros = (0,) * len(array.shape)
    return pl.BlockSpec(tuple(array.shape), lambda *_: zeros)


def simple_call(kernel, outs, inputs, scratch=(), scalars=0, scalar_outs=0):
    specs = [SMEM_SPEC] * scalars + [whole(x) for x in inputs[scalars:]]
    return pl.pallas_call(
        kernel,
        out_shape=outs,
        in_specs=specs,
        out_specs=tuple(whole(x) for x in outs[: len(outs) - scalar_outs]) + (SMEM_SPEC,) * scalar_outs,
        scratch_shapes=scratch,
    )(*inputs)


def on_device(
    features,
    element_kinds,
    bin_cells,
    kind_embed,
    norm_gain,
    w_query,
    w_key,
    w_value,
    w_out,
    cotangent,
):
    regions = lax.axis_size("region")
    cores = lax.axis_size("head")
    local_rows = BINS_DEV * SLOTS
    capacity = local_rows // regions
    count, half = features.shape
    width = w_query.shape[0]
    heads = width // HEAD_DIM
    assert cores == BINS_DEV and half * cores == width and half == LANES
    core = lax.axis_index("head").astype(I32).reshape(1)
    swap = [(i, (i + 1) % cores) for i in range(cores)]

    def other_core(x):
        return lax.ppermute(x, "head", swap)

    def exchange(x):
        return lax.all_to_all(x, "region", split_axis=0, concat_axis=0, tiled=True)

    gain = norm_gain.reshape(1, width)
    kinds_row = element_kinds.reshape(1, count)
    packed_shape = shape((regions, capacity, half), BF16)
    tagged_shape = shape((regions, capacity + TAG_ROWS, half), BF16)
    packed_base, target, w_own = simple_call(
        functools.partial(pack_kernel, regions, capacity),
        (tagged_shape, shape((1, count), I32), shape((4, width, half), BF16)),
        (bin_cells.reshape(1, count), kinds_row, features, kind_embed, w_query, w_key, w_value, w_out),
    )
    w_other = other_core(w_own)
    got_base = exchange(packed_base)
    (packed_cot,) = simple_call(
        functools.partial(pack_cot_kernel, regions, capacity), (tagged_shape,), (target, kinds_row, cotangent)
    )
    got_base, packed_cot = lax.optimization_barrier((got_base, packed_cot))
    got_cot = exchange(packed_cot)
    got_base_other = other_core(got_base)
    rows_shape = shape((SLOTS, half), BF16)
    lift = pltpu.VMEM((SLOTS + capacity, half), F32)

    turned_shape = shape((width, SLOTS), BF16)
    exps_shape = shape((heads, SLOTS, SLOTS), BF16)
    exps_spec = pl.BlockSpec((PER_STEP, SLOTS, SLOTS), lambda h: (h, 0, 0))
    inputs = (core, got_base, got_base_other, w_own, w_other, gain)
    outs = (
        shape((SLOTS, width), BF16),
        turned_shape,
        shape((SLOTS, width), BF16),
        turned_shape,
        exps_shape,
        shape((width, SLOTS), F32),
        shape((heads, SLOTS), F32),
        rows_shape,
        rows_shape,
        shape((2, regions + 1), I32),
    )
    work = heads * SLOTS * SLOTS
    slab, queries_t, keys, values_t, exps, context_t, inv_t, attn_keep, attn_send, marks = pl.pallas_call(
        functools.partial(forward_kernel, heads, regions, capacity),
        grid=(heads // PER_STEP,),
        out_shape=outs,
        in_specs=[SMEM_SPEC] + [whole(x) for x in inputs[1:]],
        out_specs=tuple(exps_spec if x is exps_shape else whole(x) for x in outs[:-1]) + (SMEM_SPEC,),
        scratch_shapes=(pltpu.VMEM((width, SLOTS), BF16), pltpu.VMEM((width, width), BF16), lift, lift),
        cost_estimate=pl.CostEstimate(flops=4 * work * width, transcendentals=work, bytes_accessed=2 * work),
        name="forward",
    )(*inputs)
    attn_other = other_core(attn_send)
    (packed_attn,) = simple_call(
        functools.partial(ungroup_kernel, regions, capacity),
        (packed_shape,),
        (core, marks, attn_keep, attn_other),
        scratch=(lift, lift),
        scalars=2,
    )

    got_cot_other = other_core(got_cot)
    grad_rows = 4 * width + 16
    inputs = (core, marks, slab, got_cot, got_cot_other, w_own, w_other, gain, queries_t, keys, values_t, exps, context_t, inv_t)
    outs = (rows_shape, rows_shape, shape((grad_rows, half), F32), shape((grad_rows, half), BF16))
    d_keep, d_send, grad_keep, grad_send = pl.pallas_call(
        functools.partial(backward_kernel, heads, regions, capacity),
        grid=(heads // PER_STEP,),
        out_shape=outs,
        in_specs=[SMEM_SPEC] * 2 + [exps_spec if x is exps else whole(x) for x in inputs[2:]],
        out_specs=tuple(whole(x) for x in outs),
        scratch_shapes=(
            pltpu.VMEM((width, SLOTS), BF16),
            pltpu.VMEM((SLOTS, width), F32),
            pltpu.VMEM((width, SLOTS), F32),
            pltpu.VMEM((width, SLOTS), F32),
            pltpu.VMEM((SLOTS, width), BF16),
            lift,
            lift,
        ),
        cost_estimate=pl.CostEstimate(flops=8 * work * width, transcendentals=0, bytes_accessed=2 * work),
        name="backward",
    )(*inputs)

    share = 4 * width // regions
    pairs, gain_part = simple_call(
        functools.partial(pair_kernel, regions),
        (shape((regions, share, half), BF16), shape((16, half), BF16)),
        (grad_keep, other_core(grad_send)),
    )
    payload_shape = shape((regions, capacity + share + KIND_ROWS, half), BF16)
    packed_grad, extra = simple_call(
        functools.partial(ungroup_grad_kernel, regions, capacity),
        (payload_shape, shape((KIND_ROWS, half), BF16)),
        (core, marks, d_keep, other_core(d_send), got_cot, gain_part),
        scratch=(lift, lift),
        scalars=2,
    )
    got_cot, packed_attn = lax.optimization_barrier((got_cot, packed_attn))
    home_attn = exchange(packed_attn)
    home_attn, pairs = lax.optimization_barrier((home_attn, pairs))
    shares = exchange(pairs)
    payload = pl.pallas_call(
        functools.partial(share_kernel, regions, capacity),
        out_shape=payload_shape,
        in_specs=[whole(shares), whole(extra), pl.BlockSpec(memory_space=pl.ANY)],
        out_specs=pl.BlockSpec(memory_space=pl.ANY),
        scratch_shapes=(pltpu.VMEM((share + KIND_ROWS, half), BF16), pltpu.SemaphoreType.DMA((regions,))),
        input_output_aliases={2: 0},
        name="share",
    )(shares, extra, packed_grad)
    home_grad = exchange(payload)
    (attended,) = simple_call(pick_kernel, (shape((count, half), BF16),), (target, home_attn))
    column_shape = shape((width, half), F32)
    grad_feats, grad_q, grad_k, grad_v, grad_o, grad_gain, grad_embed = simple_call(
        functools.partial(last_kernel, regions, capacity, float(count * regions) ** (-0.5)),
        (
            shape((count, half), BF16),
            column_shape,
            column_shape,
            column_shape,
            shape((half, width), F32),
            shape((1, width), F32),
            shape((KINDS, half), F32),
        ),
        (target, home_grad),
        scratch=(pltpu.VMEM((4 * width, half), F32),),
    )
    return (attended, grad_feats, grad_q, grad_k, grad_v, grad_o, grad_gain.reshape(width), grad_embed)


def solution(mesh):
    placed = (
        P(("groups", "region"), "head"),
        P(("groups", "region")),
        P(("groups", "region")),
        P(None, "head"),
        P(),
        P(None, "head"),
        P(None, "head"),
        P(None, "head"),
        P("head", None),
        P(("groups", "region"), "head"),
    )

    return jax.shard_map(
        on_device,
        mesh=mesh,
        in_specs=placed,
        out_specs=(
            P(("groups", "region"), "head"),
            P(("groups", "region"), "head"),
            P("groups", "head"),
            P("groups", "head"),
            P("groups", "head"),
            P(("groups", "head"), None),
            P("groups"),
            P("groups", "head"),
        ),
        check_vma=False,
    )
```

```python
import functools

import jax
import jax.numpy as jnp
from jax import lax
from jax.experimental import pallas as pl
from jax.experimental.pallas import tpu as pltpu
from jax.sharding import PartitionSpec as P


HEAD_DIM = 32
KINDS = 12
SLOTS = 1024
BINS_DEV = 2
MASKED = -1000000000.0
EPSILON = 1e-06
LOG2E = 1.4426950408889634

F32 = jnp.float32
BF16 = jnp.bfloat16
I32 = jnp.int32
LANES = 128
TAG_ROWS = 16
KIND_ROWS = 16
HEAD_PAD = 48
PER_STEP = 2
NT = (((1,), (1,)), ((), ()))
TN = (((0,), (0,)), ((), ()))


def iota(shape, axis):
    return lax.broadcasted_iota(I32, shape, axis)


def mm(a, b):
    return jnp.dot(a, b, preferred_element_type=F32)


def mm_nt(a, b):
    return lax.dot_general(a, b, NT, preferred_element_type=F32)


def mm_tn(a, b):
    return lax.dot_general(a, b, TN, preferred_element_type=F32)


def hot(condition):
    return jnp.where(condition, 1.0, 0.0).astype(BF16)


def log2_of(n):
    return n.bit_length() - 1


def turned(row):
    return jnp.transpose(jnp.broadcast_to(row.astype(F32), (LANES, row.shape[1])))


def running(group_hot):
    rows, count = group_hot.shape
    blocks = count // LANES
    stacked = jnp.concatenate([group_hot[:, k * LANES : (k + 1) * LANES] for k in range(blocks)], axis=0)
    before = hot(iota((LANES, LANES), 0) < iota((LANES, LANES), 1))
    inside = mm(stacked.astype(BF16), before)
    sums = jnp.sum(stacked, axis=1, keepdims=True)
    offset = jnp.zeros((rows, 1), F32)
    pieces = []
    for k in range(blocks):
        part = slice(k * rows, (k + 1) * rows)
        pieces.append(inside[part] + offset)
        offset = offset + sums[part]
    return jnp.concatenate(pieces, axis=1), offset


def positions(regions, capacity, cell):
    count = cell.shape[1]
    owner = lax.shift_right_logical(cell, log2_of(BINS_DEV * SLOTS))
    group = lax.shift_right_logical(cell, log2_of(SLOTS))
    classes = max(BINS_DEV * regions, 16)
    group_hot = jnp.where(iota((classes, count), 0) == group, 1.0, 0.0)
    before, counts = running(group_hot)
    rank = jnp.sum(before * group_hot, axis=0, keepdims=True).astype(I32)
    second = jnp.bitwise_and(group, 1) > 0
    return owner, jnp.where(second, capacity - 1 - rank, rank), counts


def to_chunks(capacity, place, owner_column, rows, first, many):
    chosen = hot(iota((capacity, place.shape[1]), 0) == place)
    wide = rows.astype(F32)
    masked = [jnp.where(owner_column == float(first + k), wide, 0.0).astype(BF16) for k in range(many)]
    return mm(chosen, jnp.concatenate(masked, axis=1)).astype(BF16)


def pack_kernel(regions, capacity, cells, kinds, feats, embed, w_q, w_k, w_v, w_o, out_base, out_target, out_w):
    count, half = feats.shape
    owner, place, counts = positions(regions, capacity, cells[...])
    out_target[...] = owner * capacity + place
    kinds_hot = hot(iota((KINDS, count), 0) == kinds[...])
    base = (feats[...].astype(F32) + mm_tn(kinds_hot, embed[...])).astype(BF16)
    owner_column = turned(owner)
    tag_place = iota((TAG_ROWS, half), 0)
    for r in range(0, regions, 2):
        moved = to_chunks(capacity, place, owner_column, base, r, 2)
        for k in range(2):
            out_base[r + k, 0:capacity, :] = moved[:, k * half : (k + 1) * half]
            pair = 2 * (r + k)
            first = counts[pair : pair + 1]
            second = counts[pair + 1 : pair + 2]
            tags = jnp.where(tag_place == 0, first, jnp.where(tag_place == 1, second, 0.0))
            out_base[r + k, capacity : capacity + TAG_ROWS, :] = tags.astype(BF16)
    out_w[0] = w_q[...]
    out_w[1] = w_k[...]
    out_w[2] = w_v[...]
    out_w[3, 0:half, :] = w_o[:, 0:half]
    out_w[3, half:, :] = w_o[:, half:]


def pack_cot_kernel(regions, capacity, target_ref, kinds, cot, out_cot):
    count, half = cot.shape
    target = target_ref[...]
    owner = lax.shift_right_logical(target, log2_of(capacity))
    place = jnp.bitwise_and(target, capacity - 1)
    owner_column = turned(owner)
    tags = jnp.where(iota((TAG_ROWS, count), 0) == 0, kinds[...] + 1, 0).astype(F32).astype(BF16)
    for r in range(0, regions, 2):
        moved = to_chunks(capacity, place, owner_column, cot[...], r, 2)
        for k in range(2):
            out_cot[r + k, 0:capacity, :] = moved[:, k * half : (k + 1) * half]
    for r in range(regions):
        chosen = hot(iota((capacity, count), 0) + r * capacity == target)
        tag = mm_nt(tags, chosen)
        if capacity >= LANES:
            tag = jnp.concatenate([tag[0:8, 0:LANES], tag[0:8, LANES : 2 * LANES]], axis=0)
        else:
            tag = jnp.concatenate([tag, jnp.zeros((TAG_ROWS, LANES - capacity), F32)], axis=1)
        out_cot[r, capacity : capacity + TAG_ROWS, :] = tag.astype(BF16)


def count_rows(regions, capacity, got, marks):
    start = jnp.int32(0)
    end = jnp.int32(SLOTS)
    for r in range(regions):
        block = got[r, capacity : capacity + TAG_ROWS, :].astype(F32)
        marks[0, r] = start
        marks[1, r] = end
        start = start + jnp.max(block[0:1, :]).astype(I32)
        end = end - jnp.max(block[1:2, :]).astype(I32)
    marks[0, regions] = start
    marks[1, regions] = end


def is_filled(regions, core, marks, place):
    first = jnp.where(place < marks[0, regions], 1.0, 0.0)
    second = jnp.where(place >= marks[1, regions], 1.0, 0.0)
    return jnp.where(core[0] > 0, second, first)


def bin_rows(regions, capacity, core, marks, own, other, lift, lift_other):
    flag = core[0] > 0
    for r in range(regions):
        place = pl.ds(marks[core[0], r], capacity)
        lift[place, :] = own[r, 0:capacity, :].astype(F32)
        lift_other[place, :] = other[r, 0:capacity, :].astype(F32)
    place = pl.ds(pl.multiple_of(core[0] * capacity, capacity), SLOTS)
    rows = jnp.concatenate(ordered(flag, lift[place, :], lift_other[place, :]), axis=1)
    filled = is_filled(regions, core, marks, iota((SLOTS, 1), 0))
    return jnp.where(filled > 0.5, rows, 0.0).astype(BF16)


def arrival_rows(regions, capacity, core, marks, own, other, out, front, back):
    flag = core[0] > 0
    x = own[...].astype(F32)
    y = other[...].astype(F32)
    front[0:SLOTS, :] = jnp.where(flag, y, x)
    front[SLOTS:, :] = jnp.zeros((capacity, x.shape[1]), F32)
    back[0:capacity, :] = jnp.zeros((capacity, x.shape[1]), F32)
    back[capacity:, :] = jnp.where(flag, x, y)
    row = iota((capacity, 1), 0)
    for r in range(regions):
        held = marks[0, r + 1] - marks[0, r]
        rows = jnp.where(row < held, front[pl.ds(marks[0, r], capacity), :], back[pl.ds(marks[1, r], capacity), :])
        out[r, 0:capacity, :] = rows.astype(BF16)


def ungroup_kernel(regions, capacity, core, marks, own, other, out, front, back):
    arrival_rows(regions, capacity, core, marks, own, other, out, front, back)


def ungroup_grad_kernel(regions, capacity, core, marks, own, other, tagged, gain_part, out, extra, front, back):
    arrival_rows(regions, capacity, core, marks, own, other, out, front, back)
    total = jnp.zeros((KIND_ROWS, own.shape[1]), F32)
    for r in range(regions):
        block = tagged[r, capacity : capacity + TAG_ROWS, :].astype(F32)
        if capacity >= LANES:
            kind = jnp.concatenate([block[0:1], block[8:9]], axis=1)
        else:
            kind = block[0:1, 0:capacity]
        kinds_hot = hot(iota((KIND_ROWS, capacity), 0) == kind.astype(I32) - 1)
        total = total + mm(kinds_hot, out[r, 0:capacity, :])
    place = iota((KIND_ROWS, 1), 0)
    first = gain_part[0:1, :].astype(F32)
    second = gain_part[1:2, :].astype(F32)
    extra[...] = jnp.where(place == KINDS, first, jnp.where(place == KINDS + 1, second, total)).astype(BF16)


def pair_kernel(regions, own, received, out, gain_part):
    share = out.shape[1]
    for r in range(regions):
        rows = slice(r * share, (r + 1) * share)
        out[r] = (own[rows, :].astype(F32) + received[rows, :].astype(F32)).astype(BF16)
    gain_part[...] = (own[regions * share :, :].astype(F32) + received[regions * share :, :].astype(F32)).astype(BF16)


def share_kernel(regions, capacity, got, extra, packed, out, tail, sems):
    total = got[0].astype(F32)
    for r in range(1, regions):
        total = total + got[r].astype(F32)
    share = total.shape[0]
    tail[0:share, :] = total.astype(BF16)
    tail[share:, :] = extra[...]
    copies = [
        pltpu.make_async_copy(tail, out.at[r, pl.ds(capacity, share + KIND_ROWS), :], sems.at[r]) for r in range(regions)
    ]
    for copy in copies:
        copy.start()
    for copy in copies:
        copy.wait()


def last_kernel(regions, capacity, factor, target_ref, got, out, out_q, out_k, out_v, out_o, out_gain, out_embed, flat):
    pick_kernel(target_ref, got, out)
    width, half = out_q.shape
    share = 4 * width // regions
    extra = jnp.zeros((KIND_ROWS, half), F32)
    for r in range(regions):
        flat[r * share : (r + 1) * share, :] = got[r, capacity : capacity + share, :].astype(F32) * factor
        extra = extra + got[r, capacity + share : capacity + share + KIND_ROWS, :].astype(F32)
    extra = extra * factor
    out_q[...] = flat[0:width]
    out_k[...] = flat[width : 2 * width]
    out_v[...] = flat[2 * width : 3 * width]
    out_o[:, 0:half] = flat[3 * width : 3 * width + half]
    out_o[:, half:] = flat[3 * width + half : 4 * width]
    out_embed[...] = extra[0:KINDS]
    out_gain[:, 0:half] = extra[KINDS : KINDS + 1]
    out_gain[:, half:] = extra[KINDS + 1 : KINDS + 2]


def pick_kernel(target_ref, got, out):
    regions = got.shape[0]
    capacity = BINS_DEV * SLOTS // regions
    count, half = out.shape
    target = target_ref[...]
    owner_column = turned(lax.shift_right_logical(target, log2_of(capacity)))
    place_column = turned(jnp.bitwise_and(target, capacity - 1))
    width = min(capacity, LANES)
    lane = iota((1, width), 1).astype(F32)
    step = 256
    for s in range(0, count, step):
        owner = owner_column[s : s + step]
        place = place_column[s : s + step, 0:width]
        chosen = [hot(place - float(k) == lane) for k in range(0, capacity, width)]
        chosen = jnp.concatenate(chosen, axis=1)
        total = jnp.zeros((step, half), F32)
        for r in range(0, regions, 2):
            chunks = jnp.concatenate([got[r, 0:capacity, :], got[r + 1, 0:capacity, :]], axis=1)
            rows = mm(chosen, chunks)
            total = jnp.where(owner == float(r), rows[:, :half], jnp.where(owner == float(r + 1), rows[:, half:], total))
        out[s : s + step, :] = total.astype(BF16)


def ordered(flag, own, other):
    first = jnp.where(flag, other, own)
    second = jnp.where(flag, own, other)
    return first, second


def full_weights(core, own, other):
    flag = core[0] > 0
    half = own.shape[2]
    columns = []
    for k in range(3):
        columns.append(jnp.concatenate(ordered(flag, own[k], other[k]), axis=1))
    top, bottom = ordered(flag, own[3], other[3])
    rows = [jnp.concatenate([part[0:half], part[half:]], axis=1) for part in (top, bottom)]
    return columns + [jnp.concatenate(rows, axis=0)]


def norm_rows(slab, gain, width):
    wide = slab.astype(F32)
    inverse = lax.rsqrt(jnp.sum(wide * wide, axis=1, keepdims=True) / width + EPSILON)
    return wide, inverse, (wide * inverse * gain).astype(BF16)


def stack_rows(rows, extra):
    place = iota((HEAD_PAD - HEAD_DIM, rows.shape[1]), 0)
    tail = jnp.zeros(place.shape, F32)
    for k, value in enumerate(extra):
        tail = jnp.where(place == k, value, tail)
    return jnp.concatenate([rows.astype(F32), tail], axis=0)


def forward_kernel(
    heads, regions, capacity, core, got, got_other, w_own, w_other, gain, slab_out, queries_t, keys_out, values_t, exps_out,
    context_t, inv_t, keep_out, send_out, marks, keys_t, w_out, lift, lift_other
):
    step = pl.program_id(0)
    width = heads * HEAD_DIM
    half = width // 2
    flag = core[0] > 0
    scale = HEAD_DIM**-0.5

    @pl.when(step == 0)
    def _():
        w_q, w_k, w_v, w_o = full_weights(core, w_own, w_other)
        w_out[...] = w_o
        count_rows(regions, capacity, got, marks)
        slab = bin_rows(regions, capacity, core, marks, got, got_other, lift, lift_other)
        slab_out[...] = slab
        _, _, normed = norm_rows(slab, gain[...], width)
        queries_t[...] = jnp.transpose(mm(normed, w_q)).astype(BF16)
        k = mm(normed, w_k)
        keys_out[...] = k.astype(BF16)
        keys_t[...] = jnp.transpose(k).astype(BF16)
        values_t[...] = jnp.transpose(mm(normed, w_v)).astype(BF16)

    bias = jnp.where(is_filled(regions, core, marks, iota((1, SLOTS), 1)) > 0.5, 0.0, MASKED / scale)
    for k in range(PER_STEP):
        h = step * PER_STEP + k
        head_rows = pl.ds(pl.multiple_of(h * HEAD_DIM, HEAD_DIM), HEAD_DIM)
        scaled = queries_t[head_rows, :].astype(F32) * (scale * LOG2E)
        high = scaled.astype(BF16).astype(F32)
        left = jnp.transpose(jnp.concatenate([high, stack_rows(scaled - high, (1.0,))], axis=0)).astype(BF16)
        k_rows = keys_t[head_rows, :].astype(F32)
        scores = mm(left, jnp.concatenate([k_rows, stack_rows(k_rows, (bias,))], axis=0).astype(BF16))
        top = jnp.max(scores, axis=1, keepdims=True)
        exps = jnp.exp2(scores - top).astype(BF16)
        exps_out[k] = exps
        summed = mm_nt(stack_rows(values_t[head_rows, :], (1.0,)).astype(BF16), exps)
        inv = 1.0 / summed[HEAD_DIM : HEAD_DIM + 1]
        context_t[head_rows, :] = summed[0:HEAD_DIM] * inv
        inv_t[pl.ds(h, 1), :] = inv

    @pl.when(step == heads // PER_STEP - 1)
    def _():
        rows_out = mm(jnp.transpose(context_t[...]).astype(BF16), w_out[...]).astype(BF16)
        keep_out[...] = jnp.where(flag, rows_out[:, half:], rows_out[:, :half])
        send_out[...] = jnp.where(flag, rows_out[:, :half], rows_out[:, half:])


def backward_kernel(
    heads, regions, capacity, core, marks, slab_in, got, got_other, w_own, w_other, gain, queries_t, keys_in, values_t, exps_in,
    context_t, inv_t, keep_out, send_out, grad_keep, grad_send, d_context_t, d_query, d_key_t, d_value_t, grad_slab, lift, lift_other
):
    step = pl.program_id(0)
    width = heads * HEAD_DIM
    half = width // 2
    flag = core[0] > 0
    lane = iota((1, width), 1)
    scale = HEAD_DIM**-0.5

    @pl.when(step == 0)
    def _():
        w_o = full_weights(core, w_own, w_other)[3]
        grad_slab[...] = bin_rows(regions, capacity, core, marks, got, got_other, lift, lift_other)
        d_context_t[...] = mm_nt(w_o, grad_slab[...]).astype(BF16)

    for k in range(PER_STEP):
        h = step * PER_STEP + k
        head_rows = pl.ds(pl.multiple_of(h * HEAD_DIM, HEAD_DIM), HEAD_DIM)
        own_lane = lax.shift_right_logical(lane, log2_of(HEAD_DIM)) == h
        scaled = (d_context_t[head_rows, :].astype(F32) * inv_t[pl.ds(h, 1), :]).astype(BF16)
        dot = -jnp.sum(scaled.astype(F32) * context_t[head_rows, :], axis=0, keepdims=True)
        dot_high = dot.astype(BF16).astype(F32)
        left = jnp.transpose(stack_rows(scaled, (dot_high, dot - dot_high))).astype(BF16)
        centred = mm(left, stack_rows(values_t[head_rows, :], (1.0, 1.0)).astype(BF16))
        exps = exps_in[k]
        d_scores = (exps.astype(F32) * centred).astype(BF16)
        dq = mm(d_scores, keys_in[...])
        d_query[...] = jnp.where(own_lane, dq * scale, d_query[...])
        d_key_t[head_rows, :] = mm(queries_t[head_rows, :], d_scores) * scale
        d_value_t[head_rows, :] = mm(scaled, exps)

    @pl.when(step == heads // PER_STEP - 1)
    def _():
        w_q, w_k, w_v, _ = full_weights(core, w_own, w_other)
        slab = slab_in[...]
        wide, inverse, normed = norm_rows(slab, gain[...], width)
        dq = d_query[...].astype(BF16)
        dk = jnp.transpose(d_key_t[...]).astype(BF16)
        dv = jnp.transpose(d_value_t[...]).astype(BF16)
        d_normed = mm_nt(dq, w_q) + mm_nt(dk, w_k) + mm_nt(dv, w_v)
        scaled = gain[...] * d_normed
        along = jnp.sum(scaled * wide, axis=1, keepdims=True)
        d_slab = (inverse * scaled - wide * (inverse * inverse * inverse) * along / width).astype(BF16)
        keep_out[...] = jnp.where(flag, d_slab[:, half:], d_slab[:, :half])
        send_out[...] = jnp.where(flag, d_slab[:, :half], d_slab[:, half:])
        normed_t = jnp.transpose(normed.astype(F32)).astype(BF16)
        place = 0
        for d_rows in (dq, dk, dv):
            grad = mm(normed_t, d_rows)
            grad_keep[place : place + width, :] = jnp.where(flag, grad[:, half:], grad[:, :half]).astype(BF16)
            grad_send[place : place + width, :] = jnp.where(flag, grad[:, :half], grad[:, half:]).astype(BF16)
            place += width
        grad = mm(context_t[...].astype(BF16), grad_slab[...])
        for part in range(2):
            block = grad[:, part * half : (part + 1) * half]
            grad_keep[place : place + half, :] = jnp.where(flag, block[half:], block[:half]).astype(BF16)
            grad_send[place : place + half, :] = jnp.where(flag, block[:half], block[half:]).astype(BF16)
            place += half
        gain_grad = jnp.sum(d_normed * wide * inverse, axis=0, keepdims=True)
        pick = iota((16, half), 0)
        block = jnp.where(pick == 0, gain_grad[:, :half], jnp.where(pick == 1, gain_grad[:, half:], 0.0))
        grad_keep[place : place + 16, :] = block.astype(BF16)
        grad_send[place : place + 16, :] = block.astype(BF16)


def shape(dims, dtype):
    return jax.ShapeDtypeStruct(tuple(dims), dtype)


SMEM_SPEC = pl.BlockSpec(memory_space=pltpu.SMEM)


def whole(array):
    zeros = (0,) * len(array.shape)
    return pl.BlockSpec(tuple(array.shape), lambda *_: zeros)


def simple_call(kernel, outs, inputs, scratch=(), scalars=0, scalar_outs=0):
    specs = [SMEM_SPEC] * scalars + [whole(x) for x in inputs[scalars:]]
    return pl.pallas_call(
        kernel,
        out_shape=outs,
        in_specs=specs,
        out_specs=tuple(whole(x) for x in outs[: len(outs) - scalar_outs]) + (SMEM_SPEC,) * scalar_outs,
        scratch_shapes=scratch,
    )(*inputs)


def on_device(
    features,
    element_kinds,
    bin_cells,
    kind_embed,
    norm_gain,
    w_query,
    w_key,
    w_value,
    w_out,
    cotangent,
):
    regions = lax.axis_size("region")
    cores = lax.axis_size("head")
    local_rows = BINS_DEV * SLOTS
    capacity = local_rows // regions
    count, half = features.shape
    width = w_query.shape[0]
    heads = width // HEAD_DIM
    assert cores == BINS_DEV and half * cores == width and half == LANES
    core = lax.axis_index("head").astype(I32).reshape(1)
    swap = [(i, (i + 1) % cores) for i in range(cores)]

    def other_core(x):
        return lax.ppermute(x, "head", swap)

    def exchange(x):
        return lax.all_to_all(x, "region", split_axis=0, concat_axis=0, tiled=True)

    gain = norm_gain.reshape(1, width)
    kinds_row = element_kinds.reshape(1, count)
    packed_shape = shape((regions, capacity, half), BF16)
    tagged_shape = shape((regions, capacity + TAG_ROWS, half), BF16)
    packed_base, target, w_own = simple_call(
        functools.partial(pack_kernel, regions, capacity),
        (tagged_shape, shape((1, count), I32), shape((4, width, half), BF16)),
        (bin_cells.reshape(1, count), kinds_row, features, kind_embed, w_query, w_key, w_value, w_out),
    )
    w_other = other_core(w_own)
    got_base = exchange(packed_base)
    (packed_cot,) = simple_call(
        functools.partial(pack_cot_kernel, regions, capacity), (tagged_shape,), (target, kinds_row, cotangent)
    )
    got_base, packed_cot = lax.optimization_barrier((got_base, packed_cot))
    got_cot = exchange(packed_cot)
    got_base_other = other_core(got_base)
    rows_shape = shape((SLOTS, half), BF16)
    lift = pltpu.VMEM((SLOTS + capacity, half), F32)

    turned_shape = shape((width, SLOTS), BF16)
    exps_shape = shape((heads, SLOTS, SLOTS), BF16)
    exps_spec = pl.BlockSpec((PER_STEP, SLOTS, SLOTS), lambda h: (h, 0, 0))
    inputs = (core, got_base, got_base_other, w_own, w_other, gain)
    outs = (
        shape((SLOTS, width), BF16),
        turned_shape,
        shape((SLOTS, width), BF16),
        turned_shape,
        exps_shape,
        shape((width, SLOTS), F32),
        shape((heads, SLOTS), F32),
        rows_shape,
        rows_shape,
        shape((2, regions + 1), I32),
    )
    work = heads * SLOTS * SLOTS
    slab, queries_t, keys, values_t, exps, context_t, inv_t, attn_keep, attn_send, marks = pl.pallas_call(
        functools.partial(forward_kernel, heads, regions, capacity),
        grid=(heads // PER_STEP,),
        out_shape=outs,
        in_specs=[SMEM_SPEC] + [whole(x) for x in inputs[1:]],
        out_specs=tuple(exps_spec if x is exps_shape else whole(x) for x in outs[:-1]) + (SMEM_SPEC,),
        scratch_shapes=(pltpu.VMEM((width, SLOTS), BF16), pltpu.VMEM((width, width), BF16), lift, lift),
        cost_estimate=pl.CostEstimate(flops=4 * work * width, transcendentals=work, bytes_accessed=2 * work),
        name="forward",
    )(*inputs)
    attn_other = other_core(attn_send)
    (packed_attn,) = simple_call(
        functools.partial(ungroup_kernel, regions, capacity),
        (packed_shape,),
        (core, marks, attn_keep, attn_other),
        scratch=(lift, lift),
        scalars=2,
    )

    got_cot_other = other_core(got_cot)
    grad_rows = 4 * width + 16
    inputs = (core, marks, slab, got_cot, got_cot_other, w_own, w_other, gain, queries_t, keys, values_t, exps, context_t, inv_t)
    outs = (rows_shape, rows_shape, shape((grad_rows, half), BF16), shape((grad_rows, half), BF16))
    d_keep, d_send, grad_keep, grad_send = pl.pallas_call(
        functools.partial(backward_kernel, heads, regions, capacity),
        grid=(heads // PER_STEP,),
        out_shape=outs,
        in_specs=[SMEM_SPEC] * 2 + [exps_spec if x is exps else whole(x) for x in inputs[2:]],
        out_specs=tuple(whole(x) for x in outs),
        scratch_shapes=(
            pltpu.VMEM((width, SLOTS), BF16),
            pltpu.VMEM((SLOTS, width), F32),
            pltpu.VMEM((width, SLOTS), F32),
            pltpu.VMEM((width, SLOTS), F32),
            pltpu.VMEM((SLOTS, width), BF16),
            lift,
            lift,
        ),
        cost_estimate=pl.CostEstimate(flops=8 * work * width, transcendentals=0, bytes_accessed=2 * work),
        name="backward",
    )(*inputs)

    share = 4 * width // regions
    pairs, gain_part = simple_call(
        functools.partial(pair_kernel, regions),
        (shape((regions, share, half), BF16), shape((16, half), BF16)),
        (grad_keep, other_core(grad_send)),
    )
    payload_shape = shape((regions, capacity + share + KIND_ROWS, half), BF16)
    packed_grad, extra = simple_call(
        functools.partial(ungroup_grad_kernel, regions, capacity),
        (payload_shape, shape((KIND_ROWS, half), BF16)),
        (core, marks, d_keep, other_core(d_send), got_cot, gain_part),
        scratch=(lift, lift),
        scalars=2,
    )
    got_cot, packed_attn = lax.optimization_barrier((got_cot, packed_attn))
    home_attn = exchange(packed_attn)
    home_attn, pairs = lax.optimization_barrier((home_attn, pairs))
    shares = exchange(pairs)
    payload = pl.pallas_call(
        functools.partial(share_kernel, regions, capacity),
        out_shape=payload_shape,
        in_specs=[whole(shares), whole(extra), pl.BlockSpec(memory_space=pl.ANY)],
        out_specs=pl.BlockSpec(memory_space=pl.ANY),
        scratch_shapes=(pltpu.VMEM((share + KIND_ROWS, half), BF16), pltpu.SemaphoreType.DMA((regions,))),
        input_output_aliases={2: 0},
        name="share",
    )(shares, extra, packed_grad)
    home_grad = exchange(payload)
    (attended,) = simple_call(pick_kernel, (shape((count, half), BF16),), (target, home_attn))
    column_shape = shape((width, half), F32)
    grad_feats, grad_q, grad_k, grad_v, grad_o, grad_gain, grad_embed = simple_call(
        functools.partial(last_kernel, regions, capacity, float(count * regions) ** (-0.5)),
        (
            shape((count, half), BF16),
            column_shape,
            column_shape,
            column_shape,
            shape((half, width), F32),
            shape((1, width), F32),
            shape((KINDS, half), F32),
        ),
        (target, home_grad),
        scratch=(pltpu.VMEM((4 * width, half), F32),),
    )
    return (attended, grad_feats, grad_q, grad_k, grad_v, grad_o, grad_gain.reshape(width), grad_embed)


def solution(mesh):
    placed = (
        P(("groups", "region"), "head"),
        P(("groups", "region")),
        P(("groups", "region")),
        P(None, "head"),
        P(),
        P(None, "head"),
        P(None, "head"),
        P(None, "head"),
        P("head", None),
        P(("groups", "region"), "head"),
    )

    return jax.shard_map(
        on_device,
        mesh=mesh,
        in_specs=placed,
        out_specs=(
            P(("groups", "region"), "head"),
            P(("groups", "region"), "head"),
            P("groups", "head"),
            P("groups", "head"),
            P("groups", "head"),
            P(("groups", "head"), None),
            P("groups"),
            P("groups", "head"),
        ),
        check_vma=False,
    )
```

```python
import functools

import jax
import jax.numpy as jnp
from jax import lax
from jax.experimental import pallas as pl
from jax.experimental.pallas import tpu as pltpu
from jax.sharding import PartitionSpec as P


HEAD_DIM = 32
KINDS = 12
SLOTS = 1024
BINS_DEV = 2
MASKED = -1000000000.0
EPSILON = 1e-06
LOG2E = 1.4426950408889634

F32 = jnp.float32
BF16 = jnp.bfloat16
I32 = jnp.int32
LANES = 128
TAG_ROWS = 16
KIND_ROWS = 16
HEAD_PAD = 48
PER_STEP = 2
NT = (((1,), (1,)), ((), ()))
TN = (((0,), (0,)), ((), ()))


def iota(shape, axis):
    return lax.broadcasted_iota(I32, shape, axis)


def mm(a, b):
    return jnp.dot(a, b, preferred_element_type=F32)


def mm_nt(a, b):
    return lax.dot_general(a, b, NT, preferred_element_type=F32)


def mm_tn(a, b):
    return lax.dot_general(a, b, TN, preferred_element_type=F32)


def hot(condition):
    return jnp.where(condition, 1.0, 0.0).astype(BF16)


def log2_of(n):
    return n.bit_length() - 1


def turned(row):
    return jnp.transpose(jnp.broadcast_to(row.astype(F32), (LANES, row.shape[1])))


def running(group_hot):
    rows, count = group_hot.shape
    blocks = count // LANES
    stacked = jnp.concatenate([group_hot[:, k * LANES : (k + 1) * LANES] for k in range(blocks)], axis=0)
    before = hot(iota((LANES, LANES), 0) < iota((LANES, LANES), 1))
    inside = mm(stacked.astype(BF16), before)
    sums = jnp.sum(stacked, axis=1, keepdims=True)
    offset = jnp.zeros((rows, 1), F32)
    pieces = []
    for k in range(blocks):
        part = slice(k * rows, (k + 1) * rows)
        pieces.append(inside[part] + offset)
        offset = offset + sums[part]
    return jnp.concatenate(pieces, axis=1), offset


def positions(regions, capacity, cell):
    count = cell.shape[1]
    owner = lax.shift_right_logical(cell, log2_of(BINS_DEV * SLOTS))
    group = lax.shift_right_logical(cell, log2_of(SLOTS))
    classes = max(BINS_DEV * regions, 16)
    group_hot = jnp.where(iota((classes, count), 0) == group, 1.0, 0.0)
    before, counts = running(group_hot)
    rank = jnp.sum(before * group_hot, axis=0, keepdims=True).astype(I32)
    second = jnp.bitwise_and(group, 1) > 0
    return owner, jnp.where(second, capacity - 1 - rank, rank), counts


def to_chunks(capacity, place, owner_column, rows, first, many):
    chosen = hot(iota((capacity, place.shape[1]), 0) == place)
    wide = rows.astype(F32)
    masked = [jnp.where(owner_column == float(first + k), wide, 0.0).astype(BF16) for k in range(many)]
    return mm(chosen, jnp.concatenate(masked, axis=1)).astype(BF16)


def pack_kernel(regions, capacity, cells, kinds, embed, feats_far, out_target, out_far, feats, out_base, sem, sems):
    count, half = feats.shape
    arrive = pltpu.make_async_copy(feats_far, feats, sem)
    arrive.start()
    owner, place, counts = positions(regions, capacity, cells[...])
    out_target[...] = owner * capacity + place
    kinds_hot = hot(iota((KINDS, count), 0) == kinds[...])
    arrive.wait()
    base = (feats[...].astype(F32) + mm_tn(kinds_hot, embed[...])).astype(BF16)
    owner_column = turned(owner)
    tag_place = iota((TAG_ROWS, half), 0)
    copies = []
    for r in range(0, regions, 2):
        moved = to_chunks(capacity, place, owner_column, base, r, 2)
        for k in range(2):
            out_base[r + k, 0:capacity, :] = moved[:, k * half : (k + 1) * half]
            pair = 2 * (r + k)
            first = counts[pair : pair + 1]
            second = counts[pair + 1 : pair + 2]
            tags = jnp.where(tag_place == 0, first, jnp.where(tag_place == 1, second, 0.0))
            out_base[r + k, capacity : capacity + TAG_ROWS, :] = tags.astype(BF16)
        copies.append(pltpu.make_async_copy(out_base.at[pl.ds(r, 2)], out_far.at[pl.ds(r, 2)], sems.at[r // 2]))
        copies[-1].start()
    for copy in copies:
        copy.wait()


def pack_cot_kernel(regions, capacity, target_ref, kinds, cot, w_q, w_k, w_v, w_o, out_cot, out_w):
    count, half = cot.shape
    out_w[0] = w_q[...]
    out_w[1] = w_k[...]
    out_w[2] = w_v[...]
    out_w[3, 0:half, :] = w_o[:, 0:half]
    out_w[3, half:, :] = w_o[:, half:]
    target = target_ref[...]
    owner = lax.shift_right_logical(target, log2_of(capacity))
    place = jnp.bitwise_and(target, capacity - 1)
    owner_column = turned(owner)
    tags = jnp.where(iota((TAG_ROWS, count), 0) == 0, kinds[...] + 1, 0).astype(F32).astype(BF16)
    for r in range(0, regions, 2):
        moved = to_chunks(capacity, place, owner_column, cot[...], r, 2)
        for k in range(2):
            out_cot[r + k, 0:capacity, :] = moved[:, k * half : (k + 1) * half]
    for r in range(regions):
        chosen = hot(iota((capacity, count), 0) + r * capacity == target)
        tag = mm_nt(tags, chosen)
        if capacity >= LANES:
            tag = jnp.concatenate([tag[0:8, 0:LANES], tag[0:8, LANES : 2 * LANES]], axis=0)
        else:
            tag = jnp.concatenate([tag, jnp.zeros((TAG_ROWS, LANES - capacity), F32)], axis=1)
        out_cot[r, capacity : capacity + TAG_ROWS, :] = tag.astype(BF16)


def count_rows(regions, capacity, got, marks):
    start = jnp.int32(0)
    end = jnp.int32(SLOTS)
    for r in range(regions):
        block = got[r, capacity : capacity + TAG_ROWS, :].astype(F32)
        marks[0, r] = start
        marks[1, r] = end
        start = start + jnp.max(block[0:1, :]).astype(I32)
        end = end - jnp.max(block[1:2, :]).astype(I32)
    marks[0, regions] = start
    marks[1, regions] = end


def is_filled(regions, core, marks, place):
    first = jnp.where(place < marks[0, regions], 1.0, 0.0)
    second = jnp.where(place >= marks[1, regions], 1.0, 0.0)
    return jnp.where(core[0] > 0, second, first)


def bin_rows(regions, capacity, core, marks, own, other, lift, lift_other):
    flag = core[0] > 0
    for r in range(regions):
        place = pl.ds(marks[core[0], r], capacity)
        lift[place, :] = own[r, 0:capacity, :].astype(F32)
        lift_other[place, :] = other[r, 0:capacity, :].astype(F32)
    place = pl.ds(pl.multiple_of(core[0] * capacity, capacity), SLOTS)
    rows = jnp.concatenate(ordered(flag, lift[place, :], lift_other[place, :]), axis=1)
    filled = is_filled(regions, core, marks, iota((SLOTS, 1), 0))
    return jnp.where(filled > 0.5, rows, 0.0).astype(BF16)


def arrival_rows(regions, capacity, core, marks, own, other, out, far, sems, front, back):
    flag = core[0] > 0
    x = own[...].astype(F32)
    y = other[...].astype(F32)
    front[0:SLOTS, :] = jnp.where(flag, y, x)
    front[SLOTS:, :] = jnp.zeros((capacity, x.shape[1]), F32)
    back[0:capacity, :] = jnp.zeros((capacity, x.shape[1]), F32)
    back[capacity:, :] = jnp.where(flag, x, y)
    row = iota((capacity, 1), 0)
    for r in range(regions):
        held = marks[0, r + 1] - marks[0, r]
        rows = jnp.where(row < held, front[pl.ds(marks[0, r], capacity), :], back[pl.ds(marks[1, r], capacity), :])
        out[r] = rows.astype(BF16)
        pltpu.make_async_copy(out.at[r], far.at[r, pl.ds(0, capacity), :], sems.at[r]).start()


def finish_rows(regions, capacity, out, far, sems):
    for r in range(regions):
        pltpu.make_async_copy(out.at[r], far.at[r, pl.ds(0, capacity), :], sems.at[r]).wait()


def ungroup_kernel(regions, capacity, core, marks, own, other, far, out, sems, front, back):
    arrival_rows(regions, capacity, core, marks, own, other, out, far, sems, front, back)
    finish_rows(regions, capacity, out, far, sems)


def ungroup_grad_kernel(regions, capacity, core, marks, own, other, tagged, gain_part, extra, far, out, sems, front, back):
    arrival_rows(regions, capacity, core, marks, own, other, out, far, sems, front, back)
    total = jnp.zeros((KIND_ROWS, own.shape[1]), F32)
    for r in range(regions):
        block = tagged[r, capacity : capacity + TAG_ROWS, :].astype(F32)
        if capacity >= LANES:
            kind = jnp.concatenate([block[0:1], block[8:9]], axis=1)
        else:
            kind = block[0:1, 0:capacity]
        kinds_hot = hot(iota((KIND_ROWS, capacity), 0) == kind.astype(I32) - 1)
        total = total + mm(kinds_hot, out[r])
    place = iota((KIND_ROWS, 1), 0)
    first = gain_part[0:1, :].astype(F32)
    second = gain_part[1:2, :].astype(F32)
    extra[...] = jnp.where(place == KINDS, first, jnp.where(place == KINDS + 1, second, total)).astype(BF16)
    finish_rows(regions, capacity, out, far, sems)


def pair_kernel(regions, own, received, out, gain_part):
    share = out.shape[1]
    for r in range(regions):
        rows = slice(r * share, (r + 1) * share)
        out[r] = (own[rows, :].astype(F32) + received[rows, :].astype(F32)).astype(BF16)
    gain_part[...] = (own[regions * share :, :].astype(F32) + received[regions * share :, :].astype(F32)).astype(BF16)


def share_kernel(regions, capacity, got, extra, packed, out, tail, sems):
    total = got[0].astype(F32)
    for r in range(1, regions):
        total = total + got[r].astype(F32)
    share = total.shape[0]
    tail[0:share, :] = total.astype(BF16)
    tail[share:, :] = extra[...]
    copies = [
        pltpu.make_async_copy(tail, out.at[r, pl.ds(capacity, share + KIND_ROWS), :], sems.at[r]) for r in range(regions)
    ]
    for copy in copies:
        copy.start()
    for copy in copies:
        copy.wait()


def last_kernel(
    regions, capacity, factor, target_ref, far, out_gain, out_embed, out_q, out_k, out_v, out_o, out_feats,
    got, sums, sums_o, feats, sems, out_sems
):
    _, half = feats.shape
    width = 2 * half
    for r in range(regions):
        pltpu.make_async_copy(far.at[r], got.at[r], sems.at[r]).start()
    share = 4 * width // regions
    extra = jnp.zeros((KIND_ROWS, half), F32)
    for r in range(regions):
        pltpu.make_async_copy(far.at[r], got.at[r], sems.at[r]).wait()
        sums[r * share : (r + 1) * share, :] = got[r, capacity : capacity + share, :].astype(F32) * factor
        extra = extra + got[r, capacity + share : capacity + share + KIND_ROWS, :].astype(F32)
    sums_o[:, 0:half] = sums[3 * width : 3 * width + half]
    sums_o[:, half:] = sums[3 * width + half : 4 * width]
    copies = [
        pltpu.make_async_copy(sums.at[pl.ds(k * width, width)], far_out, out_sems.at[k])
        for k, far_out in enumerate((out_q, out_k, out_v))
    ]
    copies.append(pltpu.make_async_copy(sums_o, out_o, out_sems.at[3]))
    for copy in copies:
        copy.start()
    extra = extra * factor
    out_embed[...] = extra[0:KINDS]
    out_gain[:, 0:half] = extra[KINDS : KINDS + 1]
    out_gain[:, half:] = extra[KINDS + 1 : KINDS + 2]
    pick_kernel(target_ref, got, feats)
    copies.append(pltpu.make_async_copy(feats, out_feats, out_sems.at[4]))
    copies[-1].start()
    for copy in copies:
        copy.wait()


def pick_kernel(target_ref, got, out):
    regions = got.shape[0]
    capacity = BINS_DEV * SLOTS // regions
    count, half = out.shape
    target = target_ref[...]
    owner_column = turned(lax.shift_right_logical(target, log2_of(capacity)))
    place_column = turned(jnp.bitwise_and(target, capacity - 1))
    width = min(capacity, LANES)
    lane = iota((1, width), 1).astype(F32)
    step = 256
    for s in range(0, count, step):
        owner = owner_column[s : s + step]
        place = place_column[s : s + step, 0:width]
        chosen = [hot(place - float(k) == lane) for k in range(0, capacity, width)]
        chosen = jnp.concatenate(chosen, axis=1)
        total = jnp.zeros((step, half), F32)
        for r in range(0, regions, 2):
            chunks = jnp.concatenate([got[r, 0:capacity, :], got[r + 1, 0:capacity, :]], axis=1)
            rows = mm(chosen, chunks)
            total = jnp.where(owner == float(r), rows[:, :half], jnp.where(owner == float(r + 1), rows[:, half:], total))
        out[s : s + step, :] = total.astype(BF16)


def ordered(flag, own, other):
    first = jnp.where(flag, other, own)
    second = jnp.where(flag, own, other)
    return first, second


def full_weights(core, own, other):
    flag = core[0] > 0
    half = own.shape[2]
    columns = []
    for k in range(3):
        columns.append(jnp.concatenate(ordered(flag, own[k], other[k]), axis=1))
    top, bottom = ordered(flag, own[3], other[3])
    rows = [jnp.concatenate([part[0:half], part[half:]], axis=1) for part in (top, bottom)]
    return columns + [jnp.concatenate(rows, axis=0)]


def norm_rows(slab, gain, width):
    wide = slab.astype(F32)
    inverse = lax.rsqrt(jnp.sum(wide * wide, axis=1, keepdims=True) / width + EPSILON)
    return wide, inverse, (wide * inverse * gain).astype(BF16)


def stack_rows(rows, extra):
    place = iota((HEAD_PAD - HEAD_DIM, rows.shape[1]), 0)
    tail = jnp.zeros(place.shape, F32)
    for k, value in enumerate(extra):
        tail = jnp.where(place == k, value, tail)
    return jnp.concatenate([rows.astype(F32), tail], axis=0)


def forward_kernel(
    heads, regions, capacity, core, got, got_other, w_own, w_other, gain, slab_out, queries_t, keys_out, values_t, exps_out,
    context_t, inv_t, keep_out, send_out, marks, keys_t, w_out, lift, lift_other
):
    step = pl.program_id(0)
    width = heads * HEAD_DIM
    half = width // 2
    flag = core[0] > 0
    scale = HEAD_DIM**-0.5

    @pl.when(step == 0)
    def _():
        w_q, w_k, w_v, w_o = full_weights(core, w_own, w_other)
        w_out[...] = w_o
        count_rows(regions, capacity, got, marks)
        slab = bin_rows(regions, capacity, core, marks, got, got_other, lift, lift_other)
        slab_out[...] = slab
        _, _, normed = norm_rows(slab, gain[...], width)
        queries_t[...] = jnp.transpose(mm(normed, w_q)).astype(BF16)
        k = mm(normed, w_k)
        keys_out[...] = k.astype(BF16)
        keys_t[...] = jnp.transpose(k).astype(BF16)
        values_t[...] = jnp.transpose(mm(normed, w_v)).astype(BF16)

    bias = jnp.where(is_filled(regions, core, marks, iota((1, SLOTS), 1)) > 0.5, 0.0, MASKED / scale)
    for k in range(PER_STEP):
        h = step * PER_STEP + k
        head_rows = pl.ds(pl.multiple_of(h * HEAD_DIM, HEAD_DIM), HEAD_DIM)
        scaled = queries_t[head_rows, :].astype(F32) * (scale * LOG2E)
        high = scaled.astype(BF16).astype(F32)
        left = jnp.transpose(jnp.concatenate([high, stack_rows(scaled - high, (1.0,))], axis=0)).astype(BF16)
        k_rows = keys_t[head_rows, :].astype(F32)
        scores = mm(left, jnp.concatenate([k_rows, stack_rows(k_rows, (bias,))], axis=0).astype(BF16))
        top = jnp.max(scores, axis=1, keepdims=True)
        exps = jnp.exp2(scores - top).astype(BF16)
        exps_out[k] = exps
        summed = mm_nt(stack_rows(values_t[head_rows, :], (1.0,)).astype(BF16), exps)
        inv = 1.0 / summed[HEAD_DIM : HEAD_DIM + 1]
        context_t[head_rows, :] = summed[0:HEAD_DIM] * inv
        inv_t[pl.ds(h, 1), :] = inv

    @pl.when(step == heads // PER_STEP - 1)
    def _():
        rows_out = mm(jnp.transpose(context_t[...]).astype(BF16), w_out[...]).astype(BF16)
        keep_out[...] = jnp.where(flag, rows_out[:, half:], rows_out[:, :half])
        send_out[...] = jnp.where(flag, rows_out[:, :half], rows_out[:, half:])


def backward_kernel(
    heads, regions, capacity, core, marks, slab_in, got, got_other, w_own, w_other, gain, queries_t, keys_in, values_t, exps_in,
    context_t, inv_t, keep_out, send_out, grad_keep, grad_send, d_context_t, d_query, d_key_t, d_value_t, grad_slab, lift, lift_other
):
    step = pl.program_id(0)
    width = heads * HEAD_DIM
    half = width // 2
    flag = core[0] > 0
    lane = iota((1, width), 1)
    scale = HEAD_DIM**-0.5

    @pl.when(step == 0)
    def _():
        w_o = full_weights(core, w_own, w_other)[3]
        grad_slab[...] = bin_rows(regions, capacity, core, marks, got, got_other, lift, lift_other)
        d_context_t[...] = mm_nt(w_o, grad_slab[...]).astype(BF16)

    for k in range(PER_STEP):
        h = step * PER_STEP + k
        head_rows = pl.ds(pl.multiple_of(h * HEAD_DIM, HEAD_DIM), HEAD_DIM)
        own_lane = lax.shift_right_logical(lane, log2_of(HEAD_DIM)) == h
        scaled = (d_context_t[head_rows, :].astype(F32) * inv_t[pl.ds(h, 1), :]).astype(BF16)
        dot = -jnp.sum(scaled.astype(F32) * context_t[head_rows, :], axis=0, keepdims=True)
        dot_high = dot.astype(BF16).astype(F32)
        left = jnp.transpose(stack_rows(scaled, (dot_high, dot - dot_high))).astype(BF16)
        centred = mm(left, stack_rows(values_t[head_rows, :], (1.0, 1.0)).astype(BF16))
        exps = exps_in[k]
        d_scores = (exps.astype(F32) * centred).astype(BF16)
        dq = mm(d_scores, keys_in[...])
        d_query[...] = jnp.where(own_lane, dq * scale, d_query[...])
        d_key_t[head_rows, :] = mm(queries_t[head_rows, :], d_scores) * scale
        d_value_t[head_rows, :] = mm(scaled, exps)

    @pl.when(step == heads // PER_STEP - 1)
    def _():
        w_q, w_k, w_v, _ = full_weights(core, w_own, w_other)
        slab = slab_in[...]
        wide, inverse, normed = norm_rows(slab, gain[...], width)
        dq = d_query[...].astype(BF16)
        dk = jnp.transpose(d_key_t[...]).astype(BF16)
        dv = jnp.transpose(d_value_t[...]).astype(BF16)
        d_normed = mm_nt(dq, w_q) + mm_nt(dk, w_k) + mm_nt(dv, w_v)
        scaled = gain[...] * d_normed
        along = jnp.sum(scaled * wide, axis=1, keepdims=True)
        d_slab = (inverse * scaled - wide * (inverse * inverse * inverse) * along / width).astype(BF16)
        keep_out[...] = jnp.where(flag, d_slab[:, half:], d_slab[:, :half])
        send_out[...] = jnp.where(flag, d_slab[:, :half], d_slab[:, half:])
        normed_t = jnp.transpose(normed.astype(F32)).astype(BF16)
        place = 0
        for d_rows in (dq, dk, dv):
            grad = mm(normed_t, d_rows)
            grad_keep[place : place + width, :] = jnp.where(flag, grad[:, half:], grad[:, :half]).astype(BF16)
            grad_send[place : place + width, :] = jnp.where(flag, grad[:, :half], grad[:, half:]).astype(BF16)
            place += width
        grad = mm(context_t[...].astype(BF16), grad_slab[...])
        for part in range(2):
            block = grad[:, part * half : (part + 1) * half]
            grad_keep[place : place + half, :] = jnp.where(flag, block[half:], block[:half]).astype(BF16)
            grad_send[place : place + half, :] = jnp.where(flag, block[:half], block[half:]).astype(BF16)
            place += half
        gain_grad = jnp.sum(d_normed * wide * inverse, axis=0, keepdims=True)
        pick = iota((16, half), 0)
        block = jnp.where(pick == 0, gain_grad[:, :half], jnp.where(pick == 1, gain_grad[:, half:], 0.0))
        grad_keep[place : place + 16, :] = block.astype(BF16)
        grad_send[place : place + 16, :] = block.astype(BF16)


def shape(dims, dtype):
    return jax.ShapeDtypeStruct(tuple(dims), dtype)


SMEM_SPEC = pl.BlockSpec(memory_space=pltpu.SMEM)


def whole(array):
    zeros = (0,) * len(array.shape)
    return pl.BlockSpec(tuple(array.shape), lambda *_: zeros)


FAR_SPEC = pl.BlockSpec(memory_space=pl.ANY)


def simple_call(kernel, outs, inputs, scratch=(), scalars=0, far=0, far_outs=0):
    near = inputs[scalars : len(inputs) - far]
    return pl.pallas_call(
        kernel,
        out_shape=outs,
        in_specs=[SMEM_SPEC] * scalars + [whole(x) for x in near] + [FAR_SPEC] * far,
        out_specs=tuple(whole(x) for x in outs[: len(outs) - far_outs]) + (FAR_SPEC,) * far_outs,
        scratch_shapes=scratch,
    )(*inputs)


def on_device(
    features,
    element_kinds,
    bin_cells,
    kind_embed,
    norm_gain,
    w_query,
    w_key,
    w_value,
    w_out,
    cotangent,
):
    regions = lax.axis_size("region")
    cores = lax.axis_size("head")
    local_rows = BINS_DEV * SLOTS
    capacity = local_rows // regions
    count, half = features.shape
    width = w_query.shape[0]
    heads = width // HEAD_DIM
    assert cores == BINS_DEV and half * cores == width and half == LANES
    core = lax.axis_index("head").astype(I32).reshape(1)
    swap = [(i, (i + 1) % cores) for i in range(cores)]

    def other_core(x):
        return lax.ppermute(x, "head", swap)

    def exchange(x):
        return lax.all_to_all(x, "region", split_axis=0, concat_axis=0, tiled=True)

    gain = norm_gain.reshape(1, width)
    kinds_row = element_kinds.reshape(1, count)
    packed_shape = shape((regions, capacity, half), BF16)
    tagged_shape = shape((regions, capacity + TAG_ROWS, half), BF16)
    target, packed_base = simple_call(
        functools.partial(pack_kernel, regions, capacity),
        (shape((1, count), I32), tagged_shape),
        (bin_cells.reshape(1, count), kinds_row, kind_embed, features),
        scratch=(
            pltpu.VMEM((count, half), BF16),
            pltpu.VMEM(tagged_shape.shape, BF16),
            pltpu.SemaphoreType.DMA(()),
            pltpu.SemaphoreType.DMA((regions // 2,)),
        ),
        far=1,
        far_outs=1,
    )
    got_base = exchange(packed_base)
    packed_cot, w_own = simple_call(
        functools.partial(pack_cot_kernel, regions, capacity),
        (tagged_shape, shape((4, width, half), BF16)),
        (target, kinds_row, cotangent, w_query, w_key, w_value, w_out),
    )
    w_other = other_core(w_own)
    got_base, packed_cot = lax.optimization_barrier((got_base, packed_cot))
    got_cot = exchange(packed_cot)
    got_base_other = other_core(got_base)
    rows_shape = shape((SLOTS, half), BF16)
    lift = pltpu.VMEM((SLOTS + capacity, half), F32)

    turned_shape = shape((width, SLOTS), BF16)
    exps_shape = shape((heads, SLOTS, SLOTS), BF16)
    exps_spec = pl.BlockSpec((PER_STEP, SLOTS, SLOTS), lambda h: (h, 0, 0))
    inputs = (core, got_base, got_base_other, w_own, w_other, gain)
    outs = (
        shape((SLOTS, width), BF16),
        turned_shape,
        shape((SLOTS, width), BF16),
        turned_shape,
        exps_shape,
        shape((width, SLOTS), F32),
        shape((heads, SLOTS), F32),
        rows_shape,
        rows_shape,
        shape((2, regions + 1), I32),
    )
    work = heads * SLOTS * SLOTS
    slab, queries_t, keys, values_t, exps, context_t, inv_t, attn_keep, attn_send, marks = pl.pallas_call(
        functools.partial(forward_kernel, heads, regions, capacity),
        grid=(heads // PER_STEP,),
        out_shape=outs,
        in_specs=[SMEM_SPEC] + [whole(x) for x in inputs[1:]],
        out_specs=tuple(exps_spec if x is exps_shape else whole(x) for x in outs[:-1]) + (SMEM_SPEC,),
        scratch_shapes=(pltpu.VMEM((width, SLOTS), BF16), pltpu.VMEM((width, width), BF16), lift, lift),
        cost_estimate=pl.CostEstimate(flops=4 * work * width, transcendentals=work, bytes_accessed=2 * work),
        name="forward",
    )(*inputs)
    attn_other = other_core(attn_send)
    (packed_attn,) = simple_call(
        functools.partial(ungroup_kernel, regions, capacity),
        (packed_shape,),
        (core, marks, attn_keep, attn_other),
        scratch=(pltpu.VMEM(packed_shape.shape, BF16), pltpu.SemaphoreType.DMA((regions,)), lift, lift),
        scalars=2,
        far_outs=1,
    )

    got_cot_other = other_core(got_cot)
    grad_rows = 4 * width + 16
    inputs = (core, marks, slab, got_cot, got_cot_other, w_own, w_other, gain, queries_t, keys, values_t, exps, context_t, inv_t)
    outs = (rows_shape, rows_shape, shape((grad_rows, half), BF16), shape((grad_rows, half), BF16))
    d_keep, d_send, grad_keep, grad_send = pl.pallas_call(
        functools.partial(backward_kernel, heads, regions, capacity),
        grid=(heads // PER_STEP,),
        out_shape=outs,
        in_specs=[SMEM_SPEC] * 2 + [exps_spec if x is exps else whole(x) for x in inputs[2:]],
        out_specs=tuple(whole(x) for x in outs),
        scratch_shapes=(
            pltpu.VMEM((width, SLOTS), BF16),
            pltpu.VMEM((SLOTS, width), F32),
            pltpu.VMEM((width, SLOTS), F32),
            pltpu.VMEM((width, SLOTS), F32),
            pltpu.VMEM((SLOTS, width), BF16),
            lift,
            lift,
        ),
        cost_estimate=pl.CostEstimate(flops=8 * work * width, transcendentals=0, bytes_accessed=2 * work),
        name="backward",
    )(*inputs)

    share = 4 * width // regions
    pairs, gain_part = simple_call(
        functools.partial(pair_kernel, regions),
        (shape((regions, share, half), BF16), shape((16, half), BF16)),
        (grad_keep, other_core(grad_send)),
    )
    payload_shape = shape((regions, capacity + share + KIND_ROWS, half), BF16)
    extra, packed_grad = simple_call(
        functools.partial(ungroup_grad_kernel, regions, capacity),
        (shape((KIND_ROWS, half), BF16), payload_shape),
        (core, marks, d_keep, other_core(d_send), got_cot, gain_part),
        scratch=(pltpu.VMEM(packed_shape.shape, BF16), pltpu.SemaphoreType.DMA((regions,)), lift, lift),
        scalars=2,
        far_outs=1,
    )
    got_cot, packed_attn = lax.optimization_barrier((got_cot, packed_attn))
    home_attn = exchange(packed_attn)
    home_attn, pairs = lax.optimization_barrier((home_attn, pairs))
    shares = exchange(pairs)
    payload = pl.pallas_call(
        functools.partial(share_kernel, regions, capacity),
        out_shape=payload_shape,
        in_specs=[whole(shares), whole(extra), pl.BlockSpec(memory_space=pl.ANY)],
        out_specs=pl.BlockSpec(memory_space=pl.ANY),
        scratch_shapes=(pltpu.VMEM((share + KIND_ROWS, half), BF16), pltpu.SemaphoreType.DMA((regions,))),
        input_output_aliases={2: 0},
        name="share",
    )(shares, extra, packed_grad)
    home_grad = exchange(payload)
    (attended,) = simple_call(pick_kernel, (shape((count, half), BF16),), (target, home_attn))
    column_shape = shape((width, half), F32)
    grad_gain, grad_embed, grad_q, grad_k, grad_v, grad_o, grad_feats = simple_call(
        functools.partial(last_kernel, regions, capacity, float(count * regions) ** (-0.5)),
        (
            shape((1, width), F32),
            shape((KINDS, half), F32),
            column_shape,
            column_shape,
            column_shape,
            shape((half, width), F32),
            shape((count, half), BF16),
        ),
        (target, home_grad),
        scratch=(
            pltpu.VMEM(payload_shape.shape, BF16),
            pltpu.VMEM((4 * width, half), F32),
            pltpu.VMEM((half, width), F32),
            pltpu.VMEM((count, half), BF16),
            pltpu.SemaphoreType.DMA((regions,)),
            pltpu.SemaphoreType.DMA((5,)),
        ),
        far=1,
        far_outs=5,
    )
    return (attended, grad_feats, grad_q, grad_k, grad_v, grad_o, grad_gain.reshape(width), grad_embed)


def solution(mesh):
    placed = (
        P(("groups", "region"), "head"),
        P(("groups", "region")),
        P(("groups", "region")),
        P(None, "head"),
        P(),
        P(None, "head"),
        P(None, "head"),
        P(None, "head"),
        P("head", None),
        P(("groups", "region"), "head"),
    )

    return jax.shard_map(
        on_device,
        mesh=mesh,
        in_specs=placed,
        out_specs=(
            P(("groups", "region"), "head"),
            P(("groups", "region"), "head"),
            P("groups", "head"),
            P("groups", "head"),
            P("groups", "head"),
            P(("groups", "head"), None),
            P("groups"),
            P("groups", "head"),
        ),
        check_vma=False,
    )
```

```python
import functools

import jax
import jax.numpy as jnp
from jax import lax
from jax.experimental import pallas as pl
from jax.experimental.pallas import tpu as pltpu
from jax.sharding import PartitionSpec as P


HEAD_DIM = 32
KINDS = 12
SLOTS = 1024
BINS_DEV = 2
MASKED = -1000000000.0
EPSILON = 1e-06
LOG2E = 1.4426950408889634

F32 = jnp.float32
BF16 = jnp.bfloat16
I32 = jnp.int32
LANES = 128
TAG_ROWS = 16
KIND_ROWS = 16
HEAD_PAD = 48
PER_STEP = 2
CHUNK = 256
ATTENTION_BYTES = 40 << 20
ROWS_BYTES = 16 << 20
NT = (((1,), (1,)), ((), ()))
TN = (((0,), (0,)), ((), ()))


def iota(shape, axis):
    return lax.broadcasted_iota(I32, shape, axis)


def mm(a, b):
    return jnp.dot(a, b, preferred_element_type=F32)


def mm_nt(a, b):
    return lax.dot_general(a, b, NT, preferred_element_type=F32)


def mm_tn(a, b):
    return lax.dot_general(a, b, TN, preferred_element_type=F32)


def hot(condition):
    return jnp.where(condition, 1.0, 0.0).astype(BF16)


def log2_of(n):
    return n.bit_length() - 1


def turned(row):
    return jnp.transpose(jnp.broadcast_to(row.astype(F32), (LANES, row.shape[1])))


def running(group_hot):
    rows, count = group_hot.shape
    blocks = count // LANES
    stacked = jnp.concatenate([group_hot[:, k * LANES : (k + 1) * LANES] for k in range(blocks)], axis=0)
    before = hot(iota((LANES, LANES), 0) < iota((LANES, LANES), 1))
    inside = mm(stacked.astype(BF16), before)
    sums = jnp.sum(stacked, axis=1, keepdims=True)
    offset = jnp.zeros((rows, 1), F32)
    pieces = []
    for k in range(blocks):
        part = slice(k * rows, (k + 1) * rows)
        pieces.append(inside[part] + offset)
        offset = offset + sums[part]
    return jnp.concatenate(pieces, axis=1), offset


def positions(regions, capacity, cell):
    count = cell.shape[1]
    owner = lax.shift_right_logical(cell, log2_of(BINS_DEV * SLOTS))
    group = lax.shift_right_logical(cell, log2_of(SLOTS))
    classes = max(BINS_DEV * regions, 16)
    group_hot = jnp.where(iota((classes, count), 0) == group, 1.0, 0.0)
    before, counts = running(group_hot)
    rank = jnp.sum(before * group_hot, axis=0, keepdims=True).astype(I32)
    second = jnp.bitwise_and(group, 1) > 0
    return owner, jnp.where(second, capacity - 1 - rank, rank), counts


def to_chunks(capacity, place, owner_column, rows, first, many):
    chosen = hot(iota((capacity, place.shape[1]), 0) == place)
    wide = rows.astype(F32)
    masked = [jnp.where(owner_column == float(first + k), wide, 0.0).astype(BF16) for k in range(many)]
    return mm(chosen, jnp.concatenate(masked, axis=1)).astype(BF16)


def pack_kernel(regions, capacity, cells, kinds, feats, embed, out_base, out_target):
    count, half = feats.shape
    owner, place, counts = positions(regions, capacity, cells[...])
    out_target[...] = owner * capacity + place
    kinds_hot = hot(iota((KINDS, count), 0) == kinds[...])
    base = (feats[...].astype(F32) + mm_tn(kinds_hot, embed[...])).astype(BF16)
    owner_column = turned(owner)
    tag_place = iota((TAG_ROWS, half), 0)
    for r in range(0, regions, 2):
        moved = to_chunks(capacity, place, owner_column, base, r, 2)
        for k in range(2):
            out_base[r + k, 0:capacity, :] = moved[:, k * half : (k + 1) * half]
            pair = 2 * (r + k)
            first = counts[pair : pair + 1]
            second = counts[pair + 1 : pair + 2]
            tags = jnp.where(tag_place == 0, first, jnp.where(tag_place == 1, second, 0.0))
            out_base[r + k, capacity : capacity + TAG_ROWS, :] = tags.astype(BF16)


def pack_cot_kernel(regions, capacity, target_ref, kinds, cot, w_q, w_k, w_v, w_o, out_cot, out_w):
    count, half = cot.shape
    out_w[0] = w_q[...]
    out_w[1] = w_k[...]
    out_w[2] = w_v[...]
    out_w[3, 0:half, :] = w_o[:, 0:half]
    out_w[3, half:, :] = w_o[:, half:]
    target = target_ref[...]
    owner = lax.shift_right_logical(target, log2_of(capacity))
    place = jnp.bitwise_and(target, capacity - 1)
    owner_column = turned(owner)
    tags = jnp.where(iota((TAG_ROWS, count), 0) == 0, kinds[...] + 1, 0).astype(F32).astype(BF16)
    for r in range(0, regions, 2):
        moved = to_chunks(capacity, place, owner_column, cot[...], r, 2)
        for k in range(2):
            out_cot[r + k, 0:capacity, :] = moved[:, k * half : (k + 1) * half]
    for r in range(regions):
        chosen = hot(iota((capacity, count), 0) + r * capacity == target)
        tag = mm_nt(tags, chosen)
        if capacity >= LANES:
            tag = jnp.concatenate([tag[0:8, 0:LANES], tag[0:8, LANES : 2 * LANES]], axis=0)
        else:
            tag = jnp.concatenate([tag, jnp.zeros((TAG_ROWS, LANES - capacity), F32)], axis=1)
        out_cot[r, capacity : capacity + TAG_ROWS, :] = tag.astype(BF16)


def count_rows(regions, capacity, got, marks):
    start = jnp.int32(0)
    end = jnp.int32(SLOTS)
    for r in range(regions):
        block = got[r, capacity : capacity + TAG_ROWS, :].astype(F32)
        marks[0, r] = start
        marks[1, r] = end
        start = start + jnp.max(block[0:1, :]).astype(I32)
        end = end - jnp.max(block[1:2, :]).astype(I32)
    marks[0, regions] = start
    marks[1, regions] = end


def is_filled(regions, core, marks, place):
    first = jnp.where(place < marks[0, regions], 1.0, 0.0)
    second = jnp.where(place >= marks[1, regions], 1.0, 0.0)
    return jnp.where(core[0] > 0, second, first)


def lift_rows(regions, capacity, core, marks, own, other, lift, lift_other):
    for r in range(regions):
        place = pl.ds(marks[core[0], r], capacity)
        lift[place, :] = own[r, 0:capacity, :].astype(F32)
        lift_other[place, :] = other[r, 0:capacity, :].astype(F32)


def bin_rows(regions, capacity, core, marks, lift, lift_other, first, many):
    place = pl.ds(pl.multiple_of(core[0] * capacity, capacity) + first, many)
    rows = jnp.concatenate(ordered(core[0] > 0, lift[place, :], lift_other[place, :]), axis=1)
    filled = is_filled(regions, core, marks, iota((many, 1), 0) + first)
    return jnp.where(filled > 0.5, rows, 0.0).astype(BF16)


def arrival_rows(regions, capacity, core, marks, own, other, out, front, back):
    flag = core[0] > 0
    x = own[...].astype(F32)
    y = other[...].astype(F32)
    front[0:SLOTS, :] = jnp.where(flag, y, x)
    front[SLOTS:, :] = jnp.zeros((capacity, x.shape[1]), F32)
    back[0:capacity, :] = jnp.zeros((capacity, x.shape[1]), F32)
    back[capacity:, :] = jnp.where(flag, x, y)
    row = iota((capacity, 1), 0)
    for r in range(regions):
        held = marks[0, r + 1] - marks[0, r]
        rows = jnp.where(row < held, front[pl.ds(marks[0, r], capacity), :], back[pl.ds(marks[1, r], capacity), :])
        out[r, 0:capacity, :] = rows.astype(BF16)


def ungroup_kernel(regions, capacity, core, marks, own, other, out, front, back):
    arrival_rows(regions, capacity, core, marks, own, other, out, front, back)


def ungroup_grad_kernel(regions, capacity, core, marks, own, other, tagged, gain_part, out, extra, front, back):
    arrival_rows(regions, capacity, core, marks, own, other, out, front, back)
    total = jnp.zeros((KIND_ROWS, own.shape[1]), F32)
    for r in range(regions):
        block = tagged[r, capacity : capacity + TAG_ROWS, :].astype(F32)
        if capacity >= LANES:
            kind = jnp.concatenate([block[0:1], block[8:9]], axis=1)
        else:
            kind = block[0:1, 0:capacity]
        kinds_hot = hot(iota((KIND_ROWS, capacity), 0) == kind.astype(I32) - 1)
        total = total + mm(kinds_hot, out[r, 0:capacity, :])
    place = iota((KIND_ROWS, 1), 0)
    first = gain_part[0:1, :].astype(F32)
    second = gain_part[1:2, :].astype(F32)
    extra[...] = jnp.where(place == KINDS, first, jnp.where(place == KINDS + 1, second, total)).astype(BF16)


def share_kernel(regions, capacity, got, extra, packed, out, tail, sems):
    total = got[0].astype(F32)
    for r in range(1, regions):
        total = total + got[r].astype(F32)
    share = total.shape[0]
    tail[0:share, :] = total.astype(BF16)
    tail[share:, :] = extra[...]
    copies = [
        pltpu.make_async_copy(tail, out.at[r, pl.ds(capacity, share + KIND_ROWS), :], sems.at[r]) for r in range(regions)
    ]
    for copy in copies:
        copy.start()
    for copy in copies:
        copy.wait()


def last_kernel(regions, capacity, factor, target_ref, got, out, out_q, out_k, out_v, out_o, out_gain, out_embed, flat):
    pick_kernel(target_ref, got, out)
    width, half = out_q.shape
    share = 4 * width // regions
    extra = jnp.zeros((KIND_ROWS, half), F32)
    for r in range(regions):
        flat[r * share : (r + 1) * share, :] = got[r, capacity : capacity + share, :].astype(F32) * factor
        extra = extra + got[r, capacity + share : capacity + share + KIND_ROWS, :].astype(F32)
    extra = extra * factor
    out_q[...] = flat[0:width]
    out_k[...] = flat[width : 2 * width]
    out_v[...] = flat[2 * width : 3 * width]
    out_o[:, 0:half] = flat[3 * width : 3 * width + half]
    out_o[:, half:] = flat[3 * width + half : 4 * width]
    out_embed[...] = extra[0:KINDS]
    out_gain[:, 0:half] = extra[KINDS : KINDS + 1]
    out_gain[:, half:] = extra[KINDS + 1 : KINDS + 2]


def pick_kernel(target_ref, got, out):
    regions = got.shape[0]
    capacity = BINS_DEV * SLOTS // regions
    count, half = out.shape
    target = target_ref[...]
    owner_column = turned(lax.shift_right_logical(target, log2_of(capacity)))
    place_column = turned(jnp.bitwise_and(target, capacity - 1))
    width = min(capacity, LANES)
    lane = iota((1, width), 1).astype(F32)
    step = 256
    for s in range(0, count, step):
        owner = owner_column[s : s + step]
        place = place_column[s : s + step, 0:width]
        chosen = [hot(place - float(k) == lane) for k in range(0, capacity, width)]
        chosen = jnp.concatenate(chosen, axis=1)
        total = jnp.zeros((step, half), F32)
        for r in range(0, regions, 2):
            chunks = jnp.concatenate([got[r, 0:capacity, :], got[r + 1, 0:capacity, :]], axis=1)
            rows = mm(chosen, chunks)
            total = jnp.where(owner == float(r), rows[:, :half], jnp.where(owner == float(r + 1), rows[:, half:], total))
        out[s : s + step, :] = total.astype(BF16)


def ordered(flag, own, other):
    first = jnp.where(flag, other, own)
    second = jnp.where(flag, own, other)
    return first, second


def full_weights(core, own, other):
    flag = core[0] > 0
    half = own.shape[2]
    columns = []
    for k in range(3):
        columns.append(jnp.concatenate(ordered(flag, own[k], other[k]), axis=1))
    top, bottom = ordered(flag, own[3], other[3])
    rows = [jnp.concatenate([part[0:half], part[half:]], axis=1) for part in (top, bottom)]
    return columns + [jnp.concatenate(rows, axis=0)]


def norm_rows(slab, gain, width):
    wide = slab.astype(F32)
    inverse = lax.rsqrt(jnp.sum(wide * wide, axis=1, keepdims=True) / width + EPSILON)
    return wide, inverse, (wide * inverse * gain).astype(BF16)


def stack_rows(rows, extra):
    place = iota((HEAD_PAD - HEAD_DIM, rows.shape[1]), 0)
    tail = jnp.zeros(place.shape, F32)
    for k, value in enumerate(extra):
        tail = jnp.where(place == k, value, tail)
    return jnp.concatenate([rows.astype(F32), tail], axis=0)


def forward_kernel(
    heads, regions, capacity, core, got, got_other, w_own, w_other, gain, slab_out, queries_t, keys_out, values_t, exps_out,
    context_t, inv_t, keep_out, send_out, marks, keys_t, w_out, lift, lift_other
):
    step = pl.program_id(0)
    width = heads * HEAD_DIM
    half = width // 2
    flag = core[0] > 0
    scale = HEAD_DIM**-0.5

    @pl.when(step == 0)
    def _():
        w_q, w_k, w_v, w_o = full_weights(core, w_own, w_other)
        w_out[...] = w_o
        count_rows(regions, capacity, got, marks)
        lift_rows(regions, capacity, core, marks, got, got_other, lift, lift_other)
        for first in range(0, SLOTS, CHUNK):
            rows = slice(first, first + CHUNK)
            slab = bin_rows(regions, capacity, core, marks, lift, lift_other, first, CHUNK)
            slab_out[rows, :] = slab
            _, _, normed = norm_rows(slab, gain[...], width)
            queries_t[:, rows] = jnp.transpose(mm(normed, w_q)).astype(BF16)
            k = mm(normed, w_k)
            keys_out[rows, :] = k.astype(BF16)
            keys_t[:, rows] = jnp.transpose(k).astype(BF16)
            values_t[:, rows] = jnp.transpose(mm(normed, w_v)).astype(BF16)

    bias = jnp.where(is_filled(regions, core, marks, iota((1, SLOTS), 1)) > 0.5, 0.0, MASKED / scale)
    for k in range(PER_STEP):
        h = step * PER_STEP + k
        head_rows = pl.ds(pl.multiple_of(h * HEAD_DIM, HEAD_DIM), HEAD_DIM)
        scaled = queries_t[head_rows, :].astype(F32) * (scale * LOG2E)
        high = scaled.astype(BF16).astype(F32)
        left = jnp.transpose(jnp.concatenate([high, stack_rows(scaled - high, (1.0,))], axis=0)).astype(BF16)
        k_rows = keys_t[head_rows, :].astype(F32)
        scores = mm(left, jnp.concatenate([k_rows, stack_rows(k_rows, (bias,))], axis=0).astype(BF16))
        top = jnp.max(scores, axis=1, keepdims=True)
        exps = jnp.exp2(scores - top).astype(BF16)
        exps_out[k] = exps
        summed = mm_nt(stack_rows(values_t[head_rows, :], (1.0,)).astype(BF16), exps)
        inv = 1.0 / summed[HEAD_DIM : HEAD_DIM + 1]
        context_t[head_rows, :] = summed[0:HEAD_DIM] * inv
        inv_t[pl.ds(h, 1), :] = inv

    @pl.when(step == heads // PER_STEP - 1)
    def _():
        rows_out = mm(jnp.transpose(context_t[...]).astype(BF16), w_out[...]).astype(BF16)
        keep_out[...] = jnp.where(flag, rows_out[:, half:], rows_out[:, :half])
        send_out[...] = jnp.where(flag, rows_out[:, :half], rows_out[:, half:])


def backward_kernel(
    heads, regions, capacity, core, marks, slab_in, got, got_other, w_own, w_other, gain, queries_t, keys_in, values_t, exps_in,
    context_t, inv_t, keep_out, send_out, grad_keep, grad_send, d_context_t, d_query, d_key_t, d_value_t, grad_slab, lift, lift_other, normed_t, d_low
):
    step = pl.program_id(0)
    width = heads * HEAD_DIM
    half = width // 2
    flag = core[0] > 0
    lane = iota((1, width), 1)
    scale = HEAD_DIM**-0.5

    @pl.when(step == 0)
    def _():
        w_o = full_weights(core, w_own, w_other)[3]
        lift_rows(regions, capacity, core, marks, got, got_other, lift, lift_other)
        for first in range(0, SLOTS, CHUNK):
            rows = slice(first, first + CHUNK)
            part = bin_rows(regions, capacity, core, marks, lift, lift_other, first, CHUNK)
            grad_slab[rows, :] = part
            d_context_t[:, rows] = mm_nt(w_o, part).astype(BF16)

    for k in range(PER_STEP):
        h = step * PER_STEP + k
        head_rows = pl.ds(pl.multiple_of(h * HEAD_DIM, HEAD_DIM), HEAD_DIM)
        own_lane = lax.shift_right_logical(lane, log2_of(HEAD_DIM)) == h
        scaled = (d_context_t[head_rows, :].astype(F32) * inv_t[pl.ds(h, 1), :]).astype(BF16)
        dot = -jnp.sum(scaled.astype(F32) * context_t[head_rows, :], axis=0, keepdims=True)
        dot_high = dot.astype(BF16).astype(F32)
        left = jnp.transpose(stack_rows(scaled, (dot_high, dot - dot_high))).astype(BF16)
        centred = mm(left, stack_rows(values_t[head_rows, :], (1.0, 1.0)).astype(BF16))
        exps = exps_in[k]
        d_scores = (exps.astype(F32) * centred).astype(BF16)
        dq = mm(d_scores, keys_in[...])
        d_query[...] = jnp.where(own_lane, dq * scale, d_query[...])
        d_key_t[head_rows, :] = mm(queries_t[head_rows, :], d_scores) * scale
        d_value_t[head_rows, :] = mm(scaled, exps)

    @pl.when(step == heads // PER_STEP - 1)
    def _():
        w_q, w_k, w_v, _ = full_weights(core, w_own, w_other)
        gain_grad = jnp.zeros((1, width), F32)
        for first in range(0, SLOTS, CHUNK):
            rows = slice(first, first + CHUNK)
            wide, inverse, normed = norm_rows(slab_in[rows, :], gain[...], width)
            dq = d_query[rows, :].astype(BF16)
            dk = jnp.transpose(d_key_t[:, rows]).astype(BF16)
            dv = jnp.transpose(d_value_t[:, rows]).astype(BF16)
            d_normed = mm_nt(dq, w_q) + mm_nt(dk, w_k) + mm_nt(dv, w_v)
            scaled = gain[...] * d_normed
            along = jnp.sum(scaled * wide, axis=1, keepdims=True)
            d_slab = (inverse * scaled - wide * (inverse * inverse * inverse) * along / width).astype(BF16)
            keep_out[rows, :] = jnp.where(flag, d_slab[:, half:], d_slab[:, :half])
            send_out[rows, :] = jnp.where(flag, d_slab[:, :half], d_slab[:, half:])
            gain_grad = gain_grad + jnp.sum(d_normed * wide * inverse, axis=0, keepdims=True)
            normed_t[:, rows] = jnp.transpose(normed.astype(F32)).astype(BF16)
            d_low[0, rows, :] = dq
            d_low[1, rows, :] = dk
            d_low[2, rows, :] = dv
        place = 0
        for k in range(3):
            grad = mm(normed_t[...], d_low[k])
            grad_keep[place : place + width, :] = jnp.where(flag, grad[:, half:], grad[:, :half]).astype(BF16)
            grad_send[place : place + width, :] = jnp.where(flag, grad[:, :half], grad[:, half:]).astype(BF16)
            place += width
        grad = mm(context_t[...].astype(BF16), grad_slab[...])
        for part in range(2):
            block = grad[:, part * half : (part + 1) * half]
            grad_keep[place : place + half, :] = jnp.where(flag, block[half:], block[:half]).astype(BF16)
            grad_send[place : place + half, :] = jnp.where(flag, block[:half], block[half:]).astype(BF16)
            place += half
        pick = iota((16, half), 0)
        block = jnp.where(pick == 0, gain_grad[:, :half], jnp.where(pick == 1, gain_grad[:, half:], 0.0))
        grad_keep[place : place + 16, :] = block.astype(BF16)
        grad_send[place : place + 16, :] = block.astype(BF16)


def shape(dims, dtype):
    return jax.ShapeDtypeStruct(tuple(dims), dtype)


SMEM_SPEC = pl.BlockSpec(memory_space=pltpu.SMEM)


def whole(array):
    zeros = (0,) * len(array.shape)
    return pl.BlockSpec(tuple(array.shape), lambda *_: zeros)


def simple_call(kernel, outs, inputs, scratch=(), scalars=0, scalar_outs=0):
    specs = [SMEM_SPEC] * scalars + [whole(x) for x in inputs[scalars:]]
    return pl.pallas_call(
        kernel,
        out_shape=outs,
        in_specs=specs,
        out_specs=tuple(whole(x) for x in outs[: len(outs) - scalar_outs]) + (SMEM_SPEC,) * scalar_outs,
        scratch_shapes=scratch,
        compiler_params=pltpu.CompilerParams(vmem_limit_bytes=ROWS_BYTES),
    )(*inputs)


def on_device(
    features,
    element_kinds,
    bin_cells,
    kind_embed,
    norm_gain,
    w_query,
    w_key,
    w_value,
    w_out,
    cotangent,
):
    regions = lax.axis_size("region")
    cores = lax.axis_size("head")
    local_rows = BINS_DEV * SLOTS
    capacity = local_rows // regions
    count, half = features.shape
    width = w_query.shape[0]
    heads = width // HEAD_DIM
    assert cores == BINS_DEV and half * cores == width and half == LANES
    core = lax.axis_index("head").astype(I32).reshape(1)
    swap = [(i, (i + 1) % cores) for i in range(cores)]

    def other_core(x):
        return lax.ppermute(x, "head", swap)

    def exchange(x):
        return lax.all_to_all(x, "region", split_axis=0, concat_axis=0, tiled=True)

    gain = norm_gain.reshape(1, width)
    kinds_row = element_kinds.reshape(1, count)
    packed_shape = shape((regions, capacity, half), BF16)
    tagged_shape = shape((regions, capacity + TAG_ROWS, half), BF16)
    packed_base, target = simple_call(
        functools.partial(pack_kernel, regions, capacity),
        (tagged_shape, shape((1, count), I32)),
        (bin_cells.reshape(1, count), kinds_row, features, kind_embed),
    )
    got_base = exchange(packed_base)
    packed_cot, w_own = simple_call(
        functools.partial(pack_cot_kernel, regions, capacity),
        (tagged_shape, shape((4, width, half), BF16)),
        (target, kinds_row, cotangent, w_query, w_key, w_value, w_out),
    )
    w_other = other_core(w_own)
    got_base, packed_cot = lax.optimization_barrier((got_base, packed_cot))
    got_cot = exchange(packed_cot)
    got_base_other = other_core(got_base)
    rows_shape = shape((SLOTS, half), BF16)
    lift = pltpu.VMEM((SLOTS + capacity, half), F32)

    turned_shape = shape((width, SLOTS), BF16)
    exps_shape = shape((heads, SLOTS, SLOTS), BF16)
    exps_spec = pl.BlockSpec((PER_STEP, SLOTS, SLOTS), lambda h: (h, 0, 0))
    inputs = (core, got_base, got_base_other, w_own, w_other, gain)
    outs = (
        shape((SLOTS, width), BF16),
        turned_shape,
        shape((SLOTS, width), BF16),
        turned_shape,
        exps_shape,
        shape((width, SLOTS), F32),
        shape((heads, SLOTS), F32),
        rows_shape,
        rows_shape,
        shape((2, regions + 1), I32),
    )
    work = heads * SLOTS * SLOTS
    slab, queries_t, keys, values_t, exps, context_t, inv_t, attn_keep, attn_send, marks = pl.pallas_call(
        functools.partial(forward_kernel, heads, regions, capacity),
        grid=(heads // PER_STEP,),
        out_shape=outs,
        in_specs=[SMEM_SPEC] + [whole(x) for x in inputs[1:]],
        out_specs=tuple(exps_spec if x is exps_shape else whole(x) for x in outs[:-1]) + (SMEM_SPEC,),
        scratch_shapes=(pltpu.VMEM((width, SLOTS), BF16), pltpu.VMEM((width, width), BF16), lift, lift),
        compiler_params=pltpu.CompilerParams(vmem_limit_bytes=ATTENTION_BYTES),
        cost_estimate=pl.CostEstimate(flops=4 * work * width, transcendentals=work, bytes_accessed=2 * work),
        name="forward",
    )(*inputs)
    attn_other = other_core(attn_send)
    (packed_attn,) = simple_call(
        functools.partial(ungroup_kernel, regions, capacity),
        (packed_shape,),
        (core, marks, attn_keep, attn_other),
        scratch=(lift, lift),
        scalars=2,
    )

    got_cot_other = other_core(got_cot)
    grad_rows = 4 * width + 16
    inputs = (core, marks, slab, got_cot, got_cot_other, w_own, w_other, gain, queries_t, keys, values_t, exps, context_t, inv_t)
    outs = (rows_shape, rows_shape, shape((grad_rows, half), BF16), shape((grad_rows, half), BF16))
    d_keep, d_send, grad_keep, grad_send = pl.pallas_call(
        functools.partial(backward_kernel, heads, regions, capacity),
        grid=(heads // PER_STEP,),
        out_shape=outs,
        in_specs=[SMEM_SPEC] * 2 + [exps_spec if x is exps else whole(x) for x in inputs[2:]],
        out_specs=tuple(whole(x) for x in outs),
        scratch_shapes=(
            pltpu.VMEM((width, SLOTS), BF16),
            pltpu.VMEM((SLOTS, width), F32),
            pltpu.VMEM((width, SLOTS), F32),
            pltpu.VMEM((width, SLOTS), F32),
            pltpu.VMEM((SLOTS, width), BF16),
            lift,
            lift,
            pltpu.VMEM((width, SLOTS), BF16),
            pltpu.VMEM((3, SLOTS, width), BF16),
        ),
        compiler_params=pltpu.CompilerParams(vmem_limit_bytes=ATTENTION_BYTES),
        cost_estimate=pl.CostEstimate(flops=8 * work * width, transcendentals=0, bytes_accessed=2 * work),
        name="backward",
    )(*inputs)

    share = 4 * width // regions
    grad_other = other_core(grad_send)
    pairs = (grad_keep[: 4 * width].astype(F32) + grad_other[: 4 * width].astype(F32)).astype(BF16)
    pairs = pairs.reshape(regions, share, half)
    gain_part = (grad_keep[4 * width :].astype(F32) + grad_other[4 * width :].astype(F32)).astype(BF16)
    payload_shape = shape((regions, capacity + share + KIND_ROWS, half), BF16)
    packed_grad, extra = simple_call(
        functools.partial(ungroup_grad_kernel, regions, capacity),
        (payload_shape, shape((KIND_ROWS, half), BF16)),
        (core, marks, d_keep, other_core(d_send), got_cot, gain_part),
        scratch=(lift, lift),
        scalars=2,
    )
    got_cot, packed_attn = lax.optimization_barrier((got_cot, packed_attn))
    home_attn = exchange(packed_attn)
    home_attn, pairs = lax.optimization_barrier((home_attn, pairs))
    shares = exchange(pairs)
    payload = pl.pallas_call(
        functools.partial(share_kernel, regions, capacity),
        out_shape=payload_shape,
        in_specs=[whole(shares), whole(extra), pl.BlockSpec(memory_space=pl.ANY)],
        out_specs=pl.BlockSpec(memory_space=pl.ANY),
        scratch_shapes=(pltpu.VMEM((share + KIND_ROWS, half), BF16), pltpu.SemaphoreType.DMA((regions,))),
        input_output_aliases={2: 0},
        compiler_params=pltpu.CompilerParams(vmem_limit_bytes=ROWS_BYTES),
        name="share",
    )(shares, extra, packed_grad)
    home_grad = exchange(payload)
    (attended,) = simple_call(pick_kernel, (shape((count, half), BF16),), (target, home_attn))
    column_shape = shape((width, half), F32)
    grad_feats, grad_q, grad_k, grad_v, grad_o, grad_gain, grad_embed = simple_call(
        functools.partial(last_kernel, regions, capacity, float(count * regions) ** (-0.5)),
        (
            shape((count, half), BF16),
            column_shape,
            column_shape,
            column_shape,
            shape((half, width), F32),
            shape((1, width), F32),
            shape((KINDS, half), F32),
        ),
        (target, home_grad),
        scratch=(pltpu.VMEM((4 * width, half), F32),),
    )
    return (attended, grad_feats, grad_q, grad_k, grad_v, grad_o, grad_gain.reshape(width), grad_embed)


def solution(mesh):
    placed = (
        P(("groups", "region"), "head"),
        P(("groups", "region")),
        P(("groups", "region")),
        P(None, "head"),
        P(),
        P(None, "head"),
        P(None, "head"),
        P(None, "head"),
        P("head", None),
        P(("groups", "region"), "head"),
    )

    return jax.shard_map(
        on_device,
        mesh=mesh,
        in_specs=placed,
        out_specs=(
            P(("groups", "region"), "head"),
            P(("groups", "region"), "head"),
            P("groups", "head"),
            P("groups", "head"),
            P("groups", "head"),
            P(("groups", "head"), None),
            P("groups"),
            P("groups", "head"),
        ),
        check_vma=False,
    )
```

```python
import functools

import jax
import jax.numpy as jnp
from jax import lax
from jax.experimental import pallas as pl
from jax.experimental.pallas import tpu as pltpu
from jax.sharding import PartitionSpec as P


HEAD_DIM = 32
KINDS = 12
SLOTS = 1024
BINS_DEV = 2
MASKED = -1000000000.0
EPSILON = 1e-06
LOG2E = 1.4426950408889634

F32 = jnp.float32
BF16 = jnp.bfloat16
I32 = jnp.int32
LANES = 128
TAG_ROWS = 16
KIND_ROWS = 16
HEAD_PAD = 48
PER_STEP = 2
CHUNK = 256
ATTENTION_BYTES = 40 << 20
ROWS_BYTES = 16 << 20
NT = (((1,), (1,)), ((), ()))
TN = (((0,), (0,)), ((), ()))


def iota(shape, axis):
    return lax.broadcasted_iota(I32, shape, axis)


def mm(a, b):
    return jnp.dot(a, b, preferred_element_type=F32)


def mm_nt(a, b):
    return lax.dot_general(a, b, NT, preferred_element_type=F32)


def mm_tn(a, b):
    return lax.dot_general(a, b, TN, preferred_element_type=F32)


def hot(condition):
    return jnp.where(condition, 1.0, 0.0).astype(BF16)


def log2_of(n):
    return n.bit_length() - 1


def turned(row):
    return jnp.transpose(jnp.broadcast_to(row.astype(F32), (LANES, row.shape[1])))


def running(group_hot):
    rows, count = group_hot.shape
    blocks = count // LANES
    stacked = jnp.concatenate([group_hot[:, k * LANES : (k + 1) * LANES] for k in range(blocks)], axis=0)
    before = hot(iota((LANES, LANES), 0) < iota((LANES, LANES), 1))
    inside = mm(stacked.astype(BF16), before)
    sums = jnp.sum(stacked, axis=1, keepdims=True)
    offset = jnp.zeros((rows, 1), F32)
    pieces = []
    for k in range(blocks):
        part = slice(k * rows, (k + 1) * rows)
        pieces.append(inside[part] + offset)
        offset = offset + sums[part]
    return jnp.concatenate(pieces, axis=1), offset


def positions(regions, capacity, cell):
    count = cell.shape[1]
    owner = lax.shift_right_logical(cell, log2_of(BINS_DEV * SLOTS))
    group = lax.shift_right_logical(cell, log2_of(SLOTS))
    classes = max(BINS_DEV * regions, 16)
    group_hot = jnp.where(iota((classes, count), 0) == group, 1.0, 0.0)
    before, counts = running(group_hot)
    rank = jnp.sum(before * group_hot, axis=0, keepdims=True).astype(I32)
    second = jnp.bitwise_and(group, 1) > 0
    return owner, jnp.where(second, capacity - 1 - rank, rank), counts


def to_chunks(capacity, place, owner_column, rows, first, many):
    chosen = hot(iota((capacity, place.shape[1]), 0) == place)
    wide = rows.astype(F32)
    masked = [jnp.where(owner_column == float(first + k), wide, 0.0).astype(BF16) for k in range(many)]
    return mm(chosen, jnp.concatenate(masked, axis=1)).astype(BF16)


def pack_kernel(regions, capacity, cells, kinds, feats, embed, out_base, out_target):
    count, half = feats.shape
    owner, place, counts = positions(regions, capacity, cells[...])
    out_target[...] = owner * capacity + place
    kinds_hot = hot(iota((KINDS, count), 0) == kinds[...])
    base = (feats[...].astype(F32) + mm_tn(kinds_hot, embed[...])).astype(BF16)
    owner_column = turned(owner)
    tag_place = iota((TAG_ROWS, half), 0)
    for r in range(0, regions, 2):
        moved = to_chunks(capacity, place, owner_column, base, r, 2)
        for k in range(2):
            out_base[r + k, 0:capacity, :] = moved[:, k * half : (k + 1) * half]
            pair = 2 * (r + k)
            first = counts[pair : pair + 1]
            second = counts[pair + 1 : pair + 2]
            tags = jnp.where(tag_place == 0, first, jnp.where(tag_place == 1, second, 0.0))
            out_base[r + k, capacity : capacity + TAG_ROWS, :] = tags.astype(BF16)


def pack_cot_kernel(regions, capacity, target_ref, kinds, cot, gain, w_q, w_k, w_v, w_o, out_cot, out_w, out_gain):
    count, half = cot.shape
    out_gain[...] = gain[...]
    out_w[0] = w_q[...]
    out_w[1] = w_k[...]
    out_w[2] = w_v[...]
    out_w[3, 0:half, :] = w_o[:, 0:half]
    out_w[3, half:, :] = w_o[:, half:]
    target = target_ref[...]
    owner = lax.shift_right_logical(target, log2_of(capacity))
    place = jnp.bitwise_and(target, capacity - 1)
    owner_column = turned(owner)
    tags = jnp.where(iota((TAG_ROWS, count), 0) == 0, kinds[...] + 1, 0).astype(F32).astype(BF16)
    for r in range(0, regions, 2):
        moved = to_chunks(capacity, place, owner_column, cot[...], r, 2)
        for k in range(2):
            out_cot[r + k, 0:capacity, :] = moved[:, k * half : (k + 1) * half]
    for r in range(regions):
        chosen = hot(iota((capacity, count), 0) + r * capacity == target)
        tag = mm_nt(tags, chosen)
        if capacity >= LANES:
            tag = jnp.concatenate([tag[0:8, 0:LANES], tag[0:8, LANES : 2 * LANES]], axis=0)
        else:
            tag = jnp.concatenate([tag, jnp.zeros((TAG_ROWS, LANES - capacity), F32)], axis=1)
        out_cot[r, capacity : capacity + TAG_ROWS, :] = tag.astype(BF16)


def count_rows(regions, capacity, got, marks):
    start = jnp.int32(0)
    end = jnp.int32(SLOTS)
    for r in range(regions):
        block = got[r, capacity : capacity + TAG_ROWS, :].astype(F32)
        marks[0, r] = start
        marks[1, r] = end
        start = start + jnp.max(block[0:1, :]).astype(I32)
        end = end - jnp.max(block[1:2, :]).astype(I32)
    marks[0, regions] = start
    marks[1, regions] = end


def is_filled(regions, core, marks, place):
    first = jnp.where(place < marks[0, regions], 1.0, 0.0)
    second = jnp.where(place >= marks[1, regions], 1.0, 0.0)
    return jnp.where(core[0] > 0, second, first)


def lift_rows(regions, capacity, core, marks, own, other, lift, lift_other):
    for r in range(regions):
        place = pl.ds(marks[core[0], r], capacity)
        lift[place, :] = own[r, 0:capacity, :].astype(F32)
        lift_other[place, :] = other[r, 0:capacity, :].astype(F32)


def bin_rows(regions, capacity, core, marks, lift, lift_other, first, many):
    place = pl.ds(pl.multiple_of(core[0] * capacity, capacity) + first, many)
    rows = jnp.concatenate(ordered(core[0] > 0, lift[place, :], lift_other[place, :]), axis=1)
    filled = is_filled(regions, core, marks, iota((many, 1), 0) + first)
    return jnp.where(filled > 0.5, rows, 0.0).astype(BF16)


def arrival_rows(regions, capacity, core, marks, own, other, out, front, back):
    flag = core[0] > 0
    x = own[...].astype(F32)
    y = other[...].astype(F32)
    front[0:SLOTS, :] = jnp.where(flag, y, x)
    front[SLOTS:, :] = jnp.zeros((capacity, x.shape[1]), F32)
    back[0:capacity, :] = jnp.zeros((capacity, x.shape[1]), F32)
    back[capacity:, :] = jnp.where(flag, x, y)
    row = iota((capacity, 1), 0)
    for r in range(regions):
        held = marks[0, r + 1] - marks[0, r]
        rows = jnp.where(row < held, front[pl.ds(marks[0, r], capacity), :], back[pl.ds(marks[1, r], capacity), :])
        out[r, 0:capacity, :] = rows.astype(BF16)


def ungroup_kernel(regions, capacity, core, marks, own, other, out, front, back):
    arrival_rows(regions, capacity, core, marks, own, other, out, front, back)


def ungroup_grad_kernel(regions, capacity, core, marks, own, other, tagged, gain_part, out, extra, front, back):
    arrival_rows(regions, capacity, core, marks, own, other, out, front, back)
    total = jnp.zeros((KIND_ROWS, own.shape[1]), F32)
    for r in range(regions):
        block = tagged[r, capacity : capacity + TAG_ROWS, :].astype(F32)
        if capacity >= LANES:
            kind = jnp.concatenate([block[0:1], block[8:9]], axis=1)
        else:
            kind = block[0:1, 0:capacity]
        kinds_hot = hot(iota((KIND_ROWS, capacity), 0) == kind.astype(I32) - 1)
        total = total + mm(kinds_hot, out[r, 0:capacity, :])
    place = iota((KIND_ROWS, 1), 0)
    first = gain_part[0:1, :].astype(F32)
    second = gain_part[1:2, :].astype(F32)
    extra[...] = jnp.where(place == KINDS, first, jnp.where(place == KINDS + 1, second, total)).astype(BF16)


def share_kernel(regions, capacity, got, extra, packed, out, tail, sems):
    total = got[0].astype(F32)
    for r in range(1, regions):
        total = total + got[r].astype(F32)
    share = total.shape[0]
    tail[0:share, :] = total.astype(BF16)
    tail[share:, :] = extra[...]
    copies = [
        pltpu.make_async_copy(tail, out.at[r, pl.ds(capacity, share + KIND_ROWS), :], sems.at[r]) for r in range(regions)
    ]
    for copy in copies:
        copy.start()
    for copy in copies:
        copy.wait()


def last_kernel(regions, capacity, factor, target_ref, got, out, out_q, out_k, out_v, out_o, out_gain, out_embed, flat):
    pick_kernel(target_ref, got, out)
    width, half = out_q.shape
    share = 4 * width // regions
    extra = jnp.zeros((KIND_ROWS, half), F32)
    for r in range(regions):
        flat[r * share : (r + 1) * share, :] = got[r, capacity : capacity + share, :].astype(F32) * factor
        extra = extra + got[r, capacity + share : capacity + share + KIND_ROWS, :].astype(F32)
    extra = extra * factor
    out_q[...] = flat[0:width]
    out_k[...] = flat[width : 2 * width]
    out_v[...] = flat[2 * width : 3 * width]
    out_o[:, 0:half] = flat[3 * width : 3 * width + half]
    out_o[:, half:] = flat[3 * width + half : 4 * width]
    out_embed[...] = extra[0:KINDS]
    out_gain[:, 0:half] = extra[KINDS : KINDS + 1]
    out_gain[:, half:] = extra[KINDS + 1 : KINDS + 2]


def pick_kernel(target_ref, got, out):
    regions = got.shape[0]
    capacity = BINS_DEV * SLOTS // regions
    count, half = out.shape
    target = target_ref[...]
    owner_column = turned(lax.shift_right_logical(target, log2_of(capacity)))
    place_column = turned(jnp.bitwise_and(target, capacity - 1))
    width = min(capacity, LANES)
    lane = iota((1, width), 1).astype(F32)
    step = 256
    for s in range(0, count, step):
        owner = owner_column[s : s + step]
        place = place_column[s : s + step, 0:width]
        chosen = [hot(place - float(k) == lane) for k in range(0, capacity, width)]
        chosen = jnp.concatenate(chosen, axis=1)
        total = jnp.zeros((step, half), F32)
        for r in range(0, regions, 2):
            chunks = jnp.concatenate([got[r, 0:capacity, :], got[r + 1, 0:capacity, :]], axis=1)
            rows = mm(chosen, chunks)
            total = jnp.where(owner == float(r), rows[:, :half], jnp.where(owner == float(r + 1), rows[:, half:], total))
        out[s : s + step, :] = total.astype(BF16)


def ordered(flag, own, other):
    first = jnp.where(flag, other, own)
    second = jnp.where(flag, own, other)
    return first, second


def full_weights(core, own, other):
    flag = core[0] > 0
    half = own.shape[2]
    columns = []
    for k in range(3):
        columns.append(jnp.concatenate(ordered(flag, own[k], other[k]), axis=1))
    top, bottom = ordered(flag, own[3], other[3])
    rows = [jnp.concatenate([part[0:half], part[half:]], axis=1) for part in (top, bottom)]
    return columns + [jnp.concatenate(rows, axis=0)]


def norm_rows(slab, gain, width):
    wide = slab.astype(F32)
    inverse = lax.rsqrt(jnp.sum(wide * wide, axis=1, keepdims=True) / width + EPSILON)
    return wide, inverse, (wide * inverse * gain).astype(BF16)


def stack_rows(rows, extra):
    place = iota((HEAD_PAD - HEAD_DIM, rows.shape[1]), 0)
    tail = jnp.zeros(place.shape, F32)
    for k, value in enumerate(extra):
        tail = jnp.where(place == k, value, tail)
    return jnp.concatenate([rows.astype(F32), tail], axis=0)


def held_places(heads, low, wide):
    width = heads * HEAD_DIM
    return (
        low.at[pl.ds(2 * width, SLOTS), pl.ds(0, width)],
        low.at[pl.ds(0, width), :],
        low.at[pl.ds(2 * width, SLOTS), pl.ds(width, width)],
        low.at[pl.ds(width, width), :],
        wide.at[pl.ds(0, width), :],
        wide.at[pl.ds(width, heads), :],
    )


def forward_kernel(
    heads, regions, capacity, core, got, got_other, w_own, w_other, gain, low_far, exps_out, wide_far,
    keep_out, send_out, marks, keys_t, w_out, lift, lift_other, slab_out, queries_t, keys_out, values_t,
    context_t, inv_t, sems
):
    step = pl.program_id(0)
    places = held_places(heads, low_far, wide_far)
    early = [
        pltpu.make_async_copy(near, far, sems.at[k])
        for k, (near, far) in enumerate(zip((slab_out, queries_t, keys_out, values_t), places[:4]))
    ]
    late = [
        pltpu.make_async_copy(near, far, sems.at[4 + k])
        for k, (near, far) in enumerate(zip((context_t, inv_t), places[4:]))
    ]
    width = heads * HEAD_DIM
    half = width // 2
    flag = core[0] > 0
    scale = HEAD_DIM**-0.5

    @pl.when(step == 0)
    def _():
        w_q, w_k, w_v, w_o = full_weights(core, w_own, w_other)
        w_out[...] = w_o
        count_rows(regions, capacity, got, marks)
        lift_rows(regions, capacity, core, marks, got, got_other, lift, lift_other)
        for first in range(0, SLOTS, CHUNK):
            rows = slice(first, first + CHUNK)
            slab = bin_rows(regions, capacity, core, marks, lift, lift_other, first, CHUNK)
            slab_out[rows, :] = slab
            _, _, normed = norm_rows(slab, gain[...], width)
            queries_t[:, rows] = jnp.transpose(mm(normed, w_q)).astype(BF16)
            k = mm(normed, w_k)
            keys_out[rows, :] = k.astype(BF16)
            keys_t[:, rows] = jnp.transpose(k).astype(BF16)
            values_t[:, rows] = jnp.transpose(mm(normed, w_v)).astype(BF16)
        for copy in early:
            copy.start()

    bias = jnp.where(is_filled(regions, core, marks, iota((1, SLOTS), 1)) > 0.5, 0.0, MASKED / scale)
    for k in range(PER_STEP):
        h = step * PER_STEP + k
        head_rows = pl.ds(pl.multiple_of(h * HEAD_DIM, HEAD_DIM), HEAD_DIM)
        scaled = queries_t[head_rows, :].astype(F32) * (scale * LOG2E)
        high = scaled.astype(BF16).astype(F32)
        left = jnp.transpose(jnp.concatenate([high, stack_rows(scaled - high, (1.0,))], axis=0)).astype(BF16)
        k_rows = keys_t[head_rows, :].astype(F32)
        scores = mm(left, jnp.concatenate([k_rows, stack_rows(k_rows, (bias,))], axis=0).astype(BF16))
        top = jnp.max(scores, axis=1, keepdims=True)
        exps = jnp.exp2(scores - top).astype(BF16)
        exps_out[k] = exps
        summed = mm_nt(stack_rows(values_t[head_rows, :], (1.0,)).astype(BF16), exps)
        inv = 1.0 / summed[HEAD_DIM : HEAD_DIM + 1]
        context_t[head_rows, :] = summed[0:HEAD_DIM] * inv
        inv_t[pl.ds(h, 1), :] = inv

    @pl.when(step == heads // PER_STEP - 1)
    def _():
        for copy in late:
            copy.start()
        rows_out = mm(jnp.transpose(context_t[...]).astype(BF16), w_out[...]).astype(BF16)
        keep_out[...] = jnp.where(flag, rows_out[:, half:], rows_out[:, :half])
        send_out[...] = jnp.where(flag, rows_out[:, :half], rows_out[:, half:])
        for copy in early + late:
            copy.wait()


def backward_kernel(
    heads, regions, capacity, core, marks, got, got_other, w_own, w_other, gain, low_far,
    exps_in, wide_far, keep_out, send_out, grad_keep, grad_send, d_context_t, d_query, d_key_t, d_value_t, grad_slab, lift, lift_other, normed_t, d_low,
    slab_in, queries_t, keys_in, values_t, context_t, inv_t, sems
):
    step = pl.program_id(0)
    places = held_places(heads, low_far, wide_far)
    early = [
        pltpu.make_async_copy(far, near, sems.at[k])
        for k, (far, near) in enumerate(zip(places, (slab_in, queries_t, keys_in, values_t, context_t, inv_t)))
    ]
    width = heads * HEAD_DIM
    half = width // 2
    flag = core[0] > 0
    lane = iota((1, width), 1)
    scale = HEAD_DIM**-0.5

    @pl.when(step == 0)
    def _():
        for copy in early:
            copy.start()
        w_o = full_weights(core, w_own, w_other)[3]
        lift_rows(regions, capacity, core, marks, got, got_other, lift, lift_other)
        for first in range(0, SLOTS, CHUNK):
            rows = slice(first, first + CHUNK)
            part = bin_rows(regions, capacity, core, marks, lift, lift_other, first, CHUNK)
            grad_slab[rows, :] = part
            d_context_t[:, rows] = mm_nt(w_o, part).astype(BF16)
        for copy in early:
            copy.wait()

    for k in range(PER_STEP):
        h = step * PER_STEP + k
        head_rows = pl.ds(pl.multiple_of(h * HEAD_DIM, HEAD_DIM), HEAD_DIM)
        own_lane = lax.shift_right_logical(lane, log2_of(HEAD_DIM)) == h
        scaled = (d_context_t[head_rows, :].astype(F32) * inv_t[pl.ds(h, 1), :]).astype(BF16)
        dot = -jnp.sum(scaled.astype(F32) * context_t[head_rows, :], axis=0, keepdims=True)
        dot_high = dot.astype(BF16).astype(F32)
        left = jnp.transpose(stack_rows(scaled, (dot_high, dot - dot_high))).astype(BF16)
        centred = mm(left, stack_rows(values_t[head_rows, :], (1.0, 1.0)).astype(BF16))
        exps = exps_in[k]
        d_scores = (exps.astype(F32) * centred).astype(BF16)
        dq = mm(d_scores, keys_in[...])
        d_query[...] = jnp.where(own_lane, dq * scale, d_query[...])
        d_key_t[head_rows, :] = mm(queries_t[head_rows, :], d_scores) * scale
        d_value_t[head_rows, :] = mm(scaled, exps)

    @pl.when(step == heads // PER_STEP - 1)
    def _():
        w_q, w_k, w_v, _ = full_weights(core, w_own, w_other)
        gain_grad = jnp.zeros((1, width), F32)
        for first in range(0, SLOTS, CHUNK):
            rows = slice(first, first + CHUNK)
            wide, inverse, normed = norm_rows(slab_in[rows, :], gain[...], width)
            dq = d_query[rows, :].astype(BF16)
            dk = jnp.transpose(d_key_t[:, rows]).astype(BF16)
            dv = jnp.transpose(d_value_t[:, rows]).astype(BF16)
            d_normed = mm_nt(dq, w_q) + mm_nt(dk, w_k) + mm_nt(dv, w_v)
            scaled = gain[...] * d_normed
            along = jnp.sum(scaled * wide, axis=1, keepdims=True)
            d_slab = (inverse * scaled - wide * (inverse * inverse * inverse) * along / width).astype(BF16)
            keep_out[rows, :] = jnp.where(flag, d_slab[:, half:], d_slab[:, :half])
            send_out[rows, :] = jnp.where(flag, d_slab[:, :half], d_slab[:, half:])
            gain_grad = gain_grad + jnp.sum(d_normed * wide * inverse, axis=0, keepdims=True)
            normed_t[:, rows] = jnp.transpose(normed.astype(F32)).astype(BF16)
            d_low[0, rows, :] = dq
            d_low[1, rows, :] = dk
            d_low[2, rows, :] = dv
        place = 0
        for k in range(3):
            grad = mm(normed_t[...], d_low[k])
            grad_keep[place : place + width, :] = jnp.where(flag, grad[:, half:], grad[:, :half]).astype(BF16)
            grad_send[place : place + width, :] = jnp.where(flag, grad[:, :half], grad[:, half:]).astype(BF16)
            place += width
        grad = mm(context_t[...].astype(BF16), grad_slab[...])
        for part in range(2):
            block = grad[:, part * half : (part + 1) * half]
            grad_keep[place : place + half, :] = jnp.where(flag, block[half:], block[:half]).astype(BF16)
            grad_send[place : place + half, :] = jnp.where(flag, block[:half], block[half:]).astype(BF16)
            place += half
        pick = iota((16, half), 0)
        block = jnp.where(pick == 0, gain_grad[:, :half], jnp.where(pick == 1, gain_grad[:, half:], 0.0))
        grad_keep[place : place + 16, :] = block.astype(BF16)
        grad_send[place : place + 16, :] = block.astype(BF16)


def shape(dims, dtype):
    return jax.ShapeDtypeStruct(tuple(dims), dtype)


SMEM_SPEC = pl.BlockSpec(memory_space=pltpu.SMEM)
FAR_SPEC = pl.BlockSpec(memory_space=pltpu.HBM)


def whole(array):
    zeros = (0,) * len(array.shape)
    return pl.BlockSpec(tuple(array.shape), lambda *_: zeros)


def simple_call(kernel, outs, inputs, scratch=(), scalars=0, scalar_outs=0, limit=ROWS_BYTES):
    specs = [SMEM_SPEC] * scalars + [whole(x) for x in inputs[scalars:]]
    return pl.pallas_call(
        kernel,
        out_shape=outs,
        in_specs=specs,
        out_specs=tuple(whole(x) for x in outs[: len(outs) - scalar_outs]) + (SMEM_SPEC,) * scalar_outs,
        scratch_shapes=scratch,
        compiler_params=pltpu.CompilerParams(vmem_limit_bytes=limit),
    )(*inputs)


def on_device(
    features,
    element_kinds,
    bin_cells,
    kind_embed,
    norm_gain,
    w_query,
    w_key,
    w_value,
    w_out,
    cotangent,
):
    regions = lax.axis_size("region")
    cores = lax.axis_size("head")
    local_rows = BINS_DEV * SLOTS
    capacity = local_rows // regions
    count, half = features.shape
    width = w_query.shape[0]
    heads = width // HEAD_DIM
    assert cores == BINS_DEV and half * cores == width and half == LANES
    core = lax.axis_index("head").astype(I32).reshape(1)
    swap = [(i, (i + 1) % cores) for i in range(cores)]

    def other_core(x):
        return lax.ppermute(x, "head", swap)

    def exchange(x):
        return lax.all_to_all(x, "region", split_axis=0, concat_axis=0, tiled=True)

    gain = norm_gain.reshape(1, width)
    kinds_row = element_kinds.reshape(1, count)
    packed_shape = shape((regions, capacity, half), BF16)
    tagged_shape = shape((regions, capacity + TAG_ROWS, half), BF16)
    packed_base, target = simple_call(
        functools.partial(pack_kernel, regions, capacity),
        (tagged_shape, shape((1, count), I32)),
        (bin_cells.reshape(1, count), kinds_row, features, kind_embed),
        limit=None,
    )
    got_base = exchange(packed_base)
    packed_cot, w_own, gain = simple_call(
        functools.partial(pack_cot_kernel, regions, capacity),
        (tagged_shape, shape((4, width, half), BF16), shape((1, width), F32)),
        (target, kinds_row, cotangent, gain, w_query, w_key, w_value, w_out),
    )
    w_other = other_core(w_own)
    got_base, packed_cot = lax.optimization_barrier((got_base, packed_cot))
    got_cot = exchange(packed_cot)
    got_base_other = other_core(got_base)
    rows_shape = shape((SLOTS, half), BF16)
    lift = pltpu.VMEM((SLOTS + capacity, half), F32)

    turned = (width, SLOTS)
    exps_shape = shape((heads, SLOTS, SLOTS), BF16)
    exps_spec = pl.BlockSpec((PER_STEP, SLOTS, SLOTS), lambda h: (h, 0, 0))
    inputs = (core, got_base, got_base_other, w_own, w_other, gain)
    outs = (
        shape((heads * SLOTS, SLOTS), BF16),
        exps_shape,
        shape((heads * SLOTS // 2, SLOTS), F32),
        rows_shape,
        rows_shape,
        shape((2, regions + 1), I32),
    )
    work = heads * SLOTS * SLOTS
    held = (
        pltpu.VMEM((SLOTS, width), BF16),
        pltpu.VMEM(turned, BF16),
        pltpu.VMEM((SLOTS, width), BF16),
        pltpu.VMEM(turned, BF16),
        pltpu.VMEM(turned, F32),
        pltpu.VMEM((heads, SLOTS), F32),
        pltpu.SemaphoreType.DMA((6,)),
    )
    low, exps, wide, attn_keep, attn_send, marks = pl.pallas_call(
        functools.partial(forward_kernel, heads, regions, capacity),
        grid=(heads // PER_STEP,),
        out_shape=outs,
        in_specs=[SMEM_SPEC] + [whole(x) for x in inputs[1:]],
        out_specs=(FAR_SPEC, exps_spec, FAR_SPEC) + tuple(whole(x) for x in outs[3:5]) + (SMEM_SPEC,),
        scratch_shapes=(pltpu.VMEM((width, SLOTS), BF16), pltpu.VMEM((width, width), BF16), lift, lift) + held,
        compiler_params=pltpu.CompilerParams(vmem_limit_bytes=ATTENTION_BYTES),
        cost_estimate=pl.CostEstimate(flops=4 * work * width, transcendentals=work, bytes_accessed=2 * work),
        name="forward",
    )(*inputs)
    attn_other = other_core(attn_send)
    (packed_attn,) = simple_call(
        functools.partial(ungroup_kernel, regions, capacity),
        (packed_shape,),
        (core, marks, attn_keep, attn_other),
        scratch=(lift, lift),
        scalars=2,
    )

    got_cot_other = other_core(got_cot)
    grad_rows = 4 * width + 16
    inputs = (core, marks, got_cot, got_cot_other, w_own, w_other, gain, low, exps, wide)
    outs = (rows_shape, rows_shape, shape((grad_rows, half), BF16), shape((grad_rows, half), BF16))
    d_keep, d_send, grad_keep, grad_send = pl.pallas_call(
        functools.partial(backward_kernel, heads, regions, capacity),
        grid=(heads // PER_STEP,),
        out_shape=outs,
        in_specs=[SMEM_SPEC] * 2 + [whole(x) for x in inputs[2:7]] + [FAR_SPEC, exps_spec, FAR_SPEC],
        out_specs=tuple(whole(x) for x in outs),
        scratch_shapes=(
            pltpu.VMEM((width, SLOTS), BF16),
            pltpu.VMEM((SLOTS, width), F32),
            pltpu.VMEM((width, SLOTS), F32),
            pltpu.VMEM((width, SLOTS), F32),
            pltpu.VMEM((SLOTS, width), BF16),
            lift,
            lift,
            pltpu.VMEM((width, SLOTS), BF16),
            pltpu.VMEM((3, SLOTS, width), BF16),
        )
        + held,
        compiler_params=pltpu.CompilerParams(vmem_limit_bytes=ATTENTION_BYTES),
        cost_estimate=pl.CostEstimate(flops=8 * work * width, transcendentals=0, bytes_accessed=2 * work),
        name="backward",
    )(*inputs)

    share = 4 * width // regions
    grad_other = other_core(grad_send)
    pairs = (grad_keep[: 4 * width].astype(F32) + grad_other[: 4 * width].astype(F32)).astype(BF16)
    pairs = pairs.reshape(regions, share, half)
    gain_part = (grad_keep[4 * width :].astype(F32) + grad_other[4 * width :].astype(F32)).astype(BF16)
    payload_shape = shape((regions, capacity + share + KIND_ROWS, half), BF16)
    packed_grad, extra = simple_call(
        functools.partial(ungroup_grad_kernel, regions, capacity),
        (payload_shape, shape((KIND_ROWS, half), BF16)),
        (core, marks, d_keep, other_core(d_send), got_cot, gain_part),
        scratch=(lift, lift),
        scalars=2,
    )
    got_cot, packed_attn = lax.optimization_barrier((got_cot, packed_attn))
    home_attn = exchange(packed_attn)
    home_attn, pairs = lax.optimization_barrier((home_attn, pairs))
    shares = exchange(pairs)
    payload = pl.pallas_call(
        functools.partial(share_kernel, regions, capacity),
        out_shape=payload_shape,
        in_specs=[whole(shares), whole(extra), pl.BlockSpec(memory_space=pl.ANY)],
        out_specs=pl.BlockSpec(memory_space=pl.ANY),
        scratch_shapes=(pltpu.VMEM((share + KIND_ROWS, half), BF16), pltpu.SemaphoreType.DMA((regions,))),
        input_output_aliases={2: 0},
        compiler_params=pltpu.CompilerParams(vmem_limit_bytes=ROWS_BYTES),
        name="share",
    )(shares, extra, packed_grad)
    home_grad = exchange(payload)
    (attended,) = simple_call(pick_kernel, (shape((count, half), BF16),), (target, home_attn))
    column_shape = shape((width, half), F32)
    grad_feats, grad_q, grad_k, grad_v, grad_o, grad_gain, grad_embed = simple_call(
        functools.partial(last_kernel, regions, capacity, float(count * regions) ** (-0.5)),
        (
            shape((count, half), BF16),
            column_shape,
            column_shape,
            column_shape,
            shape((half, width), F32),
            shape((1, width), F32),
            shape((KINDS, half), F32),
        ),
        (target, home_grad),
        scratch=(pltpu.VMEM((4 * width, half), F32),),
    )
    return (attended, grad_feats, grad_q, grad_k, grad_v, grad_o, grad_gain.reshape(width), grad_embed)


def solution(mesh):
    placed = (
        P(("groups", "region"), "head"),
        P(("groups", "region")),
        P(("groups", "region")),
        P(None, "head"),
        P(),
        P(None, "head"),
        P(None, "head"),
        P(None, "head"),
        P("head", None),
        P(("groups", "region"), "head"),
    )

    return jax.shard_map(
        on_device,
        mesh=mesh,
        in_specs=placed,
        out_specs=(
            P(("groups", "region"), "head"),
            P(("groups", "region"), "head"),
            P("groups", "head"),
            P("groups", "head"),
            P("groups", "head"),
            P(("groups", "head"), None),
            P("groups"),
            P("groups", "head"),
        ),
        check_vma=False,
    )
```

```python
import functools

import jax
import jax.numpy as jnp
from jax import lax
from jax.experimental import pallas as pl
from jax.experimental.pallas import tpu as pltpu
from jax.sharding import PartitionSpec as P


HEAD_DIM = 32
KINDS = 12
SLOTS = 1024
BINS_DEV = 2
MASKED = -1000000000.0
EPSILON = 1e-06
LOG2E = 1.4426950408889634

F32 = jnp.float32
BF16 = jnp.bfloat16
I32 = jnp.int32
LANES = 128
TAG_ROWS = 16
KIND_ROWS = 16
HEAD_PAD = 48
PER_STEP = 2
CHUNK = 256
ATTENTION_BYTES = 40 << 20
ROWS_BYTES = 16 << 20
NT = (((1,), (1,)), ((), ()))
TN = (((0,), (0,)), ((), ()))


def iota(shape, axis):
    return lax.broadcasted_iota(I32, shape, axis)


def mm(a, b):
    return jnp.dot(a, b, preferred_element_type=F32)


def mm_nt(a, b):
    return lax.dot_general(a, b, NT, preferred_element_type=F32)


def mm_tn(a, b):
    return lax.dot_general(a, b, TN, preferred_element_type=F32)


def hot(condition):
    return jnp.where(condition, 1.0, 0.0).astype(BF16)


def log2_of(n):
    return n.bit_length() - 1


def turned(row):
    return jnp.transpose(jnp.broadcast_to(row.astype(F32), (LANES, row.shape[1])))


def running(group_hot):
    rows, count = group_hot.shape
    blocks = count // LANES
    stacked = jnp.concatenate([group_hot[:, k * LANES : (k + 1) * LANES] for k in range(blocks)], axis=0)
    before = hot(iota((LANES, LANES), 0) < iota((LANES, LANES), 1))
    inside = mm(stacked.astype(BF16), before)
    sums = jnp.sum(stacked, axis=1, keepdims=True)
    offset = jnp.zeros((rows, 1), F32)
    pieces = []
    for k in range(blocks):
        part = slice(k * rows, (k + 1) * rows)
        pieces.append(inside[part] + offset)
        offset = offset + sums[part]
    return jnp.concatenate(pieces, axis=1), offset


def positions(regions, capacity, cell):
    count = cell.shape[1]
    owner = lax.shift_right_logical(cell, log2_of(BINS_DEV * SLOTS))
    group = lax.shift_right_logical(cell, log2_of(SLOTS))
    classes = max(BINS_DEV * regions, 16)
    group_hot = jnp.where(iota((classes, count), 0) == group, 1.0, 0.0)
    before, counts = running(group_hot)
    rank = jnp.sum(before * group_hot, axis=0, keepdims=True).astype(I32)
    second = jnp.bitwise_and(group, 1) > 0
    return owner, jnp.where(second, capacity - 1 - rank, rank), counts


def to_chunks(capacity, place, owner_column, rows, first, many):
    chosen = hot(iota((capacity, place.shape[1]), 0) == place)
    wide = rows.astype(F32)
    masked = [jnp.where(owner_column == float(first + k), wide, 0.0).astype(BF16) for k in range(many)]
    return mm(chosen, jnp.concatenate(masked, axis=1)).astype(BF16)


def pack_kernel(regions, capacity, cells, kinds, feats, embed, out_base, out_target):
    count, half = feats.shape
    owner, place, counts = positions(regions, capacity, cells[...])
    out_target[...] = owner * capacity + place
    kinds_hot = hot(iota((KINDS, count), 0) == kinds[...])
    base = (feats[...].astype(F32) + mm_tn(kinds_hot, embed[...])).astype(BF16)
    owner_column = turned(owner)
    tag_place = iota((TAG_ROWS, half), 0)
    for r in range(0, regions, 2):
        moved = to_chunks(capacity, place, owner_column, base, r, 2)
        for k in range(2):
            out_base[r + k, 0:capacity, :] = moved[:, k * half : (k + 1) * half]
            pair = 2 * (r + k)
            first = counts[pair : pair + 1]
            second = counts[pair + 1 : pair + 2]
            tags = jnp.where(tag_place == 0, first, jnp.where(tag_place == 1, second, 0.0))
            out_base[r + k, capacity : capacity + TAG_ROWS, :] = tags.astype(BF16)


def pack_cot_kernel(regions, capacity, target_ref, kinds, cot, gain, w_q, w_k, w_v, w_o, out_cot, out_w, out_gain):
    count, half = cot.shape
    out_gain[...] = gain[...]
    out_w[0] = w_q[...]
    out_w[1] = w_k[...]
    out_w[2] = w_v[...]
    out_w[3, 0:half, :] = w_o[:, 0:half]
    out_w[3, half:, :] = w_o[:, half:]
    target = target_ref[...]
    owner = lax.shift_right_logical(target, log2_of(capacity))
    place = jnp.bitwise_and(target, capacity - 1)
    owner_column = turned(owner)
    tags = jnp.where(iota((TAG_ROWS, count), 0) == 0, kinds[...] + 1, 0).astype(F32).astype(BF16)
    for r in range(0, regions, 2):
        moved = to_chunks(capacity, place, owner_column, cot[...], r, 2)
        for k in range(2):
            out_cot[r + k, 0:capacity, :] = moved[:, k * half : (k + 1) * half]
    for r in range(regions):
        chosen = hot(iota((capacity, count), 0) + r * capacity == target)
        tag = mm_nt(tags, chosen)
        if capacity >= LANES:
            tag = jnp.concatenate([tag[0:8, 0:LANES], tag[0:8, LANES : 2 * LANES]], axis=0)
        else:
            tag = jnp.concatenate([tag, jnp.zeros((TAG_ROWS, LANES - capacity), F32)], axis=1)
        out_cot[r, capacity : capacity + TAG_ROWS, :] = tag.astype(BF16)


def count_rows(regions, capacity, got, marks):
    start = jnp.int32(0)
    end = jnp.int32(SLOTS)
    for r in range(regions):
        block = got[r, capacity : capacity + TAG_ROWS, :].astype(F32)
        marks[0, r] = start
        marks[1, r] = end
        start = start + jnp.max(block[0:1, :]).astype(I32)
        end = end - jnp.max(block[1:2, :]).astype(I32)
    marks[0, regions] = start
    marks[1, regions] = end


def is_filled(regions, core, marks, place):
    first = jnp.where(place < marks[0, regions], 1.0, 0.0)
    second = jnp.where(place >= marks[1, regions], 1.0, 0.0)
    return jnp.where(core[0] > 0, second, first)


def lift_rows(regions, capacity, core, marks, own, other, lift, lift_other):
    for r in range(regions):
        place = pl.ds(marks[core[0], r], capacity)
        lift[place, :] = own[r, 0:capacity, :].astype(F32)
        lift_other[place, :] = other[r, 0:capacity, :].astype(F32)


def bin_rows(regions, capacity, core, marks, lift, lift_other, first, many):
    place = pl.ds(pl.multiple_of(core[0] * capacity, capacity) + first, many)
    rows = jnp.concatenate(ordered(core[0] > 0, lift[place, :], lift_other[place, :]), axis=1)
    filled = is_filled(regions, core, marks, iota((many, 1), 0) + first)
    return jnp.where(filled > 0.5, rows, 0.0).astype(BF16)


def arrival_rows(regions, capacity, core, marks, own, other, out, front, back):
    flag = core[0] > 0
    x = own[...].astype(F32)
    y = other[...].astype(F32)
    front[0:SLOTS, :] = jnp.where(flag, y, x)
    front[SLOTS:, :] = jnp.zeros((capacity, x.shape[1]), F32)
    back[0:capacity, :] = jnp.zeros((capacity, x.shape[1]), F32)
    back[capacity:, :] = jnp.where(flag, x, y)
    row = iota((capacity, 1), 0)
    for r in range(regions):
        held = marks[0, r + 1] - marks[0, r]
        rows = jnp.where(row < held, front[pl.ds(marks[0, r], capacity), :], back[pl.ds(marks[1, r], capacity), :])
        out[r, 0:capacity, :] = rows.astype(BF16)


def ungroup_kernel(regions, capacity, core, marks, own, other, out, front, back):
    arrival_rows(regions, capacity, core, marks, own, other, out, front, back)


def ungroup_grad_kernel(regions, capacity, core, marks, own, other, tagged, gain_part, out, extra, front, back):
    arrival_rows(regions, capacity, core, marks, own, other, out, front, back)
    total = jnp.zeros((KIND_ROWS, own.shape[1]), F32)
    for r in range(regions):
        block = tagged[r, capacity : capacity + TAG_ROWS, :].astype(F32)
        if capacity >= LANES:
            kind = jnp.concatenate([block[0:1], block[8:9]], axis=1)
        else:
            kind = block[0:1, 0:capacity]
        kinds_hot = hot(iota((KIND_ROWS, capacity), 0) == kind.astype(I32) - 1)
        total = total + mm(kinds_hot, out[r, 0:capacity, :])
    place = iota((KIND_ROWS, 1), 0)
    first = gain_part[0:1, :].astype(F32)
    second = gain_part[1:2, :].astype(F32)
    extra[...] = jnp.where(place == KINDS, first, jnp.where(place == KINDS + 1, second, total)).astype(BF16)


def share_kernel(regions, capacity, got, extra, packed, out, tail, sems):
    total = got[0].astype(F32)
    for r in range(1, regions):
        total = total + got[r].astype(F32)
    share = total.shape[0]
    tail[0:share, :] = total.astype(BF16)
    tail[share:, :] = extra[...]
    copies = [
        pltpu.make_async_copy(tail, out.at[r, pl.ds(capacity, share + KIND_ROWS), :], sems.at[r]) for r in range(regions)
    ]
    for copy in copies:
        copy.start()
    for copy in copies:
        copy.wait()


def last_kernel(regions, capacity, factor, target_ref, got, out, out_q, out_k, out_v, out_o, out_gain, out_embed, flat):
    pick_kernel(target_ref, got, out)
    width, half = out_q.shape
    share = 4 * width // regions
    extra = jnp.zeros((KIND_ROWS, half), F32)
    for r in range(regions):
        flat[r * share : (r + 1) * share, :] = got[r, capacity : capacity + share, :].astype(F32) * factor
        extra = extra + got[r, capacity + share : capacity + share + KIND_ROWS, :].astype(F32)
    extra = extra * factor
    out_q[...] = flat[0:width]
    out_k[...] = flat[width : 2 * width]
    out_v[...] = flat[2 * width : 3 * width]
    out_o[:, 0:half] = flat[3 * width : 3 * width + half]
    out_o[:, half:] = flat[3 * width + half : 4 * width]
    out_embed[...] = extra[0:KINDS]
    out_gain[:, 0:half] = extra[KINDS : KINDS + 1]
    out_gain[:, half:] = extra[KINDS + 1 : KINDS + 2]


def pick_kernel(target_ref, got, out):
    regions = got.shape[0]
    capacity = BINS_DEV * SLOTS // regions
    count, half = out.shape
    target = target_ref[...]
    owner_column = turned(lax.shift_right_logical(target, log2_of(capacity)))
    place_column = turned(jnp.bitwise_and(target, capacity - 1))
    width = min(capacity, LANES)
    lane = iota((1, width), 1).astype(F32)
    step = 256
    for s in range(0, count, step):
        owner = owner_column[s : s + step]
        place = place_column[s : s + step, 0:width]
        chosen = [hot(place - float(k) == lane) for k in range(0, capacity, width)]
        chosen = jnp.concatenate(chosen, axis=1)
        total = jnp.zeros((step, half), F32)
        for r in range(0, regions, 2):
            chunks = jnp.concatenate([got[r, 0:capacity, :], got[r + 1, 0:capacity, :]], axis=1)
            rows = mm(chosen, chunks)
            total = jnp.where(owner == float(r), rows[:, :half], jnp.where(owner == float(r + 1), rows[:, half:], total))
        out[s : s + step, :] = total.astype(BF16)


def ordered(flag, own, other):
    first = jnp.where(flag, other, own)
    second = jnp.where(flag, own, other)
    return first, second


def full_weights(core, own, other):
    flag = core[0] > 0
    half = own.shape[2]
    columns = []
    for k in range(3):
        columns.append(jnp.concatenate(ordered(flag, own[k], other[k]), axis=1))
    top, bottom = ordered(flag, own[3], other[3])
    rows = [jnp.concatenate([part[0:half], part[half:]], axis=1) for part in (top, bottom)]
    return columns + [jnp.concatenate(rows, axis=0)]


def norm_rows(slab, gain, width):
    wide = slab.astype(F32)
    inverse = lax.rsqrt(jnp.sum(wide * wide, axis=1, keepdims=True) / width + EPSILON)
    return wide, inverse, (wide * inverse * gain).astype(BF16)


def stack_rows(rows, extra):
    place = iota((HEAD_PAD - HEAD_DIM, rows.shape[1]), 0)
    tail = jnp.zeros(place.shape, F32)
    for k, value in enumerate(extra):
        tail = jnp.where(place == k, value, tail)
    return jnp.concatenate([rows.astype(F32), tail], axis=0)


def held_places(heads, low, wide):
    width = heads * HEAD_DIM
    return (
        low.at[pl.ds(2 * width, SLOTS), pl.ds(0, width)],
        low.at[pl.ds(0, width), :],
        low.at[pl.ds(2 * width, SLOTS), pl.ds(width, width)],
        low.at[pl.ds(width, width), :],
        wide.at[pl.ds(0, width), :],
        wide.at[pl.ds(width, heads), :],
    )


def forward_kernel(
    heads, regions, capacity, core, got, got_other, w_own, w_other, gain, low_far, exps_far, wide_far,
    keep_out, send_out, marks, keys_t, w_out, lift, lift_other, slab_out, queries_t, keys_out, values_t,
    context_t, inv_t, sems, exps_near, exps_sems
):
    step = pl.program_id(0)
    slot = jnp.bitwise_and(step, 1)
    steps = heads // PER_STEP

    def store(at, k):
        where = jnp.bitwise_and(at, 1)
        return pltpu.make_async_copy(exps_near.at[where, k], exps_far.at[at * PER_STEP + k], exps_sems.at[where, k])

    places = held_places(heads, low_far, wide_far)
    early = [
        pltpu.make_async_copy(near, far, sems.at[k])
        for k, (near, far) in enumerate(zip((slab_out, queries_t, keys_out, values_t), places[:4]))
    ]
    late = [
        pltpu.make_async_copy(near, far, sems.at[4 + k])
        for k, (near, far) in enumerate(zip((context_t, inv_t), places[4:]))
    ]
    width = heads * HEAD_DIM
    half = width // 2
    flag = core[0] > 0
    scale = HEAD_DIM**-0.5

    @pl.when(step == 0)
    def _():
        w_q, w_k, w_v, w_o = full_weights(core, w_own, w_other)
        w_out[...] = w_o
        count_rows(regions, capacity, got, marks)
        lift_rows(regions, capacity, core, marks, got, got_other, lift, lift_other)
        for first in range(0, SLOTS, CHUNK):
            rows = slice(first, first + CHUNK)
            slab = bin_rows(regions, capacity, core, marks, lift, lift_other, first, CHUNK)
            slab_out[rows, :] = slab
            _, _, normed = norm_rows(slab, gain[...], width)
            queries_t[:, rows] = jnp.transpose(mm(normed, w_q)).astype(BF16)
            k = mm(normed, w_k)
            keys_out[rows, :] = k.astype(BF16)
            keys_t[:, rows] = jnp.transpose(k).astype(BF16)
            values_t[:, rows] = jnp.transpose(mm(normed, w_v)).astype(BF16)
        for copy in early:
            copy.start()

    bias = jnp.where(is_filled(regions, core, marks, iota((1, SLOTS), 1)) > 0.5, 0.0, MASKED / scale)

    @pl.when(step >= 2)
    def _():
        for k in range(PER_STEP):
            store(step - 2, k).wait()

    for k in range(PER_STEP):
        h = step * PER_STEP + k
        head_rows = pl.ds(pl.multiple_of(h * HEAD_DIM, HEAD_DIM), HEAD_DIM)
        scaled = queries_t[head_rows, :].astype(F32) * (scale * LOG2E)
        high = scaled.astype(BF16).astype(F32)
        left = jnp.transpose(jnp.concatenate([high, stack_rows(scaled - high, (1.0,))], axis=0)).astype(BF16)
        k_rows = keys_t[head_rows, :].astype(F32)
        scores = mm(left, jnp.concatenate([k_rows, stack_rows(k_rows, (bias,))], axis=0).astype(BF16))
        top = jnp.max(scores, axis=1, keepdims=True)
        exps = jnp.exp2(scores - top).astype(BF16)
        exps_near[slot, k] = exps
        store(step, k).start()
        summed = mm_nt(stack_rows(values_t[head_rows, :], (1.0,)).astype(BF16), exps)
        inv = 1.0 / summed[HEAD_DIM : HEAD_DIM + 1]
        context_t[head_rows, :] = summed[0:HEAD_DIM] * inv
        inv_t[pl.ds(h, 1), :] = inv

    @pl.when(step == heads // PER_STEP - 1)
    def _():
        for copy in late:
            copy.start()
        rows_out = mm(jnp.transpose(context_t[...]).astype(BF16), w_out[...]).astype(BF16)
        keep_out[...] = jnp.where(flag, rows_out[:, half:], rows_out[:, :half])
        send_out[...] = jnp.where(flag, rows_out[:, :half], rows_out[:, half:])
        for copy in early + late:
            copy.wait()
        for at in range(steps - 2, steps):
            for k in range(PER_STEP):
                store(at, k).wait()


def backward_kernel(
    heads, regions, capacity, core, marks, got, got_other, w_own, w_other, gain, low_far,
    exps_in, wide_far, keep_out, send_out, grad_keep, grad_send, d_context_t, d_query, d_key_t, d_value_t, grad_slab, lift, lift_other, normed_t, d_low,
    slab_in, queries_t, keys_in, values_t, context_t, inv_t, sems
):
    step = pl.program_id(0)
    places = held_places(heads, low_far, wide_far)
    early = [
        pltpu.make_async_copy(far, near, sems.at[k])
        for k, (far, near) in enumerate(zip(places, (slab_in, queries_t, keys_in, values_t, context_t, inv_t)))
    ]
    width = heads * HEAD_DIM
    half = width // 2
    flag = core[0] > 0
    lane = iota((1, width), 1)
    scale = HEAD_DIM**-0.5

    @pl.when(step == 0)
    def _():
        for copy in early[1:] + early[:1]:
            copy.start()
        w_o = full_weights(core, w_own, w_other)[3]
        lift_rows(regions, capacity, core, marks, got, got_other, lift, lift_other)
        for first in range(0, SLOTS, CHUNK):
            rows = slice(first, first + CHUNK)
            part = bin_rows(regions, capacity, core, marks, lift, lift_other, first, CHUNK)
            grad_slab[rows, :] = part
            d_context_t[:, rows] = mm_nt(w_o, part).astype(BF16)
        for copy in early[1:]:
            copy.wait()

    for k in range(PER_STEP):
        h = step * PER_STEP + k
        head_rows = pl.ds(pl.multiple_of(h * HEAD_DIM, HEAD_DIM), HEAD_DIM)
        own_lane = lax.shift_right_logical(lane, log2_of(HEAD_DIM)) == h
        scaled = (d_context_t[head_rows, :].astype(F32) * inv_t[pl.ds(h, 1), :]).astype(BF16)
        dot = -jnp.sum(scaled.astype(F32) * context_t[head_rows, :], axis=0, keepdims=True)
        dot_high = dot.astype(BF16).astype(F32)
        left = jnp.transpose(stack_rows(scaled, (dot_high, dot - dot_high))).astype(BF16)
        centred = mm(left, stack_rows(values_t[head_rows, :], (1.0, 1.0)).astype(BF16))
        exps = exps_in[k]
        d_scores = (exps.astype(F32) * centred).astype(BF16)
        dq = mm(d_scores, keys_in[...])
        d_query[...] = jnp.where(own_lane, dq * scale, d_query[...])
        d_key_t[head_rows, :] = mm(queries_t[head_rows, :], d_scores) * scale
        d_value_t[head_rows, :] = mm(scaled, exps)

    @pl.when(step == heads // PER_STEP - 1)
    def _():
        w_q, w_k, w_v, _ = full_weights(core, w_own, w_other)
        early[0].wait()
        gain_grad = jnp.zeros((1, width), F32)
        for first in range(0, SLOTS, CHUNK):
            rows = slice(first, first + CHUNK)
            wide, inverse, normed = norm_rows(slab_in[rows, :], gain[...], width)
            dq = d_query[rows, :].astype(BF16)
            dk = jnp.transpose(d_key_t[:, rows]).astype(BF16)
            dv = jnp.transpose(d_value_t[:, rows]).astype(BF16)
            d_normed = mm_nt(dq, w_q) + mm_nt(dk, w_k) + mm_nt(dv, w_v)
            scaled = gain[...] * d_normed
            along = jnp.sum(scaled * wide, axis=1, keepdims=True)
            d_slab = (inverse * scaled - wide * (inverse * inverse * inverse) * along / width).astype(BF16)
            keep_out[rows, :] = jnp.where(flag, d_slab[:, half:], d_slab[:, :half])
            send_out[rows, :] = jnp.where(flag, d_slab[:, :half], d_slab[:, half:])
            gain_grad = gain_grad + jnp.sum(d_normed * wide * inverse, axis=0, keepdims=True)
            normed_t[:, rows] = jnp.transpose(normed.astype(F32)).astype(BF16)
            d_low[0, rows, :] = dq
            d_low[1, rows, :] = dk
            d_low[2, rows, :] = dv
        place = 0
        for k in range(3):
            grad = mm(normed_t[...], d_low[k])
            grad_keep[place : place + width, :] = jnp.where(flag, grad[:, half:], grad[:, :half]).astype(BF16)
            grad_send[place : place + width, :] = jnp.where(flag, grad[:, :half], grad[:, half:]).astype(BF16)
            place += width
        grad = mm(context_t[...].astype(BF16), grad_slab[...])
        for part in range(2):
            block = grad[:, part * half : (part + 1) * half]
            grad_keep[place : place + half, :] = jnp.where(flag, block[half:], block[:half]).astype(BF16)
            grad_send[place : place + half, :] = jnp.where(flag, block[:half], block[half:]).astype(BF16)
            place += half
        pick = iota((16, half), 0)
        block = jnp.where(pick == 0, gain_grad[:, :half], jnp.where(pick == 1, gain_grad[:, half:], 0.0))
        grad_keep[place : place + 16, :] = block.astype(BF16)
        grad_send[place : place + 16, :] = block.astype(BF16)


def shape(dims, dtype):
    return jax.ShapeDtypeStruct(tuple(dims), dtype)


SMEM_SPEC = pl.BlockSpec(memory_space=pltpu.SMEM)
FAR_SPEC = pl.BlockSpec(memory_space=pltpu.HBM)


def whole(array):
    zeros = (0,) * len(array.shape)
    return pl.BlockSpec(tuple(array.shape), lambda *_: zeros)


def simple_call(kernel, outs, inputs, scratch=(), scalars=0, scalar_outs=0, limit=ROWS_BYTES):
    specs = [SMEM_SPEC] * scalars + [whole(x) for x in inputs[scalars:]]
    return pl.pallas_call(
        kernel,
        out_shape=outs,
        in_specs=specs,
        out_specs=tuple(whole(x) for x in outs[: len(outs) - scalar_outs]) + (SMEM_SPEC,) * scalar_outs,
        scratch_shapes=scratch,
        compiler_params=pltpu.CompilerParams(vmem_limit_bytes=limit),
    )(*inputs)


def on_device(
    features,
    element_kinds,
    bin_cells,
    kind_embed,
    norm_gain,
    w_query,
    w_key,
    w_value,
    w_out,
    cotangent,
):
    regions = lax.axis_size("region")
    cores = lax.axis_size("head")
    local_rows = BINS_DEV * SLOTS
    capacity = local_rows // regions
    count, half = features.shape
    width = w_query.shape[0]
    heads = width // HEAD_DIM
    assert cores == BINS_DEV and half * cores == width and half == LANES
    core = lax.axis_index("head").astype(I32).reshape(1)
    swap = [(i, (i + 1) % cores) for i in range(cores)]

    def other_core(x):
        return lax.ppermute(x, "head", swap)

    def exchange(x):
        return lax.all_to_all(x, "region", split_axis=0, concat_axis=0, tiled=True)

    gain = norm_gain.reshape(1, width)
    kinds_row = element_kinds.reshape(1, count)
    packed_shape = shape((regions, capacity, half), BF16)
    tagged_shape = shape((regions, capacity + TAG_ROWS, half), BF16)
    packed_base, target = simple_call(
        functools.partial(pack_kernel, regions, capacity),
        (tagged_shape, shape((1, count), I32)),
        (bin_cells.reshape(1, count), kinds_row, features, kind_embed),
        limit=None,
    )
    got_base = exchange(packed_base)
    packed_cot, w_own, gain = simple_call(
        functools.partial(pack_cot_kernel, regions, capacity),
        (tagged_shape, shape((4, width, half), BF16), shape((1, width), F32)),
        (target, kinds_row, cotangent, gain, w_query, w_key, w_value, w_out),
    )
    w_other = other_core(w_own)
    got_base, packed_cot = lax.optimization_barrier((got_base, packed_cot))
    got_cot = exchange(packed_cot)
    got_base_other = other_core(got_base)
    rows_shape = shape((SLOTS, half), BF16)
    lift = pltpu.VMEM((SLOTS + capacity, half), F32)

    turned = (width, SLOTS)
    exps_shape = shape((heads, SLOTS, SLOTS), BF16)
    exps_spec = pl.BlockSpec((PER_STEP, SLOTS, SLOTS), lambda h: (h, 0, 0))
    inputs = (core, got_base, got_base_other, w_own, w_other, gain)
    outs = (
        shape((heads * SLOTS, SLOTS), BF16),
        exps_shape,
        shape((heads * SLOTS // 2, SLOTS), F32),
        rows_shape,
        rows_shape,
        shape((2, regions + 1), I32),
    )
    work = heads * SLOTS * SLOTS
    held = (
        pltpu.VMEM((SLOTS, width), BF16),
        pltpu.VMEM(turned, BF16),
        pltpu.VMEM((SLOTS, width), BF16),
        pltpu.VMEM(turned, BF16),
        pltpu.VMEM(turned, F32),
        pltpu.VMEM((heads, SLOTS), F32),
        pltpu.SemaphoreType.DMA((6,)),
    )
    staged = (pltpu.VMEM((2, PER_STEP, SLOTS, SLOTS), BF16), pltpu.SemaphoreType.DMA((2, PER_STEP)))
    low, exps, wide, attn_keep, attn_send, marks = pl.pallas_call(
        functools.partial(forward_kernel, heads, regions, capacity),
        grid=(heads // PER_STEP,),
        out_shape=outs,
        in_specs=[SMEM_SPEC] + [whole(x) for x in inputs[1:]],
        out_specs=(FAR_SPEC,) * 3 + tuple(whole(x) for x in outs[3:5]) + (SMEM_SPEC,),
        scratch_shapes=(pltpu.VMEM((width, SLOTS), BF16), pltpu.VMEM((width, width), BF16), lift, lift) + held + staged,
        compiler_params=pltpu.CompilerParams(vmem_limit_bytes=ATTENTION_BYTES),
        cost_estimate=pl.CostEstimate(flops=4 * work * width, transcendentals=work, bytes_accessed=2 * work),
        name="forward",
    )(*inputs)
    attn_other = other_core(attn_send)
    (packed_attn,) = simple_call(
        functools.partial(ungroup_kernel, regions, capacity),
        (packed_shape,),
        (core, marks, attn_keep, attn_other),
        scratch=(lift, lift),
        scalars=2,
    )

    got_cot_other = other_core(got_cot)
    grad_rows = 4 * width + 16
    inputs = (core, marks, got_cot, got_cot_other, w_own, w_other, gain, low, exps, wide)
    outs = (rows_shape, rows_shape, shape((grad_rows, half), BF16), shape((grad_rows, half), BF16))
    d_keep, d_send, grad_keep, grad_send = pl.pallas_call(
        functools.partial(backward_kernel, heads, regions, capacity),
        grid=(heads // PER_STEP,),
        out_shape=outs,
        in_specs=[SMEM_SPEC] * 2 + [whole(x) for x in inputs[2:7]] + [FAR_SPEC, exps_spec, FAR_SPEC],
        out_specs=tuple(whole(x) for x in outs),
        scratch_shapes=(
            pltpu.VMEM((width, SLOTS), BF16),
            pltpu.VMEM((SLOTS, width), F32),
            pltpu.VMEM((width, SLOTS), F32),
            pltpu.VMEM((width, SLOTS), F32),
            pltpu.VMEM((SLOTS, width), BF16),
            lift,
            lift,
            pltpu.VMEM((width, SLOTS), BF16),
            pltpu.VMEM((3, SLOTS, width), BF16),
        )
        + held,
        compiler_params=pltpu.CompilerParams(vmem_limit_bytes=ATTENTION_BYTES),
        cost_estimate=pl.CostEstimate(flops=8 * work * width, transcendentals=0, bytes_accessed=2 * work),
        name="backward",
    )(*inputs)

    share = 4 * width // regions
    grad_other = other_core(grad_send)
    pairs = (grad_keep[: 4 * width].astype(F32) + grad_other[: 4 * width].astype(F32)).astype(BF16)
    pairs = pairs.reshape(regions, share, half)
    gain_part = (grad_keep[4 * width :].astype(F32) + grad_other[4 * width :].astype(F32)).astype(BF16)
    payload_shape = shape((regions, capacity + share + KIND_ROWS, half), BF16)
    packed_grad, extra = simple_call(
        functools.partial(ungroup_grad_kernel, regions, capacity),
        (payload_shape, shape((KIND_ROWS, half), BF16)),
        (core, marks, d_keep, other_core(d_send), got_cot, gain_part),
        scratch=(lift, lift),
        scalars=2,
    )
    got_cot, packed_attn = lax.optimization_barrier((got_cot, packed_attn))
    home_attn = exchange(packed_attn)
    home_attn, pairs = lax.optimization_barrier((home_attn, pairs))
    shares = exchange(pairs)
    payload = pl.pallas_call(
        functools.partial(share_kernel, regions, capacity),
        out_shape=payload_shape,
        in_specs=[whole(shares), whole(extra), pl.BlockSpec(memory_space=pl.ANY)],
        out_specs=pl.BlockSpec(memory_space=pl.ANY),
        scratch_shapes=(pltpu.VMEM((share + KIND_ROWS, half), BF16), pltpu.SemaphoreType.DMA((regions,))),
        input_output_aliases={2: 0},
        compiler_params=pltpu.CompilerParams(vmem_limit_bytes=ROWS_BYTES),
        name="share",
    )(shares, extra, packed_grad)
    home_grad = exchange(payload)
    (attended,) = simple_call(pick_kernel, (shape((count, half), BF16),), (target, home_attn))
    column_shape = shape((width, half), F32)
    grad_feats, grad_q, grad_k, grad_v, grad_o, grad_gain, grad_embed = simple_call(
        functools.partial(last_kernel, regions, capacity, float(count * regions) ** (-0.5)),
        (
            shape((count, half), BF16),
            column_shape,
            column_shape,
            column_shape,
            shape((half, width), F32),
            shape((1, width), F32),
            shape((KINDS, half), F32),
        ),
        (target, home_grad),
        scratch=(pltpu.VMEM((4 * width, half), F32),),
    )
    return (attended, grad_feats, grad_q, grad_k, grad_v, grad_o, grad_gain.reshape(width), grad_embed)


def solution(mesh):
    placed = (
        P(("groups", "region"), "head"),
        P(("groups", "region")),
        P(("groups", "region")),
        P(None, "head"),
        P(),
        P(None, "head"),
        P(None, "head"),
        P(None, "head"),
        P("head", None),
        P(("groups", "region"), "head"),
    )

    return jax.shard_map(
        on_device,
        mesh=mesh,
        in_specs=placed,
        out_specs=(
            P(("groups", "region"), "head"),
            P(("groups", "region"), "head"),
            P("groups", "head"),
            P("groups", "head"),
            P("groups", "head"),
            P(("groups", "head"), None),
            P("groups"),
            P("groups", "head"),
        ),
        check_vma=False,
    )
```

```python
import functools

import jax
import jax.numpy as jnp
from jax import lax
from jax.experimental import pallas as pl
from jax.experimental.pallas import tpu as pltpu
from jax.sharding import PartitionSpec as P


HEAD_DIM = 32
KINDS = 12
SLOTS = 1024
BINS_DEV = 2
MASKED = -1000000000.0
EPSILON = 1e-06
LOG2E = 1.4426950408889634

F32 = jnp.float32
BF16 = jnp.bfloat16
I32 = jnp.int32
LANES = 128
TAG_ROWS = 16
COUNT_ROWS = 8
KIND_ROWS = 16
HEAD_PAD = 48
PER_STEP = 2
CHUNK = 256
ATTENTION_BYTES = 40 << 20
ROWS_BYTES = 16 << 20
NT = (((1,), (1,)), ((), ()))
TN = (((0,), (0,)), ((), ()))


def iota(shape, axis):
    return lax.broadcasted_iota(I32, shape, axis)


def mm(a, b):
    return jnp.dot(a, b, preferred_element_type=F32)


def mm_nt(a, b):
    return lax.dot_general(a, b, NT, preferred_element_type=F32)


def mm_tn(a, b):
    return lax.dot_general(a, b, TN, preferred_element_type=F32)


def hot(condition):
    return jnp.where(condition, 1.0, 0.0).astype(BF16)


def log2_of(n):
    return n.bit_length() - 1


def turned(row):
    return jnp.transpose(jnp.broadcast_to(row.astype(F32), (LANES, row.shape[1])))


def running(group_hot):
    rows, count = group_hot.shape
    blocks = count // LANES
    stacked = jnp.concatenate([group_hot[:, k * LANES : (k + 1) * LANES] for k in range(blocks)], axis=0)
    before = hot(iota((LANES, LANES), 0) < iota((LANES, LANES), 1))
    inside = mm(stacked.astype(BF16), before)
    sums = jnp.sum(stacked, axis=1, keepdims=True)
    offset = jnp.zeros((rows, 1), F32)
    pieces = []
    for k in range(blocks):
        part = slice(k * rows, (k + 1) * rows)
        pieces.append(inside[part] + offset)
        offset = offset + sums[part]
    return jnp.concatenate(pieces, axis=1), offset


def positions(regions, capacity, cell):
    count = cell.shape[1]
    owner = lax.shift_right_logical(cell, log2_of(BINS_DEV * SLOTS))
    group = lax.shift_right_logical(cell, log2_of(SLOTS))
    classes = max(BINS_DEV * regions, 16)
    group_hot = jnp.where(iota((classes, count), 0) == group, 1.0, 0.0)
    before, counts = running(group_hot)
    rank = jnp.sum(before * group_hot, axis=0, keepdims=True).astype(I32)
    second = jnp.bitwise_and(group, 1) > 0
    return owner, jnp.where(second, capacity - 1 - rank, rank), counts


def to_chunks(capacity, place, owner_column, rows, first, many):
    chosen = hot(iota((capacity, place.shape[1]), 0) == place)
    wide = rows.astype(F32)
    masked = [jnp.where(owner_column == float(first + k), wide, 0.0).astype(BF16) for k in range(many)]
    return mm(chosen, jnp.concatenate(masked, axis=1)).astype(BF16)


def pack_kernel(regions, capacity, cells, kinds, feats, embed, out_base, out_target):
    count, half = feats.shape
    owner, place, counts = positions(regions, capacity, cells[...])
    out_target[...] = owner * capacity + place
    kinds_hot = hot(iota((KINDS, count), 0) == kinds[...])
    base = (feats[...].astype(F32) + mm_tn(kinds_hot, embed[...])).astype(BF16)
    owner_column = turned(owner)
    tag_place = iota((COUNT_ROWS, half), 0)
    for r in range(0, regions, 2):
        moved = to_chunks(capacity, place, owner_column, base, r, 2)
        for k in range(2):
            out_base[r + k, 0:capacity, :] = moved[:, k * half : (k + 1) * half]
            pair = 2 * (r + k)
            first = counts[pair : pair + 1]
            second = counts[pair + 1 : pair + 2]
            tags = jnp.where(tag_place == 0, first, jnp.where(tag_place == 1, second, 0.0))
            out_base[r + k, capacity : capacity + COUNT_ROWS, :] = tags.astype(BF16)


def pack_cot_kernel(regions, capacity, target_ref, kinds, cot, gain, w_q, w_k, w_v, w_o, out_cot, out_w, out_gain):
    count, half = cot.shape
    out_gain[...] = gain[...]
    out_w[0] = w_q[...]
    out_w[1] = w_k[...]
    out_w[2] = w_v[...]
    out_w[3, 0:half, :] = w_o[:, 0:half]
    out_w[3, half:, :] = w_o[:, half:]
    target = target_ref[...]
    owner = lax.shift_right_logical(target, log2_of(capacity))
    place = jnp.bitwise_and(target, capacity - 1)
    owner_column = turned(owner)
    tags = jnp.where(iota((TAG_ROWS, count), 0) == 0, kinds[...] + 1, 0).astype(F32).astype(BF16)
    for r in range(0, regions, 2):
        moved = to_chunks(capacity, place, owner_column, cot[...], r, 2)
        for k in range(2):
            out_cot[r + k, 0:capacity, :] = moved[:, k * half : (k + 1) * half]
    for r in range(regions):
        chosen = hot(iota((capacity, count), 0) + r * capacity == target)
        tag = mm_nt(tags, chosen)
        if capacity >= LANES:
            tag = jnp.concatenate([tag[0:8, 0:LANES], tag[0:8, LANES : 2 * LANES]], axis=0)
        else:
            tag = jnp.concatenate([tag, jnp.zeros((TAG_ROWS, LANES - capacity), F32)], axis=1)
        out_cot[r, capacity : capacity + TAG_ROWS, :] = tag.astype(BF16)


def count_rows(regions, capacity, got, marks):
    start = jnp.int32(0)
    end = jnp.int32(SLOTS)
    for r in range(regions):
        block = got[r, capacity : capacity + COUNT_ROWS, :].astype(F32)
        marks[0, r] = start
        marks[1, r] = end
        start = start + jnp.max(block[0:1, :]).astype(I32)
        end = end - jnp.max(block[1:2, :]).astype(I32)
    marks[0, regions] = start
    marks[1, regions] = end


def is_filled(regions, core, marks, place):
    first = jnp.where(place < marks[0, regions], 1.0, 0.0)
    second = jnp.where(place >= marks[1, regions], 1.0, 0.0)
    return jnp.where(core[0] > 0, second, first)


def lift_rows(regions, capacity, core, marks, own, other, lift, lift_other):
    for r in range(regions):
        place = pl.ds(marks[core[0], r], capacity)
        lift[place, :] = own[r, 0:capacity, :].astype(F32)
        lift_other[place, :] = other[r, 0:capacity, :].astype(F32)


def bin_rows(regions, capacity, core, marks, lift, lift_other, first, many):
    place = pl.ds(pl.multiple_of(core[0] * capacity, capacity) + first, many)
    rows = jnp.concatenate(ordered(core[0] > 0, lift[place, :], lift_other[place, :]), axis=1)
    filled = is_filled(regions, core, marks, iota((many, 1), 0) + first)
    return jnp.where(filled > 0.5, rows, 0.0).astype(BF16)


def arrival_rows(regions, capacity, core, marks, own, other, out, front, back):
    flag = core[0] > 0
    x = own[...].astype(F32)
    y = other[...].astype(F32)
    front[0:SLOTS, :] = jnp.where(flag, y, x)
    front[SLOTS:, :] = jnp.zeros((capacity, x.shape[1]), F32)
    back[0:capacity, :] = jnp.zeros((capacity, x.shape[1]), F32)
    back[capacity:, :] = jnp.where(flag, x, y)
    row = iota((capacity, 1), 0)
    for r in range(regions):
        held = marks[0, r + 1] - marks[0, r]
        rows = jnp.where(row < held, front[pl.ds(marks[0, r], capacity), :], back[pl.ds(marks[1, r], capacity), :])
        out[r, 0:capacity, :] = rows.astype(BF16)


def ungroup_kernel(regions, capacity, core, marks, own, other, out, front, back):
    arrival_rows(regions, capacity, core, marks, own, other, out, front, back)


def ungroup_grad_kernel(regions, capacity, core, marks, own, other, tagged, gain_part, out, extra, front, back):
    arrival_rows(regions, capacity, core, marks, own, other, out, front, back)
    total = jnp.zeros((KIND_ROWS, own.shape[1]), F32)
    for r in range(regions):
        block = tagged[r, capacity : capacity + TAG_ROWS, :].astype(F32)
        if capacity >= LANES:
            kind = jnp.concatenate([block[0:1], block[8:9]], axis=1)
        else:
            kind = block[0:1, 0:capacity]
        kinds_hot = hot(iota((KIND_ROWS, capacity), 0) == kind.astype(I32) - 1)
        total = total + mm(kinds_hot, out[r, 0:capacity, :])
    place = iota((KIND_ROWS, 1), 0)
    first = gain_part[0:1, :].astype(F32)
    second = gain_part[1:2, :].astype(F32)
    extra[...] = jnp.where(place == KINDS, first, jnp.where(place == KINDS + 1, second, total)).astype(BF16)


def share_kernel(regions, capacity, got, extra, packed, out, tail, sems):
    total = got[0].astype(F32)
    for r in range(1, regions):
        total = total + got[r].astype(F32)
    share = total.shape[0]
    tail[0:share, :] = total.astype(BF16)
    tail[share:, :] = extra[...]
    copies = [
        pltpu.make_async_copy(tail, out.at[r, pl.ds(capacity, share + KIND_ROWS), :], sems.at[r]) for r in range(regions)
    ]
    for copy in copies:
        copy.start()
    for copy in copies:
        copy.wait()


def last_kernel(regions, capacity, factor, target_ref, got, out, out_q, out_k, out_v, out_o, out_gain, out_embed, flat):
    pick_kernel(target_ref, got, out)
    width, half = out_q.shape
    share = 4 * width // regions
    extra = jnp.zeros((KIND_ROWS, half), F32)
    for r in range(regions):
        flat[r * share : (r + 1) * share, :] = got[r, capacity : capacity + share, :].astype(F32) * factor
        extra = extra + got[r, capacity + share : capacity + share + KIND_ROWS, :].astype(F32)
    extra = extra * factor
    out_q[...] = flat[0:width]
    out_k[...] = flat[width : 2 * width]
    out_v[...] = flat[2 * width : 3 * width]
    out_o[:, 0:half] = flat[3 * width : 3 * width + half]
    out_o[:, half:] = flat[3 * width + half : 4 * width]
    out_embed[...] = extra[0:KINDS]
    out_gain[:, 0:half] = extra[KINDS : KINDS + 1]
    out_gain[:, half:] = extra[KINDS + 1 : KINDS + 2]


def pick_kernel(target_ref, got, out):
    regions = got.shape[0]
    capacity = BINS_DEV * SLOTS // regions
    count, half = out.shape
    target = target_ref[...]
    owner_column = turned(lax.shift_right_logical(target, log2_of(capacity)))
    place_column = turned(jnp.bitwise_and(target, capacity - 1))
    width = min(capacity, LANES)
    lane = iota((1, width), 1).astype(F32)
    step = 256
    for s in range(0, count, step):
        owner = owner_column[s : s + step]
        place = place_column[s : s + step, 0:width]
        chosen = [hot(place - float(k) == lane) for k in range(0, capacity, width)]
        chosen = jnp.concatenate(chosen, axis=1)
        total = jnp.zeros((step, half), F32)
        for r in range(0, regions, 2):
            chunks = jnp.concatenate([got[r, 0:capacity, :], got[r + 1, 0:capacity, :]], axis=1)
            rows = mm(chosen, chunks)
            total = jnp.where(owner == float(r), rows[:, :half], jnp.where(owner == float(r + 1), rows[:, half:], total))
        out[s : s + step, :] = total.astype(BF16)


def ordered(flag, own, other):
    first = jnp.where(flag, other, own)
    second = jnp.where(flag, own, other)
    return first, second


def full_weights(core, own, other):
    flag = core[0] > 0
    half = own.shape[2]
    columns = []
    for k in range(3):
        columns.append(jnp.concatenate(ordered(flag, own[k], other[k]), axis=1))
    top, bottom = ordered(flag, own[3], other[3])
    rows = [jnp.concatenate([part[0:half], part[half:]], axis=1) for part in (top, bottom)]
    return columns + [jnp.concatenate(rows, axis=0)]


def norm_rows(slab, gain, width):
    wide = slab.astype(F32)
    inverse = lax.rsqrt(jnp.sum(wide * wide, axis=1, keepdims=True) / width + EPSILON)
    return wide, inverse, (wide * inverse * gain).astype(BF16)


def stack_rows(rows, extra):
    place = iota((HEAD_PAD - HEAD_DIM, rows.shape[1]), 0)
    tail = jnp.zeros(place.shape, F32)
    for k, value in enumerate(extra):
        tail = jnp.where(place == k, value, tail)
    return jnp.concatenate([rows.astype(F32), tail], axis=0)


def held_places(heads, low, wide):
    width = heads * HEAD_DIM
    return (
        low.at[pl.ds(2 * width, SLOTS), pl.ds(0, width)],
        low.at[pl.ds(0, width), :],
        low.at[pl.ds(2 * width, SLOTS), pl.ds(width, width)],
        low.at[pl.ds(width, width), :],
        wide.at[pl.ds(0, width), :],
        wide.at[pl.ds(width, heads), :],
    )


def forward_kernel(
    heads, regions, capacity, core, got, got_other, w_own, w_other, gain, low_far, exps_far, wide_far,
    keep_out, send_out, marks, keys_t, w_out, lift, lift_other, slab_out, queries_t, keys_out, values_t,
    context_t, inv_t, sems, exps_near, exps_sems
):
    step = pl.program_id(0)
    slot = jnp.bitwise_and(step, 1)
    steps = heads // PER_STEP

    def store(at, k):
        where = jnp.bitwise_and(at, 1)
        return pltpu.make_async_copy(exps_near.at[where, k], exps_far.at[at * PER_STEP + k], exps_sems.at[where, k])

    places = held_places(heads, low_far, wide_far)
    early = [
        pltpu.make_async_copy(near, far, sems.at[k])
        for k, (near, far) in enumerate(zip((slab_out, queries_t, keys_out, values_t), places[:4]))
    ]
    late = [
        pltpu.make_async_copy(near, far, sems.at[4 + k])
        for k, (near, far) in enumerate(zip((context_t, inv_t), places[4:]))
    ]
    width = heads * HEAD_DIM
    half = width // 2
    flag = core[0] > 0
    scale = HEAD_DIM**-0.5

    @pl.when(step == 0)
    def _():
        w_q, w_k, w_v, w_o = full_weights(core, w_own, w_other)
        w_out[...] = w_o
        count_rows(regions, capacity, got, marks)
        lift_rows(regions, capacity, core, marks, got, got_other, lift, lift_other)
        for first in range(0, SLOTS, CHUNK):
            rows = slice(first, first + CHUNK)
            slab = bin_rows(regions, capacity, core, marks, lift, lift_other, first, CHUNK)
            slab_out[rows, :] = slab
            _, _, normed = norm_rows(slab, gain[...], width)
            queries_t[:, rows] = jnp.transpose(mm(normed, w_q)).astype(BF16)
            k = mm(normed, w_k)
            keys_out[rows, :] = k.astype(BF16)
            keys_t[:, rows] = jnp.transpose(k).astype(BF16)
            values_t[:, rows] = jnp.transpose(mm(normed, w_v)).astype(BF16)
        for copy in early:
            copy.start()

    bias = jnp.where(is_filled(regions, core, marks, iota((1, SLOTS), 1)) > 0.5, 0.0, MASKED / scale)

    @pl.when(step >= 2)
    def _():
        for k in range(PER_STEP):
            store(step - 2, k).wait()

    for k in range(PER_STEP):
        h = step * PER_STEP + k
        head_rows = pl.ds(pl.multiple_of(h * HEAD_DIM, HEAD_DIM), HEAD_DIM)
        scaled = queries_t[head_rows, :].astype(F32) * (scale * LOG2E)
        high = scaled.astype(BF16).astype(F32)
        left = jnp.transpose(jnp.concatenate([high, stack_rows(scaled - high, (1.0,))], axis=0)).astype(BF16)
        k_rows = keys_t[head_rows, :].astype(F32)
        scores = mm(left, jnp.concatenate([k_rows, stack_rows(k_rows, (bias,))], axis=0).astype(BF16))
        top = jnp.max(scores, axis=1, keepdims=True)
        exps = jnp.exp2(scores - top).astype(BF16)
        exps_near[slot, k] = exps
        store(step, k).start()
        summed = mm_nt(stack_rows(values_t[head_rows, :], (1.0,)).astype(BF16), exps)
        inv = 1.0 / summed[HEAD_DIM : HEAD_DIM + 1]
        context_t[head_rows, :] = summed[0:HEAD_DIM] * inv
        inv_t[pl.ds(h, 1), :] = inv

    @pl.when(step == heads // PER_STEP - 1)
    def _():
        for copy in late:
            copy.start()
        rows_out = mm(jnp.transpose(context_t[...]).astype(BF16), w_out[...]).astype(BF16)
        keep_out[...] = jnp.where(flag, rows_out[:, half:], rows_out[:, :half])
        send_out[...] = jnp.where(flag, rows_out[:, :half], rows_out[:, half:])
        for copy in early + late:
            copy.wait()
        for at in range(steps - 2, steps):
            for k in range(PER_STEP):
                store(at, k).wait()


def backward_kernel(
    heads, regions, capacity, core, marks, got, got_other, w_own, w_other, gain, low_far,
    exps_in, wide_far, keep_out, send_out, grad_keep, grad_send, d_context_t, d_query, d_key_t, d_value_t, grad_slab, lift, lift_other, normed_t, d_low,
    slab_in, queries_t, keys_in, values_t, context_t, inv_t, sems
):
    step = pl.program_id(0)
    places = held_places(heads, low_far, wide_far)
    early = [
        pltpu.make_async_copy(far, near, sems.at[k])
        for k, (far, near) in enumerate(zip(places, (slab_in, queries_t, keys_in, values_t, context_t, inv_t)))
    ]
    width = heads * HEAD_DIM
    half = width // 2
    flag = core[0] > 0
    lane = iota((1, width), 1)
    scale = HEAD_DIM**-0.5

    @pl.when(step == 0)
    def _():
        for copy in early[1:] + early[:1]:
            copy.start()
        w_o = full_weights(core, w_own, w_other)[3]
        lift_rows(regions, capacity, core, marks, got, got_other, lift, lift_other)
        for first in range(0, SLOTS, CHUNK):
            rows = slice(first, first + CHUNK)
            part = bin_rows(regions, capacity, core, marks, lift, lift_other, first, CHUNK)
            grad_slab[rows, :] = part
            d_context_t[:, rows] = mm_nt(w_o, part).astype(BF16)
        for copy in early[1:]:
            copy.wait()

    for k in range(PER_STEP):
        h = step * PER_STEP + k
        head_rows = pl.ds(pl.multiple_of(h * HEAD_DIM, HEAD_DIM), HEAD_DIM)
        own_lane = lax.shift_right_logical(lane, log2_of(HEAD_DIM)) == h
        scaled = (d_context_t[head_rows, :].astype(F32) * inv_t[pl.ds(h, 1), :]).astype(BF16)
        dot = -jnp.sum(scaled.astype(F32) * context_t[head_rows, :], axis=0, keepdims=True)
        dot_high = dot.astype(BF16).astype(F32)
        left = jnp.transpose(stack_rows(scaled, (dot_high, dot - dot_high))).astype(BF16)
        centred = mm(left, stack_rows(values_t[head_rows, :], (1.0, 1.0)).astype(BF16))
        exps = exps_in[k]
        d_scores = (exps.astype(F32) * centred).astype(BF16)
        dq = mm(d_scores, keys_in[...])
        d_query[...] = jnp.where(own_lane, dq * scale, d_query[...])
        d_key_t[head_rows, :] = mm(queries_t[head_rows, :], d_scores) * scale
        d_value_t[head_rows, :] = mm(scaled, exps)

    @pl.when(step == heads // PER_STEP - 1)
    def _():
        w_q, w_k, w_v, _ = full_weights(core, w_own, w_other)
        early[0].wait()
        gain_grad = jnp.zeros((1, width), F32)
        for first in range(0, SLOTS, CHUNK):
            rows = slice(first, first + CHUNK)
            wide, inverse, normed = norm_rows(slab_in[rows, :], gain[...], width)
            dq = d_query[rows, :].astype(BF16)
            dk = jnp.transpose(d_key_t[:, rows]).astype(BF16)
            dv = jnp.transpose(d_value_t[:, rows]).astype(BF16)
            d_normed = mm_nt(dq, w_q) + mm_nt(dk, w_k) + mm_nt(dv, w_v)
            scaled = gain[...] * d_normed
            along = jnp.sum(scaled * wide, axis=1, keepdims=True)
            d_slab = (inverse * scaled - wide * (inverse * inverse * inverse) * along / width).astype(BF16)
            keep_out[rows, :] = jnp.where(flag, d_slab[:, half:], d_slab[:, :half])
            send_out[rows, :] = jnp.where(flag, d_slab[:, :half], d_slab[:, half:])
            gain_grad = gain_grad + jnp.sum(d_normed * wide * inverse, axis=0, keepdims=True)
            normed_t[:, rows] = jnp.transpose(normed.astype(F32)).astype(BF16)
            d_low[0, rows, :] = dq
            d_low[1, rows, :] = dk
            d_low[2, rows, :] = dv
        place = 0
        for k in range(3):
            grad = mm(normed_t[...], d_low[k])
            grad_keep[place : place + width, :] = jnp.where(flag, grad[:, half:], grad[:, :half]).astype(BF16)
            grad_send[place : place + width, :] = jnp.where(flag, grad[:, :half], grad[:, half:]).astype(BF16)
            place += width
        grad = mm(context_t[...].astype(BF16), grad_slab[...])
        for part in range(2):
            block = grad[:, part * half : (part + 1) * half]
            grad_keep[place : place + half, :] = jnp.where(flag, block[half:], block[:half]).astype(BF16)
            grad_send[place : place + half, :] = jnp.where(flag, block[:half], block[half:]).astype(BF16)
            place += half
        pick = iota((16, half), 0)
        block = jnp.where(pick == 0, gain_grad[:, :half], jnp.where(pick == 1, gain_grad[:, half:], 0.0))
        grad_keep[place : place + 16, :] = block.astype(BF16)
        grad_send[place : place + 16, :] = block.astype(BF16)


def shape(dims, dtype):
    return jax.ShapeDtypeStruct(tuple(dims), dtype)


SMEM_SPEC = pl.BlockSpec(memory_space=pltpu.SMEM)
FAR_SPEC = pl.BlockSpec(memory_space=pltpu.HBM)


def whole(array):
    zeros = (0,) * len(array.shape)
    return pl.BlockSpec(tuple(array.shape), lambda *_: zeros)


def simple_call(kernel, outs, inputs, scratch=(), scalars=0, scalar_outs=0, limit=ROWS_BYTES):
    specs = [SMEM_SPEC] * scalars + [whole(x) for x in inputs[scalars:]]
    return pl.pallas_call(
        kernel,
        out_shape=outs,
        in_specs=specs,
        out_specs=tuple(whole(x) for x in outs[: len(outs) - scalar_outs]) + (SMEM_SPEC,) * scalar_outs,
        scratch_shapes=scratch,
        compiler_params=pltpu.CompilerParams(vmem_limit_bytes=limit),
    )(*inputs)


def on_device(
    features,
    element_kinds,
    bin_cells,
    kind_embed,
    norm_gain,
    w_query,
    w_key,
    w_value,
    w_out,
    cotangent,
):
    regions = lax.axis_size("region")
    cores = lax.axis_size("head")
    local_rows = BINS_DEV * SLOTS
    capacity = local_rows // regions
    count, half = features.shape
    width = w_query.shape[0]
    heads = width // HEAD_DIM
    assert cores == BINS_DEV and half * cores == width and half == LANES
    core = lax.axis_index("head").astype(I32).reshape(1)
    swap = [(i, (i + 1) % cores) for i in range(cores)]

    def other_core(x):
        return lax.ppermute(x, "head", swap)

    def exchange(x):
        return lax.all_to_all(x, "region", split_axis=0, concat_axis=0, tiled=True)

    gain = norm_gain.reshape(1, width)
    kinds_row = element_kinds.reshape(1, count)
    packed_shape = shape((regions, capacity, half), BF16)
    tagged_shape = shape((regions, capacity + TAG_ROWS, half), BF16)
    packed_base, target = simple_call(
        functools.partial(pack_kernel, regions, capacity),
        (shape((regions, capacity + COUNT_ROWS, half), BF16), shape((1, count), I32)),
        (bin_cells.reshape(1, count), kinds_row, features, kind_embed),
        limit=None,
    )
    got_base = exchange(packed_base)
    packed_cot, w_own, gain = simple_call(
        functools.partial(pack_cot_kernel, regions, capacity),
        (tagged_shape, shape((4, width, half), BF16), shape((1, width), F32)),
        (target, kinds_row, cotangent, gain, w_query, w_key, w_value, w_out),
    )
    w_other = other_core(w_own)
    got_base, packed_cot = lax.optimization_barrier((got_base, packed_cot))
    got_cot = exchange(packed_cot)
    got_base_other = other_core(got_base)
    rows_shape = shape((SLOTS, half), BF16)
    lift = pltpu.VMEM((SLOTS + capacity, half), F32)

    turned = (width, SLOTS)
    exps_shape = shape((heads, SLOTS, SLOTS), BF16)
    exps_spec = pl.BlockSpec((PER_STEP, SLOTS, SLOTS), lambda h: (h, 0, 0))
    inputs = (core, got_base, got_base_other, w_own, w_other, gain)
    outs = (
        shape((heads * SLOTS, SLOTS), BF16),
        exps_shape,
        shape((heads * SLOTS // 2, SLOTS), F32),
        rows_shape,
        rows_shape,
        shape((2, regions + 1), I32),
    )
    work = heads * SLOTS * SLOTS
    held = (
        pltpu.VMEM((SLOTS, width), BF16),
        pltpu.VMEM(turned, BF16),
        pltpu.VMEM((SLOTS, width), BF16),
        pltpu.VMEM(turned, BF16),
        pltpu.VMEM(turned, F32),
        pltpu.VMEM((heads, SLOTS), F32),
        pltpu.SemaphoreType.DMA((6,)),
    )
    staged = (pltpu.VMEM((2, PER_STEP, SLOTS, SLOTS), BF16), pltpu.SemaphoreType.DMA((2, PER_STEP)))
    low, exps, wide, attn_keep, attn_send, marks = pl.pallas_call(
        functools.partial(forward_kernel, heads, regions, capacity),
        grid=(heads // PER_STEP,),
        out_shape=outs,
        in_specs=[SMEM_SPEC] + [whole(x) for x in inputs[1:]],
        out_specs=(FAR_SPEC,) * 3 + tuple(whole(x) for x in outs[3:5]) + (SMEM_SPEC,),
        scratch_shapes=(pltpu.VMEM((width, SLOTS), BF16), pltpu.VMEM((width, width), BF16), lift, lift) + held + staged,
        compiler_params=pltpu.CompilerParams(vmem_limit_bytes=ATTENTION_BYTES),
        cost_estimate=pl.CostEstimate(flops=4 * work * width, transcendentals=work, bytes_accessed=2 * work),
        name="forward",
    )(*inputs)
    attn_other = other_core(attn_send)
    (packed_attn,) = simple_call(
        functools.partial(ungroup_kernel, regions, capacity),
        (packed_shape,),
        (core, marks, attn_keep, attn_other),
        scratch=(lift, lift),
        scalars=2,
    )

    got_cot_other = other_core(got_cot)
    grad_rows = 4 * width + 16
    inputs = (core, marks, got_cot, got_cot_other, w_own, w_other, gain, low, exps, wide)
    outs = (rows_shape, rows_shape, shape((grad_rows, half), BF16), shape((grad_rows, half), BF16))
    d_keep, d_send, grad_keep, grad_send = pl.pallas_call(
        functools.partial(backward_kernel, heads, regions, capacity),
        grid=(heads // PER_STEP,),
        out_shape=outs,
        in_specs=[SMEM_SPEC] * 2 + [whole(x) for x in inputs[2:7]] + [FAR_SPEC, exps_spec, FAR_SPEC],
        out_specs=tuple(whole(x) for x in outs),
        scratch_shapes=(
            pltpu.VMEM((width, SLOTS), BF16),
            pltpu.VMEM((SLOTS, width), F32),
            pltpu.VMEM((width, SLOTS), F32),
            pltpu.VMEM((width, SLOTS), F32),
            pltpu.VMEM((SLOTS, width), BF16),
            lift,
            lift,
            pltpu.VMEM((width, SLOTS), BF16),
            pltpu.VMEM((3, SLOTS, width), BF16),
        )
        + held,
        compiler_params=pltpu.CompilerParams(vmem_limit_bytes=ATTENTION_BYTES),
        cost_estimate=pl.CostEstimate(flops=8 * work * width, transcendentals=0, bytes_accessed=2 * work),
        name="backward",
    )(*inputs)

    share = 4 * width // regions
    grad_other = other_core(grad_send)
    pairs = (grad_keep[: 4 * width].astype(F32) + grad_other[: 4 * width].astype(F32)).astype(BF16)
    pairs = pairs.reshape(regions, share, half)
    gain_part = (grad_keep[4 * width :].astype(F32) + grad_other[4 * width :].astype(F32)).astype(BF16)
    payload_shape = shape((regions, capacity + share + KIND_ROWS, half), BF16)
    packed_grad, extra = simple_call(
        functools.partial(ungroup_grad_kernel, regions, capacity),
        (payload_shape, shape((KIND_ROWS, half), BF16)),
        (core, marks, d_keep, other_core(d_send), got_cot, gain_part),
        scratch=(lift, lift),
        scalars=2,
    )
    got_cot, packed_attn = lax.optimization_barrier((got_cot, packed_attn))
    home_attn = exchange(packed_attn)
    home_attn, pairs = lax.optimization_barrier((home_attn, pairs))
    shares = exchange(pairs)
    payload = pl.pallas_call(
        functools.partial(share_kernel, regions, capacity),
        out_shape=payload_shape,
        in_specs=[whole(shares), whole(extra), pl.BlockSpec(memory_space=pl.ANY)],
        out_specs=pl.BlockSpec(memory_space=pl.ANY),
        scratch_shapes=(pltpu.VMEM((share + KIND_ROWS, half), BF16), pltpu.SemaphoreType.DMA((regions,))),
        input_output_aliases={2: 0},
        compiler_params=pltpu.CompilerParams(vmem_limit_bytes=ROWS_BYTES),
        name="share",
    )(shares, extra, packed_grad)
    home_grad = exchange(payload)
    (attended,) = simple_call(pick_kernel, (shape((count, half), BF16),), (target, home_attn))
    column_shape = shape((width, half), F32)
    grad_feats, grad_q, grad_k, grad_v, grad_o, grad_gain, grad_embed = simple_call(
        functools.partial(last_kernel, regions, capacity, float(count * regions) ** (-0.5)),
        (
            shape((count, half), BF16),
            column_shape,
            column_shape,
            column_shape,
            shape((half, width), F32),
            shape((1, width), F32),
            shape((KINDS, half), F32),
        ),
        (target, home_grad),
        scratch=(pltpu.VMEM((4 * width, half), F32),),
    )
    return (attended, grad_feats, grad_q, grad_k, grad_v, grad_o, grad_gain.reshape(width), grad_embed)


def solution(mesh):
    placed = (
        P(("groups", "region"), "head"),
        P(("groups", "region")),
        P(("groups", "region")),
        P(None, "head"),
        P(),
        P(None, "head"),
        P(None, "head"),
        P(None, "head"),
        P("head", None),
        P(("groups", "region"), "head"),
    )

    return jax.shard_map(
        on_device,
        mesh=mesh,
        in_specs=placed,
        out_specs=(
            P(("groups", "region"), "head"),
            P(("groups", "region"), "head"),
            P("groups", "head"),
            P("groups", "head"),
            P("groups", "head"),
            P(("groups", "head"), None),
            P("groups"),
            P("groups", "head"),
        ),
        check_vma=False,
    )
```
